32 devices in a mesh: dp: 8 (over z, y), seq: 4 (over x, core).
Axes of the slice: x: 2, y: 2, z: 4, core: 2. Of those that a mesh axis runs over, the one named last changes fastest.
Arguments:
- tokens: bfloat16 [8192, 768], P(('dp', 'seq')), may hold values from -6 to 6
- ln1_gain: bfloat16 [768], P('dp'), may hold values from 0.25 to 1.75
- w_qkv: bfloat16 [768, 2304], P('dp'), may hold values from -0.21875 to 0.21875
- w_out: bfloat16 [768, 768], P('dp'), may hold values from -1.75 to 1.75
- w_ada: bfloat16 [768, 2304], P('dp'), may hold values from -0.21875 to 0.21875
- w_up: bfloat16 [768, 3072], P('dp'), may hold values from -0.21875 to 0.21875
- w_down: bfloat16 [3072, 768], P('dp'), may hold values from -0.109375 to 0.109375
- out_grad: bfloat16 [8192, 768], P(('dp', 'seq')), may hold values from -6 to 6
- layout: int32 [8, 2], P('dp'), may hold values from 256 to 896, as said below
- timestep: int32 [8], P('dp'), may hold values from 0 to 999
Outputs:
- layer_out: bfloat16 [8192, 768], P(('dp', 'seq'))
- input_grad: bfloat16 [8192, 768], P(('dp', 'seq'))
- gain_grad: float32 [768], P('dp')
- qkv_weight_grad: float32 [768, 2304], P('dp')
- out_weight_grad: float32 [768, 768], P('dp')
- ada_weight_grad: float32 [768, 2304], P('dp')
- up_weight_grad: float32 [768, 3072], P('dp')
- down_weight_grad: float32 [3072, 768], P('dp')
The draws below stay inside these ranges and needn't reach their ends.
Inputs may be any that keep to these rules, and one draw needn't show every extreme that they name: layout[g] = (P, C): tokens below P are the prompt, the first continuation runs from P to C - 1, the second from C to 1023; P lies between 256 and 512, and each continuation holds at least a quarter of the tokens after the prompt.
All inputs are finite; a program needn't handle non-finite values.
Results may differ from the reference program's by a relative error of at most 0.017.
Values may be sent and summed in bfloat16 or wider, within the bound.
No kernel may reach another device: no remote copies, remote signals or barrier semaphores. Data moves between devices by JAX's collectives and lax.ppermute only.
A program may use at most 128 MiB of HBM per device.

```python
import math
import jax
import jax.numpy as jnp
from jax import lax

D = 768
HEADS = 12
HEAD_DIM = 64
FF = 3072
GROUP_TOK = 1024
GROUPS = 8
TOKENS = 8192


def draw_layout(key, part):
    first_key, second_key = jax.random.split(key)
    lowest = GROUP_TOK // 4
    highest = GROUP_TOK // 2
    prompt = jax.random.randint(first_key, (GROUPS,), lowest, highest + 1)
    prompt = prompt.at[0].set(highest).at[GROUPS - 1].set(lowest)
    remain = GROUP_TOK - prompt
    offset = jax.random.randint(second_key, (GROUPS,), 0, remain // 2 + 1)
    offset = offset.at[0].set(remain[0] // 2)
    second_start = prompt + remain // 4 + offset
    return jnp.stack([prompt, second_start], axis=1).astype(jnp.int32)


def with_ends(drawn, stream_key, low, top_value):
    shape = drawn.shape
    spot = [jax.random.randint(jax.random.fold_in(stream_key, axis), (), 0, shape[axis]) for axis in range(len(shape))]
    drawn = drawn.at[tuple(spot)].set(low)
    longest = shape.index(max(shape))
    spot[longest] = (spot[longest] + 1) % shape[longest]
    return drawn.at[tuple(spot)].set(top_value)


def levels(key, shape, cuts, low, largest):
    loudness = 1.0
    for position, shards_of in cuts:
        heights = jax.random.uniform(jax.random.fold_in(jax.random.fold_in(key, 6), position), (shards_of,), jnp.float32, low / len(cuts), largest / len(cuts))
        loudness = loudness * jnp.repeat(jnp.exp(heights), shape[position] // shards_of).reshape((-1,) + (1,) * (len(shape) - 1 - position))
    return loudness


def gaussian(key, extent, spread, limit, cuts=(), kind=jnp.bfloat16):
    loudness = levels(key, extent, cuts, -0.22, 0.18) if cuts else 1.0
    values = jax.random.normal(key, extent, jnp.float32) * spread * loudness
    return jnp.minimum(jnp.maximum(values, -limit), limit).astype(kind)


def setup_inputs(seed: int = 0) -> dict:
    keys = jax.random.split(jax.random.key(seed), 11)
    tokens = gaussian(keys[0], (TOKENS, D), 1.0, 6.0, ((0, 32),))
    ln1_gain = jnp.clip(1.0 + 0.15 * jax.random.normal(keys[1], (D,), jnp.float32), 0.25, 1.75).astype(jnp.bfloat16)
    w_qkv = gaussian(keys[2], (D, 3 * D), D ** -0.5, 0.21875, ((0, 8),))
    w_out = gaussian(keys[3], (D, D), (max(D * 16 // GROUP_TOK, 1)) ** -0.5, 1.75, ((0, 8),))
    w_ada = gaussian(keys[4], (D, 3 * D), D ** -0.5, 0.21875, ((0, 8),))
    w_up = gaussian(keys[5], (D, FF), D ** -0.5, 0.21875, ((0, 8),))
    w_down = gaussian(keys[6], (FF, D), FF ** -0.5, 0.109375, ((0, 8),))
    out_grad = gaussian(keys[7], (TOKENS, D), 1.0, 6.0, ((0, 32),))
    layout = draw_layout(jax.random.fold_in(keys[10], 71), 0)
    timestep = with_ends(jax.random.randint(keys[9], (GROUPS,), 0, 1000), jax.random.fold_in(keys[9], 1), 0, 999).astype(jnp.int32)
    return dict(tokens=tokens, ln1_gain=ln1_gain, w_qkv=w_qkv, w_out=w_out, w_ada=w_ada, w_up=w_up, w_down=w_down, out_grad=out_grad, layout=layout, timestep=timestep)


@jax.custom_vjp
def low(v):
    return lax.optimization_barrier(v.astype(jnp.bfloat16)).astype(jnp.float32)

@jax.custom_vjp
def low_back(v):
    return v

def low_keep(v):
    return (low(v), None)

def low_pass(kept, grad):
    return (grad,)

def back_keep(v):
    return (v, None)

def back_low(kept, grad):
    return (low(grad),)
low.defvjp(low_keep, low_pass)
low_back.defvjp(back_keep, back_low)
eps = 1e-05
neg_fill = -1e+30

def matmul(left, right):
    return jnp.dot(left, right, precision=lax.Precision.HIGHEST, preferred_element_type=jnp.float32)

def layer_norm(values_in):
    average = lax.optimization_barrier(jnp.mean(values_in, axis=-1, keepdims=True))
    centred = values_in - average
    variance = lax.optimization_barrier(jnp.mean(centred * centred, axis=-1, keepdims=True))
    return centred * lax.rsqrt(variance + eps)

def rope_tables(positions):
    half_dim = HEAD_DIM // 2
    frequency = jnp.exp(-math.log(10000.0) * 2.0 * jnp.arange(half_dim, dtype=jnp.float32) / HEAD_DIM)
    angles = positions.astype(jnp.float32)[:, None] * frequency[None, :]
    return (jnp.cos(angles), jnp.sin(angles))

def rotate(values_in, cos_table, sine_table, direction):
    half_dim = HEAD_DIM // 2
    front_half = values_in[..., :half_dim]
    back_half = values_in[..., half_dim:]
    cos_part = cos_table[:, None, :]
    sine_part = sine_table[:, None, :] * direction
    return jnp.concatenate([front_half * cos_part - back_half * sine_part, back_half * cos_part + front_half * sine_part], axis=-1)

def visible(query_pos, key_pos, prompt_end, second_start):
    query_segment = (query_pos >= prompt_end).astype(jnp.int32) + (query_pos >= second_start).astype(jnp.int32)
    key_segment = (key_pos >= prompt_end).astype(jnp.int32) + (key_pos >= second_start).astype(jnp.int32)
    return (key_pos[None, :] < prompt_end) | (query_segment[:, None] == key_segment[None, :])

def time_features(time_step):
    half_dim = D // 2
    frequency = jnp.exp(-math.log(10000.0) * jnp.arange(half_dim, dtype=jnp.float32) / half_dim)
    angles = time_step * frequency
    return jnp.concatenate([jnp.cos(angles), jnp.sin(angles)])

def group_forward(params, inputs, bounds, time_step):
    gain, qkv_weight, out_weight, ada_weight, up_weight, down_weight = params
    normed = layer_norm(inputs)
    hidden_one = low(normed * gain)
    projected = low_back(matmul(hidden_one, qkv_weight)).reshape(GROUP_TOK, 3, HEADS, HEAD_DIM)
    positions = jnp.arange(GROUP_TOK, dtype=jnp.int32)
    cos_table, sine_table = rope_tables(positions)
    rotated = jnp.stack([rotate(projected[:, 0], cos_table, sine_table, 1.0), rotate(projected[:, 1], cos_table, sine_table, 1.0), projected[:, 2]], axis=1)
    rotated = low_back(low(rotated))
    allowed = visible(positions, positions, bounds[0], bounds[1])

    def one_head(operands):
        query_head, key_head, value_head = operands
        raw_scores = matmul(query_head, key_head.T) * 0.125
        scores = low_back(jnp.where(allowed, raw_scores, neg_fill))
        row_max = lax.optimization_barrier(jnp.max(scores, axis=-1, keepdims=True))
        exponent = jnp.exp(scores - row_max)
        row_sum = lax.optimization_barrier(jnp.sum(exponent, axis=-1, keepdims=True))
        attn_probs = low(exponent / row_sum)
        return matmul(attn_probs, value_head)
    per_head = lax.map(jax.checkpoint(one_head), (jnp.transpose(rotated[:, 0], (1, 0, 2)), jnp.transpose(rotated[:, 1], (1, 0, 2)), jnp.transpose(rotated[:, 2], (1, 0, 2))))
    attended = low_back(low(jnp.transpose(per_head, (1, 0, 2)).reshape(GROUP_TOK, D)))
    middle = inputs + low_back(matmul(attended, out_weight))
    time_embed = low(time_features(time_step.astype(jnp.float32)))
    modulation = matmul(time_embed[None, :], ada_weight)[0]
    mod_scale = modulation[:D]
    mod_shift = modulation[D:2 * D]
    mod_gate = modulation[2 * D:]
    hidden_two = low(layer_norm(middle) * (1.0 + mod_scale) + mod_shift)
    pre_act = low_back(matmul(hidden_two, up_weight))
    activated = low(jax.nn.gelu(pre_act, approximate=True))
    mlp_out = low_back(matmul(activated, down_weight))
    return middle + mod_gate * mlp_out

def reference(tokens, ln1_gain, w_qkv, w_out, w_ada, w_up, w_down, out_grad, layout, timestep):
    params = (ln1_gain.astype(jnp.float32), w_qkv.astype(jnp.float32), w_out.astype(jnp.float32), w_ada.astype(jnp.float32), w_up.astype(jnp.float32), w_down.astype(jnp.float32))
    stacked_inputs = tokens.astype(jnp.float32).reshape(GROUPS, GROUP_TOK, D)

    def layer_all(params, stacked_inputs):

        def per_group(operands):
            return group_forward(params, operands[0], operands[1], operands[2])
        return lax.map(jax.checkpoint(per_group), (stacked_inputs, layout, timestep))
    outputs, pullback = jax.vjp(layer_all, params, stacked_inputs)
    grad_params, grad_inputs = pullback(out_grad.astype(jnp.float32).reshape(GROUPS, GROUP_TOK, D))
    return (outputs.reshape(TOKENS, D).astype(jnp.bfloat16), grad_inputs.reshape(TOKENS, D).astype(jnp.bfloat16), grad_params[0], grad_params[1], grad_params[2], grad_params[3], grad_params[4], grad_params[5])
```

```python
import math

import jax
import jax.numpy as jnp
from jax import lax
from jax.sharding import PartitionSpec as P

HEADS = 12
HEAD_DIM = 64

eps = 1e-05
neg_fill = -1e30

MASKS = (0, 2, 1, 3)


def layer_norm(values_in):
    average = jnp.mean(values_in, axis=-1, keepdims=True)
    centred = values_in - average
    variance = jnp.mean(centred * centred, axis=-1, keepdims=True)
    scaling = lax.rsqrt(variance + eps)
    return (centred * scaling, scaling)


def norm_back(grad_normed, normed, scaling):
    first_mean = jnp.mean(grad_normed, axis=-1, keepdims=True)
    second_mean = jnp.mean(grad_normed * normed, axis=-1, keepdims=True)
    return scaling * (grad_normed - first_mean - normed * second_mean)


def rope_tables(positions):
    half_dim = HEAD_DIM // 2
    frequency = jnp.exp(
        -math.log(10000.0) * 2.0 * jnp.arange(half_dim, dtype=jnp.float32) / HEAD_DIM
    )
    angles = positions.astype(jnp.float32)[:, None] * frequency[None, :]
    return (jnp.cos(angles), jnp.sin(angles))


def rotate(values_in, cos_table, sine_table, direction):
    half_dim = HEAD_DIM // 2
    front_half = values_in[..., :half_dim]
    back_half = values_in[..., half_dim:]
    cos_part = cos_table[:, None, :]
    sine_part = sine_table[:, None, :] * direction
    return jnp.concatenate(
        [
            front_half * cos_part - back_half * sine_part,
            back_half * cos_part + front_half * sine_part,
        ],
        axis=-1,
    )


def visible(query_pos, key_pos, prompt_end, second_start):
    query_segment = (query_pos >= prompt_end).astype(jnp.int32) + (
        query_pos >= second_start
    ).astype(jnp.int32)
    key_segment = (key_pos >= prompt_end).astype(jnp.int32) + (key_pos >= second_start).astype(
        jnp.int32
    )
    return (key_pos[None, :] < prompt_end) | (query_segment[:, None] == key_segment[None, :])


def time_table(time_steps, model_width):
    half_dim = model_width // 2
    frequency = jnp.exp(-math.log(10000.0) * jnp.arange(half_dim, dtype=jnp.float32) / half_dim)
    angles = time_steps[:, None] * frequency[None, :]
    return jnp.concatenate([jnp.cos(angles), jnp.sin(angles)], axis=1)


def left_product(left, right):
    return lax.dot_general(
        left, right, (((0,), (0,)), ((), ())), preferred_element_type=jnp.float32
    )


def right_product(left, right):
    return lax.dot_general(
        left, right, (((1,), (1,)), ((), ())), preferred_element_type=jnp.float32
    )


def low(values_in):
    return values_in.astype(jnp.bfloat16)


def wide(values_in):
    return values_in.astype(jnp.float32)


def hop(values_in, mask):
    return lax.ppermute(values_in, "seq", [(i, i ^ mask) for i in range(lax.axis_size("seq"))])


def spread(values_in):
    beside = jnp.concatenate([values_in, hop(values_in, 2)], axis=0)
    return jnp.concatenate([beside, hop(beside, 1)], axis=0)


def fold(partial):
    half = partial.shape[0] // 2
    beside = partial[:half] + wide(hop(low(partial[half:]), 1))
    quarter = half // 2
    return beside[:quarter] + wide(hop(low(beside[quarter:]), 2))


def in_order(blocks, rank):
    first, second, third, fourth = blocks
    core = (rank & 1) == 1
    chip = (rank & 2) == 2
    low_pair = (jnp.where(core, third, first), jnp.where(core, first, third))
    high_pair = (jnp.where(core, fourth, second), jnp.where(core, second, fourth))
    return (
        jnp.where(chip, high_pair[0], low_pair[0]),
        jnp.where(chip, high_pair[1], low_pair[1]),
        jnp.where(chip, low_pair[0], high_pair[0]),
        jnp.where(chip, low_pair[1], high_pair[1]),
    )


def ring_of(count):
    return [0] + list(range(1, count, 2)) + [i for i in range(count - 1, 0, -1) if i % 2 == 0]


def ring_next(data_count):
    outer = data_count // 2
    ring = ring_of(outer)
    follow = {ring[i]: ring[(i + 1) % outer] for i in range(outer)}
    return [(z * 2 + y, follow[z] * 2 + y) for z in range(outer) for y in range(2)]


def ring_places(data_count, index):
    outer = data_count // 2
    ring = ring_of(outer)
    table = [[ring[(ring.index(z) - back) % outer] for z in range(outer)] for back in range(outer)]
    return [jnp.asarray(row, jnp.int32)[index // 2] for row in table]


def pair(values_in):
    return lax.ppermute(values_in, "dp", [(i, i ^ 1) for i in range(lax.axis_size("dp"))])


def dp_gather(chunk):
    data_count = lax.axis_size("dp")
    if data_count != 8:
        return lax.all_gather(chunk, "dp", axis=0)
    index = lax.axis_index("dp")
    places = ring_places(data_count, index)
    out = jnp.zeros((data_count,) + chunk.shape, chunk.dtype)
    held = chunk
    follow = ring_next(data_count)
    for step, place in enumerate(places):
        beside = pair(held)
        own_row = place * 2 + index % 2
        other_row = place * 2 + 1 - index % 2
        out = lax.dynamic_update_index_in_dim(out, held, own_row, 0)
        out = lax.dynamic_update_index_in_dim(out, beside, other_row, 0)
        if step + 1 < len(places):
            held = lax.ppermute(held, "dp", follow)
    return out


def dp_sum(blocks):
    data_count = lax.axis_size("dp")
    if data_count != 8:
        return wide(lax.psum_scatter(blocks, "dp", scatter_dimension=0, tiled=False))
    index = lax.axis_index("dp")
    places = ring_places(data_count, index)
    follow = ring_next(data_count)
    carried = None
    for place in places[1:] + places[:1]:
        own = lax.dynamic_index_in_dim(blocks, place * 2 + index % 2, 0, keepdims=False)
        other = lax.dynamic_index_in_dim(blocks, place * 2 + 1 - index % 2, 0, keepdims=False)
        total = wide(own) + wide(pair(other))
        if carried is not None:
            total = total + wide(carried)
        if place is not places[0]:
            carried = lax.ppermute(low(total), "dp", follow)
    return total


def dp_sum_direct(blocks):
    data_count = lax.axis_size("dp")
    if data_count != 8:
        return wide(lax.psum_scatter(blocks, "dp", scatter_dimension=0, tiled=False))
    return jnp.sum(wide(lax.all_to_all(blocks, "dp", 0, 0, tiled=True)), axis=0)


def body(tokens, ln1_gain, w_qkv, w_out, w_ada, w_up, w_down, out_grad, layout, timestep):
    seq_count = lax.axis_size("seq")
    data_count = lax.axis_size("dp")
    rank = lax.axis_index("seq")
    tok_rows, width = tokens.shape
    group_rows = tok_rows * seq_count
    heads_local = HEADS // seq_count
    local_width = heads_local * HEAD_DIM
    rows = w_qkv.shape[0]
    hidden = w_up.shape[1] // seq_count
    down_rows = w_down.shape[0]
    out_piece = w_out.shape[0] // seq_count
    down_piece = down_rows // seq_count

    part_qkv = lax.dynamic_slice(
        w_qkv.reshape(rows, 3, seq_count, local_width),
        (0, 0, rank, 0),
        (rows, 3, 1, local_width),
    ).reshape(rows, 3 * local_width)
    qkv_weight = dp_gather(part_qkv).reshape(width, 3 * local_width)

    joint_there = []
    joint_back = []
    for source in range(data_count * seq_count):
        target = (source % data_count) * seq_count + source // data_count
        joint_there.append((source, target))
        joint_back.append((target, source))
    pieces = jnp.concatenate(
        [
            lax.dynamic_slice_in_dim(w_out, rank * out_piece, out_piece, 0),
            lax.dynamic_slice_in_dim(w_down, rank * down_piece, down_piece, 0),
        ],
        axis=0,
    )
    pieces = lax.ppermute(pieces, ("dp", "seq"), joint_there)
    part_up = lax.dynamic_slice_in_dim(w_up, rank * hidden, hidden, 1)
    gathered = dp_gather(pieces)
    own_out = gathered[:, :out_piece].reshape(-1, width)
    down_weight = gathered[:, out_piece:].reshape(hidden, width)
    up_weight = dp_gather(part_up).reshape(width, hidden)
    out_blocks = spread(own_out)

    embed = low(time_table(wide(timestep), width))
    sent = jnp.stack(
        [embed.reshape(data_count, rows), jnp.broadcast_to(ln1_gain, (data_count, rows))], axis=1
    )
    taken = lax.all_to_all(sent, "dp", 0, 0, tiled=True)
    embeds = taken[:, 0]
    gain = wide(taken[:, 1].reshape(width))
    mod_parts = jnp.dot(embeds, w_ada, preferred_element_type=jnp.float32)
    modulation = jnp.sum(lax.all_to_all(mod_parts, "dp", 0, 0, tiled=True), axis=0)
    mod_scale = modulation[:width]
    mod_shift = modulation[width : 2 * width]
    mod_gate = modulation[2 * width :]

    inputs_all = wide(spread(tokens))
    normed_one, _ = layer_norm(inputs_all)
    hidden_one = low(normed_one * gain)
    masks = jnp.asarray(MASKS, jnp.int32)
    positions = (
        (rank ^ masks)[:, None] * tok_rows + jnp.arange(tok_rows, dtype=jnp.int32)[None, :]
    ).reshape(group_rows)
    cos_table, sine_table = rope_tables(positions)
    projected = jnp.dot(hidden_one, qkv_weight, preferred_element_type=jnp.float32).reshape(
        group_rows, 3, heads_local, HEAD_DIM
    )
    queries = low(rotate(projected[:, 0], cos_table, sine_table, 1.0))
    keys = low(rotate(projected[:, 1], cos_table, sine_table, 1.0))
    values = low(projected[:, 2])
    scores = jnp.einsum("qhd,khd->hqk", queries, keys, preferred_element_type=jnp.float32) * 0.125
    allowed = visible(positions, positions, layout[0, 0], layout[0, 1])
    scores = jnp.where(allowed[None], scores, neg_fill)
    row_max = jnp.max(scores, axis=-1, keepdims=True)
    exponent = jnp.exp(scores - row_max)
    row_sum = jnp.sum(exponent, axis=-1, keepdims=True)
    probs = low(exponent / row_sum)
    attended = low(
        jnp.einsum("hqk,khd->qhd", probs, values, preferred_element_type=jnp.float32)
    ).reshape(group_rows, local_width)
    attended_own = [attended[:tok_rows]] + [
        hop(attended[j * tok_rows : (j + 1) * tok_rows], MASKS[j]) for j in (1, 2, 3)
    ]
    attended_own = jnp.concatenate(attended_own, axis=1)

    inputs = wide(tokens)
    middle = inputs + jnp.dot(attended_own, out_blocks, preferred_element_type=jnp.float32)
    normed_two, scaling_two = layer_norm(middle)
    hidden_two = low(normed_two * (1.0 + mod_scale) + mod_shift)

    hidden_all = spread(hidden_two)
    grad_all = wide(spread(out_grad))
    pre_act = jnp.dot(hidden_all, up_weight, preferred_element_type=jnp.float32)
    gelu_vals, gelu_pull = jax.vjp(lambda inner: jax.nn.gelu(inner, approximate=True), pre_act)
    activated = low(gelu_vals)
    grad_mlp = low(mod_gate * grad_all)
    grad_act = right_product(grad_mlp, down_weight)
    grad_pre = low(gelu_pull(grad_act)[0])
    grad_hidden_two = fold(right_product(grad_pre, up_weight))
    mlp_part = jnp.dot(activated, down_weight, preferred_element_type=jnp.float32)
    grad_gate = jnp.sum(grad_all * mlp_part, axis=0)
    mlp_out = fold(mlp_part)
    result = middle + mod_gate * mlp_out
    grad_wdown = left_product(activated, grad_mlp)
    grad_wup = left_product(hidden_all, grad_pre)

    grad_out = wide(out_grad)
    grad_scale = jnp.sum(grad_hidden_two * normed_two, axis=0)
    grad_shift = jnp.sum(grad_hidden_two, axis=0)
    grad_middle = grad_out + norm_back(grad_hidden_two * (1.0 + mod_scale), normed_two, scaling_two)
    grad_branch = low(grad_middle)
    grad_att = low(right_product(grad_branch, out_blocks))
    grad_att_parts = [grad_att[:, :local_width]] + [
        hop(grad_att[:, j * local_width : (j + 1) * local_width], MASKS[j]) for j in (1, 2, 3)
    ]
    grad_attended = jnp.concatenate(grad_att_parts, axis=0).reshape(
        group_rows, heads_local, HEAD_DIM
    )
    grad_wout = fold(left_product(attended_own, grad_branch))

    grad_mod = jnp.concatenate([grad_scale, grad_shift, grad_gate]).reshape(3, width)
    grad_mod = grad_mod + hop(grad_mod, 1)
    grad_mod = grad_mod + hop(grad_mod, 2)
    grad_mods = lax.all_to_all(
        jnp.broadcast_to(grad_mod[None], (data_count, 3, width)), "dp", 0, 0, tiled=True
    ).reshape(data_count, 3 * width)
    final_ada = lax.dot_general(
        wide(embeds), grad_mods, (((0,), (0,)), ((), ())), precision=lax.Precision.HIGHEST
    )

    value_grad = jnp.einsum("hqk,qhd->khd", probs, grad_attended, preferred_element_type=jnp.float32)
    prob_grad = jnp.einsum("qhd,khd->hqk", grad_attended, values, preferred_element_type=jnp.float32)
    pexp = exponent / row_sum
    row_centre = jnp.sum(pexp * prob_grad, axis=-1, keepdims=True)
    score_grad = low(pexp * (prob_grad - row_centre))
    query_grad = (
        jnp.einsum("hqk,khd->qhd", score_grad, keys, preferred_element_type=jnp.float32) * 0.125
    )
    key_grad = (
        jnp.einsum("hqk,qhd->khd", score_grad, queries, preferred_element_type=jnp.float32) * 0.125
    )
    grad_qkv = jnp.stack(
        [
            rotate(wide(low(query_grad)), cos_table, sine_table, -1.0),
            rotate(wide(low(key_grad)), cos_table, sine_table, -1.0),
            value_grad,
        ],
        axis=1,
    )
    grad_qkv = low(grad_qkv).reshape(group_rows, 3 * local_width)
    grad_wqkv = left_product(hidden_one, grad_qkv)
    grad_hidden_part = right_product(grad_qkv, qkv_weight)
    grad_gain = jnp.sum(grad_hidden_part * normed_one, axis=0)
    grad_hidden_one = fold(grad_hidden_part)
    normed_own, scaling_own = layer_norm(inputs)
    grad_inputs = grad_middle + norm_back(grad_hidden_one * gain, normed_own, scaling_own)

    sum_up = dp_sum(low(grad_wup).reshape(data_count, rows, hidden))
    sum_down = dp_sum(low(grad_wdown).reshape(data_count, down_piece, width))
    sum_out = dp_sum_direct(low(grad_wout).reshape(data_count, out_piece, width))
    gain_rows = jnp.pad(
        low(grad_gain).reshape(data_count, 1, rows), ((0, 0), (0, 0), (0, 3 * local_width - rows))
    )
    sum_qkv = dp_sum_direct(
        jnp.concatenate(
            [low(grad_wqkv).reshape(data_count, rows, 3 * local_width), gain_rows], axis=1
        )
    )
    back = lax.ppermute(
        jnp.concatenate([low(sum_out), low(sum_down)], axis=0), ("dp", "seq"), joint_back
    )

    def to_all(part):
        return [
            wide(block) for block in spread(part).reshape((seq_count,) + part.shape)
        ]

    final_up = jnp.concatenate(in_order(to_all(low(sum_up)), rank), axis=1)
    pieces_back = in_order(to_all(back), rank)
    final_out = jnp.concatenate([block[:out_piece] for block in pieces_back], axis=0)
    final_down = jnp.concatenate([block[out_piece:] for block in pieces_back], axis=0)
    qkv_parts = to_all(low(sum_qkv))
    final_gain = sum(block[rows, :rows] for block in qkv_parts)
    final_qkv = jnp.stack(
        in_order([block[:rows].reshape(rows, 3, local_width) for block in qkv_parts], rank), axis=2
    ).reshape(rows, 3 * width)
    return (
        low(result),
        low(grad_inputs),
        final_gain,
        final_qkv,
        final_out,
        final_ada,
        final_up,
        final_down,
    )


def solution(mesh):
    placed = (
        P(("dp", "seq"), None),
        P("dp"),
        P("dp", None),
        P("dp", None),
        P("dp", None),
        P("dp", None),
        P("dp", None),
        P(("dp", "seq"), None),
        P("dp", None),
        P("dp"),
    )
    return jax.shard_map(
        body,
        mesh=mesh,
        in_specs=placed,
        out_specs=(
            P(("dp", "seq"), None),
            P(("dp", "seq"), None),
            P("dp"),
            P("dp", None),
            P("dp", None),
            P("dp", None),
            P("dp", None),
            P("dp", None),
        ),
        check_vma=False,
    )
```

```python
import functools
import math

import jax
import jax.numpy as jnp
from jax import lax
from jax.experimental import pallas as pl
from jax.experimental.pallas import tpu as pltpu
from jax.sharding import PartitionSpec as P

HEADS = 12
HEAD_DIM = 64

eps = 1e-05

MASKS = (0, 2, 1, 3)


def time_table(time_steps, model_width):
    half_dim = model_width // 2
    frequency = jnp.exp(-math.log(10000.0) * jnp.arange(half_dim, dtype=jnp.float32) / half_dim)
    angles = time_steps[:, None] * frequency[None, :]
    return jnp.concatenate([jnp.cos(angles), jnp.sin(angles)], axis=1)


def low(values_in):
    return values_in.astype(jnp.bfloat16)


def wide(values_in):
    return values_in.astype(jnp.float32)


HEAD_TILE = 128
COST = 6.0
MASK_FILL = -1e30
GELU_IN = math.sqrt(2.0 / math.pi)
GELU_CUBE = 0.044715


def rope_tables(positions):
    half_dim = HEAD_DIM // 2
    column = jnp.arange(2 * HEAD_DIM, dtype=jnp.int32)
    frequency = jnp.exp(
        -math.log(10000.0) * 2.0 * (column % half_dim).astype(jnp.float32) / HEAD_DIM
    )
    angles = positions.astype(jnp.float32)[:, None] * frequency[None, :]
    sign = jnp.where(column % HEAD_DIM < half_dim, -1.0, 1.0)
    return (jnp.cos(angles), jnp.sin(angles) * sign[None, :])


def dot_nn(left, right):
    return lax.dot_general(
        left, right, (((1,), (0,)), ((), ())), preferred_element_type=jnp.float32
    )


def dot_nt(left, right):
    return lax.dot_general(
        left, right, (((1,), (1,)), ((), ())), preferred_element_type=jnp.float32
    )


def dot_tn(left, right):
    return lax.dot_general(
        left, right, (((0,), (0,)), ((), ())), preferred_element_type=jnp.float32
    )


def norm_rows(values_in):
    average = jnp.mean(values_in, axis=-1, keepdims=True)
    centred = values_in - average
    variance = jnp.mean(centred * centred, axis=-1, keepdims=True)
    scaling = lax.rsqrt(variance + eps)
    return (centred * scaling, scaling)


def swap_halves(values_in):
    column = lax.broadcasted_iota(jnp.int32, values_in.shape, 1)
    ahead = pltpu.roll(values_in, HEAD_TILE - HEAD_DIM // 2, 1)
    behind = pltpu.roll(values_in, HEAD_DIM // 2, 1)
    return jnp.where(column % HEAD_DIM < HEAD_DIM // 2, ahead, behind)


def whole(count):
    return [pl.BlockSpec(memory_space=pltpu.VMEM)] * count


def scalars():
    return [pl.BlockSpec(memory_space=pltpu.SMEM)]


def run(kernel, out_shapes, args, flops, scratch=(), name=None):
    nbytes = sum(a.size * a.dtype.itemsize for a in args)
    nbytes += sum(math.prod(o.shape) * o.dtype.itemsize for o in out_shapes)
    call = pl.pallas_call(
        kernel,
        out_shape=out_shapes,
        in_specs=scalars() + whole(len(args) - 1),
        out_specs=whole(len(out_shapes)),
        scratch_shapes=list(scratch),
        cost_estimate=pl.CostEstimate(flops=int(flops * COST), bytes_accessed=int(nbytes * COST), transcendentals=0),
        name=name,
    )
    return call(*args)


def shaped(shape, kind=jnp.bfloat16):
    return jax.ShapeDtypeStruct(shape, kind)


FIRST, OWNER, BLOCK, PLACE = 2, 6, 10, 14


def block_segment(info, block, rows, axis):
    shape = (rows, 1) if axis == 0 else (1, rows)
    position = info[FIRST + block] + lax.broadcasted_iota(jnp.int32, shape, axis)
    return (position >= info[0]).astype(jnp.int32) + (position >= info[1]).astype(jnp.int32)


def place_rows(info, chunks, first, rows, dest):
    for index, chunk in enumerate(chunks):
        at = pl.multiple_of(info[PLACE + index] * rows, rows)
        dest[pl.ds(at, rows), : chunk.shape[1]] = chunk[first : first + rows, :]


def first_part_kernel(info, qkv_ref, out_ref, dest):
    span = dest.shape[1] // 4
    for part in range(4):

        @pl.when(info[0] == part)
        def _():
            for third in range(3):
                at = (third * 4 + part) * span
                dest[:, third * span : (third + 1) * span] = qkv_ref[:, at : at + span]
            dest[:, 3 * span :] = out_ref[:, part * span : (part + 1) * span]


def second_part_kernel(count, info, up_ref, down_ref, dest):
    rows = up_ref.shape[0]
    piece = down_ref.shape[0] // 4
    for part in range(4):

        @pl.when(info[0] == part)
        def _():
            for index in range(count):
                at = (index * 4 + part) * piece
                dest[:rows, index * piece : (index + 1) * piece] = up_ref[:, at : at + piece]
            dest[rows:, :] = down_ref[part * piece : (part + 1) * piece, :]


def qkv_kernel(heads, count, info, *refs):
    gain, cos_ref, sin_ref = refs[:3]
    tok_refs = refs[3:7]
    chunks = refs[7 : 7 + count]
    hidden_ref, weight_ref, own_ref, q_ref, k_ref, v_ref = refs[7 + count :]
    rows, width = tok_refs[0].shape
    lw = heads * HEAD_DIM
    place_rows(info, chunks, 0, width // count, weight_ref)
    own_ref[...] = weight_ref[:, 3 * lw : 4 * lw]
    gain_row = gain[...]
    for block in range(4):
        normed, _ = norm_rows(wide(tok_refs[block][...]))
        hidden = low(normed * gain_row)
        here = slice(block * rows, (block + 1) * rows)
        hidden_ref[here, :] = hidden
        both = dot_nn(hidden, weight_ref[:, : 2 * lw])
        last = dot_nn(hidden, weight_ref[:, 2 * lw : 2 * lw + 2 * HEAD_TILE])
        cos_part = cos_ref[here, :]
        sin_part = sin_ref[here, :]
        turned = []
        for tile in range(2 * lw // HEAD_TILE):
            piece = both[:, tile * HEAD_TILE : (tile + 1) * HEAD_TILE]
            turned.append(piece * cos_part + swap_halves(piece) * sin_part)
        column = lax.broadcasted_iota(jnp.int32, (rows, HEAD_TILE), 1)
        segment = block_segment(info, block, rows, 0)
        first_fill = jnp.where(segment == 1, 0.0, MASK_FILL)
        second_fill = jnp.where(segment == 2, 0.0, MASK_FILL)
        q_mark = jnp.where(
            column == HEAD_DIM, first_fill, jnp.where(column == HEAD_DIM + 1, second_fill, 0.0)
        )
        first_mark = jnp.where(segment == 1, 1.0, 0.0)
        second_mark = jnp.where(segment == 2, 1.0, 0.0)
        k_mark = jnp.where(
            column == HEAD_DIM,
            first_mark,
            jnp.where(
                column == HEAD_DIM + 1, second_mark, jnp.where(column < HEAD_DIM + 5, 1.0, 0.0)
            ),
        )
        v_mark = jnp.where(column < HEAD_DIM + 2, 1.0, 0.0)
        for head in range(heads):
            q_at, k_at = head, heads + head
            q_tile = turned[q_at // 2]
            k_tile = turned[k_at // 2]
            v_tile = last[:, HEAD_TILE * (head // 2) : HEAD_TILE * (head // 2 + 1)]
            if q_at % 2:
                q_tile = pltpu.roll(q_tile, HEAD_DIM, 1)
            if k_at % 2:
                k_tile = pltpu.roll(k_tile, HEAD_DIM, 1)
            if head % 2:
                v_tile = pltpu.roll(v_tile, HEAD_DIM, 1)
            there = slice(head * HEAD_TILE, (head + 1) * HEAD_TILE)
            q_ref[here, there] = low(jnp.where(column < HEAD_DIM, q_tile * 0.125, q_mark))
            k_ref[here, there] = low(jnp.where(column < HEAD_DIM, k_tile, k_mark))
            v_ref[here, there] = low(jnp.where(column < HEAD_DIM, v_tile, v_mark))


def attend_kernel(heads, rows, info, q_ref, k_ref, v_ref, *outs):
    att_refs = outs[:4]
    stat_ref = outs[4]
    for block in range(4):
        here = slice(block * rows, (block + 1) * rows)
        column = lax.broadcasted_iota(jnp.int32, (rows, HEAD_TILE), 1)
        results = []
        for head in range(heads):
            there = slice(head * HEAD_TILE, (head + 1) * HEAD_TILE)
            queries = q_ref[here, there]
            scores = dot_nt(queries, k_ref[:, there])
            row_max = jnp.max(scores, axis=-1, keepdims=True)
            weights = low(jnp.exp(scores - row_max))
            summed = dot_nn(weights, v_ref[:, there])
            row_sum = summed[:, HEAD_DIM : HEAD_DIM + 1]
            results.append(summed / row_sum)
            minus = -(row_max + jnp.log(row_sum))
            first = low(minus)
            second = low(minus - wide(first))
            third = low(minus - wide(first) - wide(second))
            stat_ref[here, there] = jnp.where(
                column == HEAD_DIM + 2,
                first,
                jnp.where(
                    column == HEAD_DIM + 3, second, jnp.where(column == HEAD_DIM + 4, third, queries)
                ),
            )
        for head in range(0, heads, 2):
            if head + 1 < heads:
                both = jnp.where(
                    column < HEAD_DIM, results[head], pltpu.roll(results[head + 1], HEAD_DIM, 1)
                )
                att_refs[block][:, head * HEAD_DIM : (head + 2) * HEAD_DIM] = low(both)
            else:
                att_refs[block][:, head * HEAD_DIM :] = low(results[head][:, :HEAD_DIM])


def natural(info, blocks, dest):
    for block in range(4):
        dest[info[OWNER + block]] = blocks[block][...]


def middle_kernel(info, tok_ref, mod_ref, *refs):
    middle_ref, hidden_ref, att_ref, weight_ref = refs[8:]
    natural(info, refs[:4], weight_ref)
    natural(info, refs[4:8], att_ref)
    span = weight_ref.shape[2]
    for columns in range(4):
        there = slice(columns * span, (columns + 1) * span)
        total = wide(tok_ref[:, there])
        for part in range(4):
            total = total + dot_nn(
                att_ref[part], weight_ref[columns, part * span : (part + 1) * span, :]
            )
        middle_ref[:, there] = total
    normed, _ = norm_rows(middle_ref[...])
    hidden_ref[...] = low(normed * (1.0 + mod_ref[0:1, :]) + mod_ref[1:2, :])


def act_grad_kernel(count, skip, info, mod_ref, *refs):
    dy_refs = refs[:4]
    chunks = refs[4 : 4 + count]
    mlp_ref, act_ref, weight_ref = refs[4 + count :]
    rows = dy_refs[0].shape[0]
    place_rows(info, chunks, skip, weight_ref.shape[0] // count, weight_ref)
    gate = mod_ref[2:3, :]
    for block in range(4):
        here = slice(block * rows, (block + 1) * rows)
        grad_mlp = low(gate * wide(dy_refs[block][...]))
        mlp_ref[here, :] = grad_mlp
        act_ref[here, :] = low(dot_nt(grad_mlp, weight_ref[...]))


def forward_kernel(count, info, act_grad, *refs):
    hid_refs = refs[:4]
    chunks = refs[4 : 4 + count]
    act_ref, pre_ref, near_ref, far_ref, weight_ref = refs[4 + count :]
    rows = hid_refs[0].shape[0]
    place_rows(info, chunks, 0, weight_ref.shape[0] // count, weight_ref)
    for block in (2, 3, 1, 0):
        here = slice(block * rows, (block + 1) * rows)
        pre = dot_nn(hid_refs[block][...], weight_ref[...])
        square = pre * pre
        inner = jnp.tanh(GELU_IN * (pre + GELU_CUBE * (square * pre)))
        half = 0.5 * (1.0 + inner)
        act_ref[here, :] = low(pre * half)
        slope = half + 0.5 * pre * (1.0 - inner * inner) * (
            GELU_IN * (1.0 + 3.0 * GELU_CUBE * square)
        )
        grad_pre = low(wide(act_grad[here, :]) * slope)
        pre_ref[here, :] = grad_pre
        dest = near_ref if block < 2 else far_ref
        dest[(block % 2) * rows : (block % 2 + 1) * rows, :] = low(
            dot_nt(grad_pre, weight_ref[...])
        )


def weight_grad_kernel(count, info, act_ref, mlp_ref, pre_ref, *refs):
    hid_refs = refs[:4]
    outs = refs[4:-1]
    sums_ref = refs[-1]
    rows = hid_refs[0].shape[0]
    per = act_ref.shape[1] // count
    up = dot_tn(hid_refs[0][...], pre_ref[:rows, :])
    for block in range(1, 4):
        up = up + dot_tn(hid_refs[block][...], pre_ref[block * rows : (block + 1) * rows, :])
    for index in range(count):
        sums_ref[index, :per, :] = low(up[index * per : (index + 1) * per, :])
    down = dot_tn(act_ref[...], mlp_ref[...])
    for index in range(count):
        sums_ref[index, per:, :] = low(down[index * per : (index + 1) * per, :])
    if len(outs) == 1:
        outs[0][...] = sums_ref[...]
    else:
        for index in range(count):
            outs[index][...] = sums_ref[info[PLACE + index]]


def down_kernel(count, skip, info, act_ref, *refs):
    dy_refs = refs[:4]
    chunks = refs[4 : 4 + count]
    near_ref, far_ref, gate_ref, weight_ref = refs[4 + count :]
    rows = dy_refs[0].shape[0]
    place_rows(info, chunks, skip, weight_ref.shape[0] // count, weight_ref)
    total = jnp.zeros(gate_ref.shape, jnp.float32)
    for block in (2, 3, 1, 0):
        here = slice(block * rows, (block + 1) * rows)
        part = dot_nn(act_ref[here, :], weight_ref[...])
        total = total + jnp.sum(wide(dy_refs[block][...]) * part, axis=0, keepdims=True)
        dest = near_ref if block < 2 else far_ref
        dest[(block % 2) * rows : (block % 2 + 1) * rows, :] = low(part)
    gate_ref[...] = total


def branch_kernel(info, mod_ref, middle_ref, dy_ref, own_ref, core_ref, chip_ref, *refs):
    mid_ref, branch_ref, sums_ref = refs[4:7]
    att_refs = refs[7:11]
    weight_ref = refs[11]
    natural(info, refs[:4], weight_ref)
    rows = dy_ref.shape[0]
    grad_hidden = wide(own_ref[:rows, :]) + wide(core_ref[:rows, :]) + wide(chip_ref[...])
    normed, scaling = norm_rows(middle_ref[...])
    sums_ref[0:1, :] = jnp.sum(grad_hidden * normed, axis=0, keepdims=True)
    sums_ref[1:2, :] = jnp.sum(grad_hidden, axis=0, keepdims=True)
    grad_normed = grad_hidden * (1.0 + mod_ref[0:1, :])
    first_mean = jnp.mean(grad_normed, axis=-1, keepdims=True)
    second_mean = jnp.mean(grad_normed * normed, axis=-1, keepdims=True)
    mid_ref[...] = wide(dy_ref[...]) + scaling * (grad_normed - first_mean - normed * second_mean)
    span = weight_ref.shape[2]
    for columns in range(4):
        branch_ref[columns] = low(mid_ref[:, columns * span : (columns + 1) * span])
    for block, dest in enumerate(att_refs):
        at = pl.multiple_of(info[OWNER + block] * span, HEAD_DIM)
        total = dot_nt(branch_ref[0], weight_ref[0, pl.ds(at, span), :])
        for columns in range(1, 4):
            total = total + dot_nt(branch_ref[columns], weight_ref[columns, pl.ds(at, span), :])
        dest[...] = low(total)


def out_grad_kernel(info, branch_ref, *refs):
    near_ref, far_ref, att_ref = refs[4:]
    span = branch_ref.shape[2]
    natural(info, refs[:4], att_ref)
    for block in range(4):
        dest = near_ref if block < 2 else far_ref
        branch = branch_ref[info[OWNER + block]]
        for part in range(4):
            dest[block % 2, part * span : (part + 1) * span, :] = low(
                dot_tn(att_ref[part], branch)
            )


def attend_back_kernel(heads, rows, info, cos_ref, sin_ref, q_ref, k_ref, v_ref, *refs):
    att = refs[:4]
    grads = refs[4:8]
    out_ref, gx_ref, turn_ref, dq_ref, dk_ref, dv_ref = refs[8:]
    column = lax.broadcasted_iota(jnp.int32, (rows, HEAD_TILE), 1)

    def tile_of(ref, head):
        if head % 2 or head + 1 < heads:
            tile = wide(ref[:, HEAD_TILE * (head // 2) : HEAD_TILE * (head // 2) + HEAD_TILE])
            return pltpu.roll(tile, HEAD_DIM, 1) if head % 2 else tile
        last = wide(ref[:, head * HEAD_DIM :])
        return jnp.concatenate([last, jnp.zeros_like(last)], axis=1)

    for head in range(heads):
        there = slice(head * HEAD_TILE, (head + 1) * HEAD_TILE)
        for block in range(4):
            here = slice(block * rows, (block + 1) * rows)
            grad = jnp.where(column < HEAD_DIM, tile_of(grads[block], head), 0.0)
            minus = -jnp.sum(grad * tile_of(att[block], head), axis=-1, keepdims=True)
            first = wide(low(minus))
            gx_ref[here, :] = low(
                jnp.where(
                    column == HEAD_DIM,
                    first,
                    jnp.where(column == HEAD_DIM + 1, minus - first, grad),
                )
            )
        for block in range(4):
            here = slice(block * rows, (block + 1) * rows)
            keys = k_ref[here, there]
            probs = jnp.exp(dot_nt(keys, q_ref[:, there]))
            prob_grad = dot_nt(v_ref[here, there], gx_ref[...])
            score_grad = low(probs * prob_grad)
            dv_ref[here, there] = dot_nn(low(probs), gx_ref[...])
            dk_ref[here, there] = dot_nn(score_grad, q_ref[:, there])
            part = dot_tn(keys, score_grad)
            if block == 0:
                turn_ref[...] = part
            else:
                turn_ref[...] += part
        dq_ref[:, there] = jnp.transpose(turn_ref[...]) * 0.125

    for block in range(4):
        here = slice(block * rows, (block + 1) * rows)
        heads_of = [dq_ref[here, h * HEAD_TILE : (h + 1) * HEAD_TILE] for h in range(heads)]
        heads_of += [dk_ref[here, h * HEAD_TILE : (h + 1) * HEAD_TILE] for h in range(heads)]
        heads_of += [dv_ref[here, h * HEAD_TILE : (h + 1) * HEAD_TILE] for h in range(heads)]
        heads_of.append(jnp.zeros((rows, HEAD_TILE), jnp.float32))
        for tile in range((3 * heads + 1) // 2):
            both = jnp.where(
                column < HEAD_DIM,
                heads_of[2 * tile],
                pltpu.roll(heads_of[2 * tile + 1], HEAD_DIM, 1),
            )
            if tile < heads:
                both = both * cos_ref[here, :] - swap_halves(both) * sin_ref[here, :]
            out_ref[here, tile * HEAD_TILE : (tile + 1) * HEAD_TILE] = low(both)


def hidden_grad_kernel(info, grad_ref, weight_ref, near_ref, far_ref):
    rows = near_ref.shape[0] // 2
    span = grad_ref.shape[1]
    for block in (2, 3, 1, 0):
        dest = near_ref if block < 2 else far_ref
        at = (block % 2) * rows
        here = slice(block * rows, (block + 1) * rows)
        dest[at : at + rows, :] = low(dot_nt(grad_ref[here, :], weight_ref[:, :span]))


def qkv_grad_kernel(count, used, info, hidden_ref, grad_ref, near_ref, core_ref, chip_ref, *refs):
    outs, sums_ref = refs[:-1], refs[-1]
    total = dot_tn(hidden_ref[...], grad_ref[...])
    out_total = wide(near_ref[0]) + wide(core_ref[0]) + wide(chip_ref[0])
    per = total.shape[0] // count
    for index in range(count):
        here = slice(index * per, (index + 1) * per)
        sums_ref[index, :, :used] = low(total[here, :used])
        sums_ref[index, :, used:] = low(out_total[here, :])
    if len(outs) == 1:
        outs[0][...] = sums_ref[...]
    else:
        for index in range(count):
            outs[index][...] = sums_ref[info[PLACE + index]]


def input_kernel(info, gain, tok_ref, mid_ref, own_ref, core_ref, chip_ref, out_ref):
    rows = tok_ref.shape[0]
    grad_hidden = wide(own_ref[:rows, :]) + wide(core_ref[:rows, :]) + wide(chip_ref[...])
    normed, scaling = norm_rows(wide(tok_ref[...]))
    grad_normed = grad_hidden * gain[...]
    first_mean = jnp.mean(grad_normed, axis=-1, keepdims=True)
    second_mean = jnp.mean(grad_normed * normed, axis=-1, keepdims=True)
    out_ref[...] = low(
        mid_ref[...] + scaling * (grad_normed - first_mean - normed * second_mean)
    )


def finish_mlp_kernel(count, info, *refs):
    blocks = refs[:4]
    up_ref, down_ref, all_ref = refs[4:]
    natural(info, blocks, all_ref)
    rows = up_ref.shape[0]
    piece = down_ref.shape[0] // 4
    for part in range(4):
        value = wide(all_ref[part])
        for index in range(count):
            at = (index * 4 + part) * piece
            up_ref[:, at : at + piece] = value[:rows, index * piece : (index + 1) * piece]
        down_ref[part * piece : (part + 1) * piece, :] = value[rows:, :]


def finish_qkv_kernel(info, *refs):
    blocks = refs[:4]
    weight_ref, gain_ref, out_ref, own_ref, sums_ref, all_ref = refs[4:]
    natural(info, blocks, all_ref)
    span = all_ref.shape[2] // 4
    for part in range(4):
        value = wide(all_ref[part])
        for third in range(3):
            at = (third * 4 + part) * span
            out_ref[:, at : at + span] = value[:, third * span : (third + 1) * span]
        own_ref[:, part * span : (part + 1) * span] = value[:, 3 * span :]
    total = jnp.sum(wide(weight_ref[...]) * out_ref[...], axis=1, keepdims=True)
    wide_total = jnp.broadcast_to(total, (total.shape[0], HEAD_TILE))
    sums_ref[...] = jnp.transpose(wide_total)[0:1, :] / gain_ref[...]


def hop(values_in, mask):
    return lax.ppermute(values_in, "seq", [(i, i ^ mask) for i in range(lax.axis_size("seq"))])


def ring_of(count):
    return [0] + list(range(1, count, 2)) + [i for i in range(count - 1, 0, -1) if i % 2 == 0]


def ring_next(data_count):
    outer = data_count // 2
    ring = ring_of(outer)
    follow = {ring[i]: ring[(i + 1) % outer] for i in range(outer)}
    return [(z * 2 + y, follow[z] * 2 + y) for z in range(outer) for y in range(2)]


def ring_places(data_count, index):
    outer = data_count // 2
    ring = ring_of(outer)
    table = [[ring[(ring.index(z) - back) % outer] for z in range(outer)] for back in range(outer)]
    return [jnp.asarray(row, jnp.int32)[index // 2] for row in table]


def pair(values_in):
    return lax.ppermute(values_in, "dp", [(i, i ^ 1) for i in range(lax.axis_size("dp"))])


def dp_sum_direct(blocks):
    data_count = lax.axis_size("dp")
    if data_count != 8:
        return wide(lax.psum_scatter(blocks, "dp", scatter_dimension=0, tiled=False))
    return jnp.sum(wide(lax.all_to_all(blocks, "dp", 0, 0, tiled=True)), axis=0)


def after(values_in, *earlier):
    return lax.optimization_barrier((values_in,) + earlier)[0]


def onward(values_in):
    return lax.ppermute(values_in, "dp", ring_next(lax.axis_size("dp")))


def chunk_places():
    data_count = lax.axis_size("dp")
    if data_count != 8:
        return jnp.zeros((1,), jnp.int32)
    index = lax.axis_index("dp")
    ring = ring_of(data_count // 2)
    table = [
        [2 * ring[ring.index(one // 2) - back] + (one + side) % 2 for back in range(len(ring)) for side in (0, 1)]
        for one in range(data_count)
    ]
    return lax.dynamic_index_in_dim(jnp.asarray(table, jnp.int32), index, 0, keepdims=False)


def gathered_whole(chunk, sizes):
    gathered = lax.all_gather(chunk, "dp", axis=0)
    parts = []
    at = 0
    for size in sizes:
        parts.append(gathered[:, at : at + size].reshape(-1, chunk.shape[1]))
        at += size
    return [jnp.concatenate(parts, axis=0)]


def four(values_in):
    chip = hop(values_in, 2)
    return [values_in, chip, hop(values_in, 1), hop(chip, 1)]


def gather_back(near, far):
    rows = near.shape[0] // 2
    core = hop(far, 1)
    chip = hop(low(wide(near[rows:]) + wide(core[rows:])), 2)
    return core, chip


def body(tokens, ln1_gain, w_qkv, w_out, w_ada, w_up, w_down, out_grad, layout, timestep):
    seq_count = lax.axis_size("seq")
    data_count = lax.axis_size("dp")
    ringed = data_count == 8
    rank = lax.axis_index("seq")
    tok_rows, width = tokens.shape
    group_rows = tok_rows * seq_count
    heads_local = HEADS // seq_count
    local_width = heads_local * HEAD_DIM
    head_columns = heads_local * HEAD_TILE
    padded = (3 * heads_local + 1) // 2 * HEAD_TILE
    rows = w_qkv.shape[0]
    hidden = w_up.shape[1] // seq_count
    down_piece = w_down.shape[0] // seq_count
    rank_word = rank.reshape(1).astype(jnp.int32)

    tok_chip = hop(tokens, 2)
    first = run(
        first_part_kernel,
        [shaped((rows, 4 * local_width))],
        [rank_word, w_qkv, w_out],
        0,
        name="first_part",
    )[0]
    if ringed:
        held = [first, onward(first)]
        beside = [pair(first)]
        held[1], beside[0], tokens = lax.optimization_barrier((held[1], beside[0], tokens))
        held.append(onward(held[1]))
        beside.append(pair(held[1]))
        tok_core = hop(tokens, 1)
        held[2], beside[1], tok_chip, tok_core = lax.optimization_barrier(
            (held[2], beside[1], tok_chip, tok_core)
        )
        held.append(onward(held[2]))
        beside.append(pair(held[2]))
        tok_both = hop(tok_chip, 1)
    else:
        tok_core, tok_both = hop(tokens, 1), hop(tok_chip, 1)
    tok_blocks = [tokens, tok_chip, tok_core, tok_both]

    embed = low(time_table(wide(timestep), width))
    sent = jnp.stack(
        [embed.reshape(data_count, rows), jnp.broadcast_to(ln1_gain, (data_count, rows))], axis=1
    )
    taken = lax.all_to_all(sent, "dp", 0, 0, tiled=True)
    embeds = taken[:, 0]
    gain = wide(taken[:, 1].reshape(1, width))
    if ringed:
        embeds = after(embeds, held[1])
    mod_parts = jnp.dot(embeds, w_ada, preferred_element_type=jnp.float32)
    modulation = jnp.sum(lax.all_to_all(mod_parts, "dp", 0, 0, tiled=True), axis=0).reshape(
        3, width
    )

    masks = jnp.asarray(MASKS, jnp.int32)
    starts = (rank ^ masks) * tok_rows
    info = jnp.concatenate(
        [
            layout.reshape(-1),
            starts,
            rank ^ masks,
            masks[rank ^ jnp.arange(seq_count)],
            chunk_places(),
        ]
    )
    if ringed:
        starts = after(starts, held[2])
    positions = (starts[:, None] + jnp.arange(tok_rows, dtype=jnp.int32)[None, :]).reshape(-1)
    cos_table, sin_table = rope_tables(positions)

    second = run(
        functools.partial(second_part_kernel, data_count),
        [shaped((rows + down_piece, width))],
        [rank_word, w_up, w_down],
        0,
        name="second_part",
    )[0]
    if ringed:
        held[3], beside[2], second, *rest = lax.optimization_barrier(
            (held[3], beside[2], second, modulation, info, cos_table, sin_table, gain, tok_blocks)
        )
        modulation, info, cos_table, sin_table, gain, tok_blocks = rest
        beside.append(pair(held[3]))
        first_chunks = [part for both in zip(held, beside) for part in both]
        held = [second, onward(second)]
        grad_out, second = lax.optimization_barrier((out_grad, second, beside[3]))[:2]
        beside = [pair(second)]
        dy_chip = hop(grad_out, 2)
    else:
        first_chunks = gathered_whole(first, [rows])
        second_chunks = gathered_whole(second, [rows, down_piece])
        dy_chip = hop(out_grad, 2)
    count = len(first_chunks)
    up_rows = rows * (data_count // count)

    hidden_one, qkv_weight, own_out, queries, keys, values = run(
        functools.partial(qkv_kernel, heads_local, count),
        [
            shaped((group_rows, width)),
            shaped((width, 4 * local_width)),
            shaped((width, local_width)),
            shaped((group_rows, head_columns)),
            shaped((group_rows, head_columns)),
            shaped((group_rows, head_columns)),
        ],
        [info, gain, cos_table, sin_table] + tok_blocks + first_chunks,
        2 * group_rows * width * padded,
        name="qkv",
    )
    if ringed:
        queries, own_out, held[1], beside[0] = lax.optimization_barrier(
            (queries, own_out, held[1], beside[0])
        )
        beside.append(pair(held[1]))
        held.append(onward(held[1]))
    chip_out = hop(own_out, 2)
    *att_parts, marked = run(
        functools.partial(attend_kernel, heads_local, tok_rows),
        [shaped((tok_rows, local_width))] * 4 + [shaped((group_rows, head_columns))],
        [info, queries, keys, values],
        4 * group_rows * group_rows * head_columns,
        name="attend",
    )
    if ringed:
        att_parts, held[2], beside[1], chip_out, dy_chip = lax.optimization_barrier(
            (att_parts, held[2], beside[1], chip_out, dy_chip)
        )
        beside.append(pair(held[2]))
        held.append(onward(held[2]))
    att_own = [att_parts[0]] + [hop(att_parts[j], MASKS[j]) for j in (1, 2, 3)]
    if ringed:
        att_own, held[3], beside[2] = lax.optimization_barrier((att_own, held[3], beside[2]))
    out_blocks = [own_out, chip_out, hop(own_out, 1), hop(chip_out, 1)]
    middle, hidden_two = run(
        middle_kernel,
        [shaped((tok_rows, width), jnp.float32), shaped((tok_rows, width))],
        [info, tokens, modulation] + out_blocks + att_own,
        2 * tok_rows * width * width,
        scratch=[
            pltpu.VMEM((seq_count, tok_rows, local_width), jnp.bfloat16),
            pltpu.VMEM((seq_count, width, local_width), jnp.bfloat16),
        ],
        name="middle",
    )

    chip_hidden = hop(hidden_two, 2)
    if ringed:
        beside.append(pair(after(held[3], hidden_two)))
        second_chunks = [part for both in zip(held, beside) for part in both]
    hid_blocks = [hidden_two, chip_hidden, hop(hidden_two, 1), hop(chip_hidden, 1)]
    dy_blocks = [out_grad, dy_chip, hop(out_grad, 1), hop(dy_chip, 1)]
    grad_mlp, grad_act = run(
        functools.partial(act_grad_kernel, count, up_rows),
        [shaped((group_rows, width)), shaped((group_rows, hidden))],
        [info, modulation] + dy_blocks + second_chunks,
        2 * group_rows * width * hidden,
        scratch=[pltpu.VMEM((hidden, width), jnp.bfloat16)],
        name="act_grad",
    )
    half = shaped((group_rows // 2, width))
    activated, grad_pre, gh_near, gh_far = run(
        functools.partial(forward_kernel, count),
        [shaped((group_rows, hidden)), shaped((group_rows, hidden)), half, half],
        [info, grad_act] + hid_blocks + second_chunks,
        4 * group_rows * width * hidden,
        scratch=[pltpu.VMEM((width, hidden), jnp.bfloat16)],
        name="forward",
    )
    gh_core = hop(gh_far, 1)
    gh_send = low(wide(gh_near[tok_rows:]) + wide(gh_core[tok_rows:]))
    gh_chip = hop(gh_send, 2)
    block_shape = (rows + down_piece, width)
    grad_weights = run(
        functools.partial(weight_grad_kernel, data_count),
        [shaped(block_shape)] * count if ringed else [shaped((data_count,) + block_shape)],
        [info, after(activated, gh_send), grad_mlp, grad_pre] + hid_blocks,
        4 * group_rows * width * hidden,
        scratch=[pltpu.VMEM((data_count,) + block_shape, jnp.bfloat16)],
        name="weight_grad",
    )
    mlp_near, mlp_far, grad_gate = run(
        functools.partial(down_kernel, count, up_rows),
        [half, half, shaped((1, width), jnp.float32)],
        [info, after(activated, grad_weights[0])] + dy_blocks + second_chunks,
        2 * group_rows * width * hidden,
        scratch=[pltpu.VMEM((hidden, width), jnp.bfloat16)],
        name="down",
    )
    mlp_core = hop(mlp_far, 1)
    if ringed:
        grad_own, grad_other = list(grad_weights[0::2]), list(grad_weights[1::2])
        taken = pair(grad_other[1])

    grad_middle, branch, grad_sums, *grad_parts = run(
        branch_kernel,
        [
            shaped((tok_rows, width), jnp.float32),
            shaped((seq_count, tok_rows, local_width)),
            shaped((2, width), jnp.float32),
        ]
        + [shaped((tok_rows, local_width))] * 4,
        [info, modulation, after(middle, mlp_near), out_grad, gh_near, gh_core, gh_chip]
        + out_blocks,
        2 * tok_rows * width * width,
        scratch=[pltpu.VMEM((seq_count, width, local_width), jnp.bfloat16)],
        name="branch",
    )
    grad_parts, mlp_core = lax.optimization_barrier((grad_parts, mlp_core))
    grad_att = [grad_parts[0]] + [hop(grad_parts[j], MASKS[j]) for j in (1, 2, 3)]
    go_near, go_far = run(
        out_grad_kernel,
        [shaped((2, width, local_width))] * 2,
        [info, after(branch, grad_parts[0])] + att_own,
        2 * tok_rows * width * width,
        scratch=[pltpu.VMEM((seq_count, tok_rows, local_width), jnp.bfloat16)],
        name="out_grad",
    )
    go_core = hop(go_far, 1)
    go_send = low(wide(go_near[1:]) + wide(go_core[1:]))
    mlp_send = low(wide(mlp_near[tok_rows:]) + wide(mlp_core[tok_rows:]))

    grad_att, go_send, mlp_send = lax.optimization_barrier((grad_att, go_send, mlp_send))
    if ringed:
        ring_send = low(wide(after(grad_own[1], grad_parts[0])) + wide(taken))
        carried = onward(ring_send)
        taken = pair(after(grad_other[2], ring_send))
    go_chip = hop(go_send, 2)
    mlp_chip = hop(mlp_send, 2)
    grad_qkv = run(
        functools.partial(attend_back_kernel, heads_local, tok_rows),
        [shaped((group_rows, padded))],
        [info, cos_table, sin_table, marked, keys, values] + att_parts + grad_att,
        10 * group_rows * group_rows * head_columns,
        scratch=[
            pltpu.VMEM((group_rows, HEAD_TILE), jnp.bfloat16),
            pltpu.VMEM((HEAD_TILE, group_rows), jnp.float32),
            pltpu.VMEM((group_rows, head_columns), jnp.float32),
            pltpu.VMEM((group_rows, head_columns), jnp.float32),
            pltpu.VMEM((group_rows, head_columns), jnp.float32),
        ],
        name="attend_back",
    )[0]
    grad_qkv, go_chip = lax.optimization_barrier((grad_qkv, go_chip))
    qkv_sums = run(
        functools.partial(qkv_grad_kernel, data_count, 3 * local_width),
        [shaped((rows, 4 * local_width))] * count
        if ringed
        else [shaped((data_count, rows, 4 * local_width))],
        [info, hidden_one, grad_qkv, go_near, go_core, go_chip],
        2 * group_rows * width * padded,
        scratch=[pltpu.VMEM((data_count, rows, 4 * local_width), jnp.bfloat16)],
        name="qkv_grad",
    )
    if ringed:
        qkv_own, qkv_other = list(qkv_sums[0::2]), list(qkv_sums[1::2])
        qkv_taken = pair(qkv_other[1])
        mlp_ring = low(wide(after(grad_own[2], qkv_own[1])) + wide(taken) + wide(carried))
        carried = onward(mlp_ring)
        taken = pair(after(grad_other[3], mlp_ring))
    gq_near, gq_far = run(
        hidden_grad_kernel,
        [half, half],
        [info, after(grad_qkv, qkv_sums[0]), qkv_weight],
        2 * group_rows * width * padded,
        name="hidden_grad",
    )
    gq_core = hop(gq_far, 1)
    if ringed:
        qkv_ring = low(wide(after(qkv_own[1], gq_near)) + wide(qkv_taken))
        qkv_carried = onward(qkv_ring)
        qkv_taken = pair(after(qkv_other[2], qkv_ring))
    gq_send = low(wide(gq_near[tok_rows:]) + wide(gq_core[tok_rows:]))
    gq_send, mlp_chip = lax.optimization_barrier((gq_send, mlp_chip))
    gq_chip = hop(gq_send, 2)
    grad_mod = after(jnp.concatenate([grad_sums, grad_gate], axis=0), gq_send)
    grad_mod = grad_mod + hop(grad_mod, 1)
    mlp_out = wide(after(mlp_near[:tok_rows], gq_send)) + wide(mlp_core[:tok_rows]) + wide(mlp_chip)
    result = low(middle + modulation[2:3] * mlp_out)
    if ringed:
        qkv_carried, qkv_taken, carried, taken = lax.optimization_barrier(
            (qkv_carried, qkv_taken, carried, taken)
        )
        qkv_ring = low(wide(qkv_own[2]) + wide(qkv_taken) + wide(qkv_carried))
        qkv_carried = onward(qkv_ring)
        qkv_taken = pair(after(qkv_other[3], qkv_ring))
        mlp_ring = low(wide(after(grad_own[3], qkv_ring)) + wide(taken) + wide(carried))
        carried = onward(mlp_ring)
        taken = pair(after(grad_other[0], mlp_ring))
        qkv_carried, qkv_taken, gq_chip, grad_mod = lax.optimization_barrier(
            (qkv_carried, qkv_taken, gq_chip, grad_mod)
        )
        qkv_ring = low(wide(qkv_own[3]) + wide(qkv_taken) + wide(qkv_carried))
        qkv_carried = onward(qkv_ring)
        qkv_taken = pair(after(qkv_other[0], qkv_ring))
    grad_mod = grad_mod + hop(grad_mod, 2)
    grad_inputs = run(
        input_kernel,
        [shaped((tok_rows, width))],
        [info, gain, tokens, grad_middle, gq_near, gq_core, gq_chip],
        20 * tok_rows * width,
        name="input",
    )[0]
    if ringed:
        sum_mlp = low(wide(after(grad_own[0], qkv_ring)) + wide(taken) + wide(carried))
        sum_mlp, qkv_carried, qkv_taken, grad_inputs = lax.optimization_barrier(
            (sum_mlp, qkv_carried, qkv_taken, grad_inputs)
        )
        sum_qkv = low(wide(qkv_own[0]) + wide(qkv_taken) + wide(qkv_carried))
    else:
        sum_mlp = low(dp_sum_direct(grad_weights[0]))
        sum_qkv = low(dp_sum_direct(qkv_sums[0]))
    grad_mods = lax.all_to_all(
        jnp.broadcast_to(grad_mod[None], (data_count, 3, width)), "dp", 0, 0, tiled=True
    ).reshape(data_count, 3 * width)
    final_ada = lax.dot_general(
        wide(embeds), grad_mods, (((0,), (0,)), ((), ())), precision=lax.Precision.HIGHEST
    )

    final_up, final_down = run(
        functools.partial(finish_mlp_kernel, data_count),
        [shaped(w_up.shape, jnp.float32), shaped(w_down.shape, jnp.float32)],
        [info] + four(sum_mlp),
        0,
        scratch=[pltpu.VMEM((seq_count,) + block_shape, jnp.bfloat16)],
        name="finish_mlp",
    )
    final_qkv, final_out, final_gain = run(
        finish_qkv_kernel,
        [
            shaped(w_qkv.shape, jnp.float32),
            shaped(w_out.shape, jnp.float32),
            shaped((1, rows), jnp.float32),
        ],
        [info] + four(sum_qkv) + [w_qkv, wide(ln1_gain).reshape(1, rows)],
        0,
        scratch=[pltpu.VMEM((seq_count, rows, 4 * local_width), jnp.bfloat16)],
        name="finish_qkv",
    )
    return (
        result,
        grad_inputs,
        final_gain.reshape(-1),
        final_qkv,
        final_out,
        final_ada,
        final_up,
        final_down,
    )


def solution(mesh):
    placed = (
        P(("dp", "seq"), None),
        P("dp"),
        P("dp", None),
        P("dp", None),
        P("dp", None),
        P("dp", None),
        P("dp", None),
        P(("dp", "seq"), None),
        P("dp", None),
        P("dp"),
    )
    return jax.shard_map(
        body,
        mesh=mesh,
        in_specs=placed,
        out_specs=(
            P(("dp", "seq"), None),
            P(("dp", "seq"), None),
            P("dp"),
            P("dp", None),
            P("dp", None),
            P("dp", None),
            P("dp", None),
            P("dp", None),
        ),
        check_vma=False,
    )
```

```python
import functools
import math

import jax
import jax.numpy as jnp
from jax import lax
from jax.experimental import pallas as pl
from jax.experimental.pallas import tpu as pltpu
from jax.sharding import PartitionSpec as P

HEADS = 12
HEAD_DIM = 64

eps = 1e-05

MASKS = (0, 2, 1, 3)


def time_table(time_steps, model_width):
    half_dim = model_width // 2
    frequency = jnp.exp(-math.log(10000.0) * jnp.arange(half_dim, dtype=jnp.float32) / half_dim)
    angles = time_steps[:, None] * frequency[None, :]
    return jnp.concatenate([jnp.cos(angles), jnp.sin(angles)], axis=1)


def low(values_in):
    return values_in.astype(jnp.bfloat16)


def wide(values_in):
    return values_in.astype(jnp.float32)


HEAD_TILE = 128
COST = 1.0
VMEM_GRANT = 16 * 1024 * 1024
MASK_FILL = -1e30
GELU_IN = math.sqrt(2.0 / math.pi)
GELU_CUBE = 0.044715


def rope_tables(positions):
    half_dim = HEAD_DIM // 2
    column = jnp.arange(2 * HEAD_DIM, dtype=jnp.int32)
    frequency = jnp.exp(
        -math.log(10000.0) * 2.0 * (column % half_dim).astype(jnp.float32) / HEAD_DIM
    )
    angles = positions.astype(jnp.float32)[:, None] * frequency[None, :]
    sign = jnp.where(column % HEAD_DIM < half_dim, -1.0, 1.0)
    return (jnp.cos(angles), jnp.sin(angles) * sign[None, :])


def dot_nn(left, right):
    return lax.dot_general(
        left, right, (((1,), (0,)), ((), ())), preferred_element_type=jnp.float32
    )


def dot_nt(left, right):
    return lax.dot_general(
        left, right, (((1,), (1,)), ((), ())), preferred_element_type=jnp.float32
    )


def dot_tn(left, right):
    return lax.dot_general(
        left, right, (((0,), (0,)), ((), ())), preferred_element_type=jnp.float32
    )


def norm_rows(values_in):
    average = jnp.mean(values_in, axis=-1, keepdims=True)
    centred = values_in - average
    variance = jnp.mean(centred * centred, axis=-1, keepdims=True)
    scaling = lax.rsqrt(variance + eps)
    return (centred * scaling, scaling)


def swap_halves(values_in):
    column = lax.broadcasted_iota(jnp.int32, values_in.shape, 1)
    ahead = pltpu.roll(values_in, HEAD_TILE - HEAD_DIM // 2, 1)
    behind = pltpu.roll(values_in, HEAD_DIM // 2, 1)
    return jnp.where(column % HEAD_DIM < HEAD_DIM // 2, ahead, behind)


def whole(count):
    return [pl.BlockSpec(memory_space=pltpu.VMEM)] * count


def scalars():
    return [pl.BlockSpec(memory_space=pltpu.SMEM)]


def run(kernel, out_shapes, args, flops, scratch=(), name=None):
    nbytes = sum(a.size * a.dtype.itemsize for a in args)
    nbytes += sum(math.prod(o.shape) * o.dtype.itemsize for o in out_shapes)
    call = pl.pallas_call(
        kernel,
        out_shape=out_shapes,
        in_specs=scalars() + whole(len(args) - 1),
        out_specs=whole(len(out_shapes)),
        scratch_shapes=list(scratch),
        cost_estimate=pl.CostEstimate(flops=int(flops * COST), bytes_accessed=int(nbytes * COST), transcendentals=0),
        compiler_params=pltpu.CompilerParams(vmem_limit_bytes=VMEM_GRANT),
        name=name,
    )
    return call(*args)


def shaped(shape, kind=jnp.bfloat16):
    return jax.ShapeDtypeStruct(shape, kind)


FIRST, OWNER, PLACE = 2, 6, 10


def block_segment(info, block, rows, axis):
    shape = (rows, 1) if axis == 0 else (1, rows)
    position = info[FIRST + block] + lax.broadcasted_iota(jnp.int32, shape, axis)
    return (position >= info[0]).astype(jnp.int32) + (position >= info[1]).astype(jnp.int32)


def place_rows(info, chunks, first, rows, dest):
    for index, chunk in enumerate(chunks):
        at = pl.multiple_of(info[PLACE + index] * rows, rows)
        dest[pl.ds(at, rows), : chunk.shape[1]] = chunk[first : first + rows, :]


def store_blocks(info, sums_ref, outs):
    if len(outs) == 1:
        outs[0][...] = sums_ref[...]
    else:
        for index, dest in enumerate(outs):
            dest[...] = sums_ref[info[PLACE + index]]


def first_part_kernel(info, qkv_ref, out_ref, dest):
    span = dest.shape[1] // 4
    for part in range(4):

        @pl.when(info[0] == part)
        def _():
            for third in range(3):
                at = (third * 4 + part) * span
                dest[:, third * span : (third + 1) * span] = qkv_ref[:, at : at + span]
            dest[:, 3 * span :] = out_ref[:, part * span : (part + 1) * span]


def modulation_kernel(info, embed_ref, weight_ref, out_ref):
    width = out_ref.shape[2]
    for third in range(3):
        part = dot_nn(embed_ref[...], weight_ref[:, third * width : (third + 1) * width])
        for group in range(out_ref.shape[0]):
            out_ref[group, third : third + 1, :] = part[group : group + 1, :]


def second_part_kernel(count, info, up_ref, down_ref, dest):
    rows = up_ref.shape[0]
    piece = down_ref.shape[0] // 4
    for part in range(4):

        @pl.when(info[0] == part)
        def _():
            for index in range(count):
                at = (index * 4 + part) * piece
                dest[:rows, index * piece : (index + 1) * piece] = up_ref[:, at : at + piece]
            dest[rows:, :] = down_ref[part * piece : (part + 1) * piece, :]


def qkv_kernel(heads, count, info, *refs):
    gain, cos_ref, sin_ref = refs[:3]
    tok_refs = refs[3:7]
    chunks = refs[7 : 7 + count]
    hidden_ref, weight_ref, own_ref, q_ref, k_ref, v_ref = refs[7 + count :]
    rows, width = tok_refs[0].shape
    lw = heads * HEAD_DIM
    place_rows(info, chunks, 0, width // count, weight_ref)
    own_ref[...] = weight_ref[:, 3 * lw : 4 * lw]
    gain_row = gain[...]
    for block in range(4):
        normed, _ = norm_rows(wide(tok_refs[block][...]))
        hidden = low(normed * gain_row)
        here = slice(block * rows, (block + 1) * rows)
        hidden_ref[here, :] = hidden
        both = dot_nn(hidden, weight_ref[:, : 2 * lw])
        last = dot_nn(hidden, weight_ref[:, 2 * lw : 2 * lw + 2 * HEAD_TILE])
        cos_part = cos_ref[here, :]
        sin_part = sin_ref[here, :]
        turned = []
        for tile in range(2 * lw // HEAD_TILE):
            piece = both[:, tile * HEAD_TILE : (tile + 1) * HEAD_TILE]
            turned.append(piece * cos_part + swap_halves(piece) * sin_part)
        column = lax.broadcasted_iota(jnp.int32, (rows, HEAD_TILE), 1)
        segment = block_segment(info, block, rows, 0)
        first_fill = jnp.where(segment == 1, 0.0, MASK_FILL)
        second_fill = jnp.where(segment == 2, 0.0, MASK_FILL)
        q_mark = jnp.where(
            column == HEAD_DIM, first_fill, jnp.where(column == HEAD_DIM + 1, second_fill, 0.0)
        )
        first_mark = jnp.where(segment == 1, 1.0, 0.0)
        second_mark = jnp.where(segment == 2, 1.0, 0.0)
        k_mark = jnp.where(
            column == HEAD_DIM,
            first_mark,
            jnp.where(
                column == HEAD_DIM + 1, second_mark, jnp.where(column < HEAD_DIM + 5, 1.0, 0.0)
            ),
        )
        v_mark = jnp.where(column < HEAD_DIM + 2, 1.0, 0.0)
        for head in range(heads):
            q_at, k_at = head, heads + head
            q_tile = turned[q_at // 2]
            k_tile = turned[k_at // 2]
            v_tile = last[:, HEAD_TILE * (head // 2) : HEAD_TILE * (head // 2 + 1)]
            if q_at % 2:
                q_tile = pltpu.roll(q_tile, HEAD_DIM, 1)
            if k_at % 2:
                k_tile = pltpu.roll(k_tile, HEAD_DIM, 1)
            if head % 2:
                v_tile = pltpu.roll(v_tile, HEAD_DIM, 1)
            there = slice(head * HEAD_TILE, (head + 1) * HEAD_TILE)
            q_ref[here, there] = low(jnp.where(column < HEAD_DIM, q_tile * 0.125, q_mark))
            k_ref[here, there] = low(jnp.where(column < HEAD_DIM, k_tile, k_mark))
            v_ref[here, there] = low(jnp.where(column < HEAD_DIM, v_tile, v_mark))


def attend_kernel(heads, rows, info, q_ref, k_ref, v_ref, *outs):
    att_refs = outs[:4]
    stat_ref = outs[4]
    for block in range(4):
        here = slice(block * rows, (block + 1) * rows)
        column = lax.broadcasted_iota(jnp.int32, (rows, HEAD_TILE), 1)
        results = []
        for head in range(heads):
            there = slice(head * HEAD_TILE, (head + 1) * HEAD_TILE)
            queries = q_ref[here, there]
            scores = dot_nt(queries, k_ref[:, there])
            row_max = jnp.max(scores, axis=-1, keepdims=True)
            weights = low(jnp.exp(scores - row_max))
            summed = dot_nn(weights, v_ref[:, there])
            row_sum = summed[:, HEAD_DIM : HEAD_DIM + 1]
            results.append(summed / row_sum)
            minus = -(row_max + jnp.log(row_sum))
            first = low(minus)
            second = low(minus - wide(first))
            third = low(minus - wide(first) - wide(second))
            stat_ref[here, there] = jnp.where(
                column == HEAD_DIM + 2,
                first,
                jnp.where(
                    column == HEAD_DIM + 3, second, jnp.where(column == HEAD_DIM + 4, third, queries)
                ),
            )
        for head in range(0, heads, 2):
            if head + 1 < heads:
                both = jnp.where(
                    column < HEAD_DIM, results[head], pltpu.roll(results[head + 1], HEAD_DIM, 1)
                )
                att_refs[block][:, head * HEAD_DIM : (head + 2) * HEAD_DIM] = low(both)
            else:
                att_refs[block][:, head * HEAD_DIM :] = low(results[head][:, :HEAD_DIM])


def natural(info, blocks, dest):
    for block in range(4):
        dest[info[OWNER + block]] = blocks[block][...]


def middle_kernel(info, tok_ref, mod_ref, *refs):
    middle_ref, hidden_ref, att_ref, weight_ref = refs[8:]
    natural(info, refs[:4], weight_ref)
    natural(info, refs[4:8], att_ref)
    span = weight_ref.shape[2]
    for columns in range(4):
        there = slice(columns * span, (columns + 1) * span)
        total = wide(tok_ref[:, there])
        for part in range(4):
            total = total + dot_nn(
                att_ref[part], weight_ref[columns, part * span : (part + 1) * span, :]
            )
        middle_ref[:, there] = total
    normed, _ = norm_rows(middle_ref[...])
    hidden_ref[...] = low(normed * (1.0 + mod_ref[0:1, :]) + mod_ref[1:2, :])


def act_grad_kernel(count, skip, info, mod_ref, *refs):
    dy_refs = refs[:4]
    chunks = refs[4 : 4 + count]
    mlp_ref, act_ref, weight_ref = refs[4 + count :]
    rows = dy_refs[0].shape[0]
    place_rows(info, chunks, skip, weight_ref.shape[0] // count, weight_ref)
    gate = mod_ref[2:3, :]
    for block in range(4):
        here = slice(block * rows, (block + 1) * rows)
        grad_mlp = low(gate * wide(dy_refs[block][...]))
        mlp_ref[here, :] = grad_mlp
        act_ref[here, :] = low(dot_nt(grad_mlp, weight_ref[...]))


def forward_kernel(count, info, act_grad, *refs):
    hid_refs = refs[:4]
    chunks = refs[4 : 4 + count]
    act_ref, pre_ref, near_ref, far_ref, weight_ref = refs[4 + count :]
    rows = hid_refs[0].shape[0]
    place_rows(info, chunks, 0, weight_ref.shape[0] // count, weight_ref)
    for block in (2, 3, 1, 0):
        here = slice(block * rows, (block + 1) * rows)
        pre = dot_nn(hid_refs[block][...], weight_ref[...])
        square = pre * pre
        inner = jnp.tanh(GELU_IN * (pre + GELU_CUBE * (square * pre)))
        half = 0.5 * (1.0 + inner)
        act_ref[here, :] = low(pre * half)
        slope = half + 0.5 * pre * (1.0 - inner * inner) * (
            GELU_IN * (1.0 + 3.0 * GELU_CUBE * square)
        )
        grad_pre = low(wide(act_grad[here, :]) * slope)
        pre_ref[here, :] = grad_pre
        dest = near_ref if block < 2 else far_ref
        dest[(block % 2) * rows : (block % 2 + 1) * rows, :] = low(
            dot_nt(grad_pre, weight_ref[...])
        )


def weight_grad_kernel(count, info, act_ref, mlp_ref, pre_ref, *refs):
    hid_refs = refs[:4]
    outs, sums_ref = refs[4:-1], refs[-1]
    rows = hid_refs[0].shape[0]
    per = act_ref.shape[1] // count
    up = dot_tn(hid_refs[0][...], pre_ref[:rows, :])
    for block in range(1, 4):
        up = up + dot_tn(hid_refs[block][...], pre_ref[block * rows : (block + 1) * rows, :])
    for index in range(count):
        sums_ref[index, :per, :] = low(up[index * per : (index + 1) * per, :])
    down = dot_tn(act_ref[...], mlp_ref[...])
    for index in range(count):
        sums_ref[index, per:, :] = low(down[index * per : (index + 1) * per, :])
    store_blocks(info, sums_ref, outs)


def down_kernel(count, skip, info, act_ref, *refs):
    dy_refs = refs[:4]
    chunks = refs[4 : 4 + count]
    near_ref, far_ref, gate_ref, weight_ref = refs[4 + count :]
    rows = dy_refs[0].shape[0]
    place_rows(info, chunks, skip, weight_ref.shape[0] // count, weight_ref)
    total = jnp.zeros(gate_ref.shape, jnp.float32)
    for block in (2, 3, 1, 0):
        here = slice(block * rows, (block + 1) * rows)
        part = dot_nn(act_ref[here, :], weight_ref[...])
        total = total + jnp.sum(wide(dy_refs[block][...]) * part, axis=0, keepdims=True)
        dest = near_ref if block < 2 else far_ref
        dest[(block % 2) * rows : (block % 2 + 1) * rows, :] = low(part)
    gate_ref[...] = total


def branch_kernel(info, mod_ref, middle_ref, dy_ref, own_ref, core_ref, chip_ref, *refs):
    mid_ref, branch_ref, sums_ref = refs[4:7]
    att_refs = (refs[7], refs[8], branch_ref.at[4], refs[9])
    weight_ref = refs[10]
    natural(info, refs[:4], weight_ref)
    rows = dy_ref.shape[0]
    grad_hidden = wide(own_ref[:rows, :]) + wide(core_ref[:rows, :]) + wide(chip_ref[...])
    normed, scaling = norm_rows(middle_ref[...])
    sums_ref[0:1, :] = jnp.sum(grad_hidden * normed, axis=0, keepdims=True)
    sums_ref[1:2, :] = jnp.sum(grad_hidden, axis=0, keepdims=True)
    grad_normed = grad_hidden * (1.0 + mod_ref[0:1, :])
    first_mean = jnp.mean(grad_normed, axis=-1, keepdims=True)
    second_mean = jnp.mean(grad_normed * normed, axis=-1, keepdims=True)
    mid_ref[...] = wide(dy_ref[...]) + scaling * (grad_normed - first_mean - normed * second_mean)
    span = weight_ref.shape[2]
    for columns in range(4):
        branch_ref[columns] = low(mid_ref[:, columns * span : (columns + 1) * span])
    for block, dest in enumerate(att_refs):
        at = pl.multiple_of(info[OWNER + block] * span, HEAD_DIM)
        total = dot_nt(branch_ref[0], weight_ref[0, pl.ds(at, span), :])
        for columns in range(1, 4):
            total = total + dot_nt(branch_ref[columns], weight_ref[columns, pl.ds(at, span), :])
        dest[...] = low(total)


def out_grad_kernel(info, att_ref, core_att_ref, branch_ref, core_branch_ref, near_ref):
    span = branch_ref.shape[2]
    for block in range(2):
        owner = info[OWNER + block]
        branch, core_branch = branch_ref[owner], core_branch_ref[owner]
        for part in range(4):
            near_ref[block, part * span : (part + 1) * span, :] = low(
                dot_tn(att_ref[part], branch) + dot_tn(core_att_ref[part], core_branch)
            )


def attend_back_kernel(heads, rows, info, cos_ref, sin_ref, q_ref, k_ref, v_ref, *refs):
    att = refs[:4]
    grads = (refs[4], refs[5], refs[6].at[4], refs[7])
    out_ref, gx_ref, turn_ref, dq_ref, dk_ref, dv_ref = refs[8:]
    column = lax.broadcasted_iota(jnp.int32, (rows, HEAD_TILE), 1)

    def tile_of(ref, head):
        if head % 2 or head + 1 < heads:
            tile = wide(ref[:, HEAD_TILE * (head // 2) : HEAD_TILE * (head // 2) + HEAD_TILE])
            return pltpu.roll(tile, HEAD_DIM, 1) if head % 2 else tile
        last = wide(ref[:, head * HEAD_DIM :])
        return jnp.concatenate([last, jnp.zeros_like(last)], axis=1)

    for head in range(heads):
        there = slice(head * HEAD_TILE, (head + 1) * HEAD_TILE)
        for block in range(4):
            here = slice(block * rows, (block + 1) * rows)
            grad = jnp.where(column < HEAD_DIM, tile_of(grads[block], head), 0.0)
            minus = -jnp.sum(grad * tile_of(att[block], head), axis=-1, keepdims=True)
            first = wide(low(minus))
            gx_ref[here, :] = low(
                jnp.where(
                    column == HEAD_DIM,
                    first,
                    jnp.where(column == HEAD_DIM + 1, minus - first, grad),
                )
            )
        for block in range(4):
            here = slice(block * rows, (block + 1) * rows)
            keys = k_ref[here, there]
            probs = jnp.exp(dot_nt(keys, q_ref[:, there]))
            prob_grad = dot_nt(v_ref[here, there], gx_ref[...])
            score_grad = low(probs * prob_grad)
            dv_ref[here, there] = dot_nn(low(probs), gx_ref[...])
            dk_ref[here, there] = dot_nn(score_grad, q_ref[:, there])
            part = dot_tn(keys, score_grad)
            if block == 0:
                turn_ref[...] = part
            else:
                turn_ref[...] += part
        dq_ref[:, there] = jnp.transpose(turn_ref[...]) * 0.125

    for block in range(4):
        here = slice(block * rows, (block + 1) * rows)
        heads_of = [dq_ref[here, h * HEAD_TILE : (h + 1) * HEAD_TILE] for h in range(heads)]
        heads_of += [dk_ref[here, h * HEAD_TILE : (h + 1) * HEAD_TILE] for h in range(heads)]
        heads_of += [dv_ref[here, h * HEAD_TILE : (h + 1) * HEAD_TILE] for h in range(heads)]
        heads_of.append(jnp.zeros((rows, HEAD_TILE), jnp.float32))
        for tile in range((3 * heads + 1) // 2):
            both = jnp.where(
                column < HEAD_DIM,
                heads_of[2 * tile],
                pltpu.roll(heads_of[2 * tile + 1], HEAD_DIM, 1),
            )
            if tile < heads:
                both = both * cos_ref[here, :] - swap_halves(both) * sin_ref[here, :]
            out_ref[here, tile * HEAD_TILE : (tile + 1) * HEAD_TILE] = low(both)


def hidden_grad_kernel(info, grad_ref, weight_ref, near_ref, far_ref):
    rows = near_ref.shape[0] // 2
    span = grad_ref.shape[1]
    for block in (2, 3, 1, 0):
        dest = near_ref if block < 2 else far_ref
        at = (block % 2) * rows
        here = slice(block * rows, (block + 1) * rows)
        dest[at : at + rows, :] = low(dot_nt(grad_ref[here, :], weight_ref[:, :span]))


def qkv_grad_kernel(count, used, info, hidden_ref, grad_ref, near_ref, chip_ref, *refs):
    outs, sums_ref = refs[:-1], refs[-1]
    total = dot_tn(hidden_ref[...], grad_ref[...])
    out_total = wide(near_ref[0]) + wide(chip_ref[0])
    per = total.shape[0] // count
    for index in range(count):
        here = slice(index * per, (index + 1) * per)
        sums_ref[index, :, :used] = low(total[here, :used])
        sums_ref[index, :, used:] = low(out_total[here, :])
    store_blocks(info, sums_ref, outs)


def input_kernel(info, gain, tok_ref, mid_ref, own_ref, core_ref, chip_ref, out_ref):
    rows = tok_ref.shape[0]
    grad_hidden = wide(own_ref[:rows, :]) + wide(core_ref[:rows, :]) + wide(chip_ref[...])
    normed, scaling = norm_rows(wide(tok_ref[...]))
    grad_normed = grad_hidden * gain[...]
    first_mean = jnp.mean(grad_normed, axis=-1, keepdims=True)
    second_mean = jnp.mean(grad_normed * normed, axis=-1, keepdims=True)
    out_ref[...] = low(
        mid_ref[...] + scaling * (grad_normed - first_mean - normed * second_mean)
    )


def finish_mlp_kernel(count, info, *refs):
    blocks = refs[:4]
    up_ref, down_ref, all_ref = refs[4:]
    natural(info, blocks, all_ref)
    rows = up_ref.shape[0]
    piece = down_ref.shape[0] // 4
    for part in range(4):
        value = wide(all_ref[part])
        for index in range(count):
            at = (index * 4 + part) * piece
            up_ref[:, at : at + piece] = value[:rows, index * piece : (index + 1) * piece]
        down_ref[part * piece : (part + 1) * piece, :] = value[rows:, :]


def finish_qkv_kernel(info, *refs):
    blocks = refs[:4]
    weight_ref, gain_ref, out_ref, own_ref, sums_ref, all_ref = refs[4:]
    natural(info, blocks, all_ref)
    span = all_ref.shape[2] // 4
    total = jnp.zeros((out_ref.shape[0], 1), jnp.float32)
    for part in range(4):
        value = wide(all_ref[part])
        for third in range(3):
            at = (third * 4 + part) * span
            piece = value[:, third * span : (third + 1) * span]
            total = total + jnp.sum(
                wide(weight_ref[:, at : at + span]) * piece, axis=1, keepdims=True
            )
            out_ref[:, at : at + span] = piece
        own_ref[:, part * span : (part + 1) * span] = value[:, 3 * span :]
    turned = jnp.transpose(jnp.broadcast_to(total, (total.shape[0], HEAD_TILE)))
    sums_ref[...] = turned[0:1, :] / gain_ref[...]


def hop(values_in, mask):
    return lax.ppermute(values_in, "seq", [(i, i ^ mask) for i in range(lax.axis_size("seq"))])


def ring_of(count):
    return [0] + list(range(1, count, 2)) + [i for i in range(count - 1, 0, -1) if i % 2 == 0]


def ring_next(data_count):
    outer = data_count // 2
    ring = ring_of(outer)
    follow = {ring[i]: ring[(i + 1) % outer] for i in range(outer)}
    return [(z * 2 + y, follow[z] * 2 + y) for z in range(outer) for y in range(2)]


def pair(values_in):
    return lax.ppermute(values_in, "dp", [(i, i ^ 1) for i in range(lax.axis_size("dp"))])


def dp_sum_direct(blocks):
    data_count = lax.axis_size("dp")
    if data_count != 8:
        return wide(lax.psum_scatter(blocks, "dp", scatter_dimension=0, tiled=False))
    return jnp.sum(wide(lax.all_to_all(blocks, "dp", 0, 0, tiled=True)), axis=0)


def after(values_in, *earlier):
    return lax.optimization_barrier((values_in,) + earlier)[0]


def onward(values_in):
    return lax.ppermute(values_in, "dp", ring_next(lax.axis_size("dp")))


def kernel_info(layout, rank, tok_rows):
    data_count = lax.axis_size("dp")
    index = lax.axis_index("dp")
    column = jnp.arange(PLACE + 8, dtype=jnp.int32)

    def owner(block):
        return rank ^ ((block & 1) * 2 + block // 2)

    values = jnp.where(column == 0, layout[0, 0], layout[0, 1])
    values = jnp.where(column >= FIRST, owner(column - FIRST) * tok_rows, values)
    values = jnp.where(column >= OWNER, owner(column - OWNER), values)
    if data_count == 8:
        step = column - PLACE
        at = index // 2
        at = ((at ^ (at // 2)) - step // 2) & 3
        place = (at ^ (at // 2)) * 2 + ((index + step) & 1)
    else:
        place = jnp.zeros_like(column)
    return jnp.where(column >= PLACE, place, values)


def gathered_whole(chunk, sizes):
    gathered = lax.all_gather(chunk, "dp", axis=0)
    parts = []
    at = 0
    for size in sizes:
        parts.append(gathered[:, at : at + size].reshape(-1, chunk.shape[1]))
        at += size
    return [jnp.concatenate(parts, axis=0)]


def four(values_in):
    chip = hop(values_in, 2)
    return [values_in, chip, hop(values_in, 1), hop(chip, 1)]


def beyond(values_in, mask):
    return lax.ppermute(values_in, "dp", [(i, i ^ mask) for i in range(lax.axis_size("dp"))])


def halve_to_own(parts):
    index = lax.axis_index("dp")
    mask = 1
    while parts.shape[0] > 1:
        pairs = parts.reshape((parts.shape[0] // 2, 2) + parts.shape[1:])
        odd = (index & mask) != 0
        kept = jnp.where(odd, pairs[:, 1], pairs[:, 0])
        sent = jnp.where(odd, pairs[:, 0], pairs[:, 1])
        parts = kept + beyond(sent, mask)
        mask *= 2
    return parts[0]


def double_to_all(row):
    index = lax.axis_index("dp")
    parts = row[None]
    mask = 1
    while mask < lax.axis_size("dp"):
        other = beyond(parts, mask)
        odd = (index & mask) != 0
        parts = jnp.where(
            odd,
            jnp.concatenate([other, parts], axis=0),
            jnp.concatenate([parts, other], axis=0),
        )
        mask *= 2
    return parts


def body(tokens, ln1_gain, w_qkv, w_out, w_ada, w_up, w_down, out_grad, layout, timestep):
    seq_count = lax.axis_size("seq")
    data_count = lax.axis_size("dp")
    ringed = data_count == 8
    rank = lax.axis_index("seq")
    tok_rows, width = tokens.shape
    group_rows = tok_rows * seq_count
    heads_local = HEADS // seq_count
    local_width = heads_local * HEAD_DIM
    head_columns = heads_local * HEAD_TILE
    padded = (3 * heads_local + 1) // 2 * HEAD_TILE
    rows = w_qkv.shape[0]
    hidden = w_up.shape[1] // seq_count
    down_piece = w_down.shape[0] // seq_count
    rank_word = rank.reshape(1).astype(jnp.int32)

    tok_chip = hop(tokens, 2)
    first = run(
        first_part_kernel,
        [shaped((rows, 4 * local_width))],
        [rank_word, w_qkv, w_out],
        0,
        name="first_part",
    )[0]
    if ringed:
        held = [first, onward(first)]
        beside = [pair(first)]
        held[1], beside[0], tokens = lax.optimization_barrier((held[1], beside[0], tokens))
        held.append(onward(held[1]))
        beside.append(pair(held[1]))
        tok_core = hop(tokens, 1)
        held[2], beside[1], tok_chip, tok_core = lax.optimization_barrier(
            (held[2], beside[1], tok_chip, tok_core)
        )
        held.append(onward(held[2]))
        beside.append(pair(held[2]))
        tok_both = hop(tok_chip, 1)
    else:
        tok_core, tok_both = hop(tokens, 1), hop(tok_chip, 1)
    tok_blocks = [tokens, tok_chip, tok_core, tok_both]

    embed = low(time_table(wide(timestep), width))
    sent = jnp.stack(
        [embed.reshape(data_count, rows), jnp.broadcast_to(ln1_gain, (data_count, rows))], axis=1
    )
    taken = lax.all_to_all(sent, "dp", 0, 0, tiled=True)
    embeds = taken[:, 0]
    gain = wide(taken[:, 1].reshape(1, width))
    mod_parts = run(
        modulation_kernel,
        [shaped((data_count, 3, width), jnp.float32)],
        [rank_word, after(embeds, held[2]) if ringed else embeds, w_ada],
        2 * data_count * rows * w_ada.shape[1],
        name="modulation",
    )[0]

    info = kernel_info(layout, rank, tok_rows)
    starts = info[FIRST:OWNER]
    if ringed:
        starts = after(starts, held[2])
    positions = (starts[:, None] + jnp.arange(tok_rows, dtype=jnp.int32)[None, :]).reshape(-1)
    cos_table, sin_table = rope_tables(positions)

    second = run(
        functools.partial(second_part_kernel, data_count),
        [shaped((rows + down_piece, width))],
        [rank_word, w_up, w_down],
        0,
        name="second_part",
    )[0]
    if ringed:
        held[3], beside[2], second, *rest = lax.optimization_barrier(
            (held[3], beside[2], second, mod_parts, info, cos_table, sin_table, tok_blocks, gain)
        )
        mod_parts, info, cos_table, sin_table, tok_blocks, gain = rest
        beside.append(pair(held[3]))
        first_chunks = [part for both in zip(held, beside) for part in both]
        held = [second, onward(second)]
        beside = [pair(after(second, beside[3]))]
        dy_chip = hop(after(out_grad, held[0]), 2)
    else:
        first_chunks = gathered_whole(first, [rows])
        second_chunks = gathered_whole(second, [rows, down_piece])
        dy_chip = hop(out_grad, 2)
    modulation = halve_to_own(mod_parts)
    count = len(first_chunks)
    up_rows = rows * (data_count // count)

    hidden_one, qkv_weight, own_out, queries, keys, values = run(
        functools.partial(qkv_kernel, heads_local, count),
        [
            shaped((group_rows, width)),
            shaped((width, 4 * local_width)),
            shaped((width, local_width)),
            shaped((group_rows, head_columns)),
            shaped((group_rows, head_columns)),
            shaped((group_rows, head_columns)),
        ],
        [info, gain, cos_table, sin_table] + tok_blocks + first_chunks,
        2 * group_rows * width * padded,
        name="qkv",
    )
    if ringed:
        queries, own_out, held[1], beside[0] = lax.optimization_barrier(
            (queries, own_out, held[1], beside[0])
        )
        beside.append(pair(held[1]))
        held.append(onward(held[1]))
    chip_out = hop(own_out, 2)
    core_out = hop(own_out, 1)
    *att_parts, marked = run(
        functools.partial(attend_kernel, heads_local, tok_rows),
        [shaped((tok_rows, local_width))] * 4 + [shaped((group_rows, head_columns))],
        [info, queries, keys, values],
        4 * group_rows * group_rows * head_columns,
        name="attend",
    )
    if ringed:
        att_parts, held[2], beside[1], chip_out, core_out, dy_chip = lax.optimization_barrier(
            (att_parts, held[2], beside[1], chip_out, core_out, dy_chip)
        )
        beside.append(pair(held[2]))
        held.append(onward(held[2]))
    att_own = [att_parts[0]] + [hop(att_parts[j], MASKS[j]) for j in (1, 2, 3)]
    out_blocks = [own_out, chip_out, core_out, hop(after(chip_out, att_own[2]), 1)]
    if ringed:
        att_own, held[3], beside[2] = lax.optimization_barrier((att_own, held[3], beside[2]))
    middle, hidden_two, att_ordered = run(
        middle_kernel,
        [
            shaped((tok_rows, width), jnp.float32),
            shaped((tok_rows, width)),
            shaped((seq_count, tok_rows, local_width)),
        ],
        [info, tokens, modulation] + out_blocks + att_own,
        2 * tok_rows * width * width,
        scratch=[pltpu.VMEM((seq_count, width, local_width), jnp.bfloat16)],
        name="middle",
    )

    chip_hidden = hop(hidden_two, 2)
    if ringed:
        beside.append(pair(after(held[3], hidden_two)))
        second_chunks = [part for both in zip(held, beside) for part in both]
    dy_blocks = [out_grad, dy_chip, hop(out_grad, 1), hop(dy_chip, 1)]
    grad_mlp, grad_act = run(
        functools.partial(act_grad_kernel, count, up_rows),
        [shaped((group_rows, width)), shaped((group_rows, hidden))],
        [info, modulation] + dy_blocks + second_chunks,
        2 * group_rows * width * hidden,
        scratch=[pltpu.VMEM((hidden, width), jnp.bfloat16)],
        name="act_grad",
    )
    hid_blocks = [
        hidden_two,
        chip_hidden,
        hop(hidden_two, 1),
        hop(after(chip_hidden, grad_act), 1),
    ]
    half = shaped((group_rows // 2, width))
    activated, grad_pre, gh_near, gh_far = run(
        functools.partial(forward_kernel, count),
        [shaped((group_rows, hidden)), shaped((group_rows, hidden)), half, half],
        [info, grad_act] + hid_blocks + second_chunks,
        4 * group_rows * width * hidden,
        scratch=[pltpu.VMEM((width, hidden), jnp.bfloat16)],
        name="forward",
    )
    block_shape = (rows + down_piece, width)
    grad_weights = run(
        functools.partial(weight_grad_kernel, data_count),
        [shaped(block_shape)] * count if ringed else [shaped((data_count,) + block_shape)],
        [info, activated, grad_mlp, grad_pre] + hid_blocks,
        4 * group_rows * width * hidden,
        scratch=[pltpu.VMEM((data_count,) + block_shape, jnp.bfloat16)],
        name="weight_grad",
    )
    gh_core = hop(gh_far, 1)
    gh_core, grad_weights = lax.optimization_barrier((gh_core, grad_weights))
    gh_send = low(wide(gh_near[tok_rows:]) + wide(gh_core[tok_rows:]))
    gh_chip = hop(gh_send, 2)
    mlp_near, mlp_far, grad_gate = run(
        functools.partial(down_kernel, count, up_rows),
        [half, half, shaped((1, width), jnp.float32)],
        [info, after(activated, gh_send)] + dy_blocks + second_chunks,
        2 * group_rows * width * hidden,
        scratch=[pltpu.VMEM((hidden, width), jnp.bfloat16)],
        name="down",
    )
    if ringed:
        mlp_keep, mlp_give = list(grad_weights[0::2]), list(grad_weights[1::2])
        mlp_taken = pair(after(mlp_give[1], gh_send))
        gh_chip, mlp_far, mlp_taken = lax.optimization_barrier((gh_chip, mlp_far, mlp_taken))
        mlp_ring = low(wide(mlp_keep[1]) + wide(mlp_taken))
        gh_chip, mlp_ring = lax.optimization_barrier((gh_chip, mlp_ring))
        mlp_carried = onward(mlp_ring)
        mlp_taken = pair(after(mlp_give[2], mlp_ring))
    else:
        gh_chip, mlp_far = lax.optimization_barrier((gh_chip, mlp_far))
    mlp_core = hop(mlp_far, 1)
    core_attended = hop(after(att_ordered, gh_chip), 1)

    grad_middle, branch, grad_sums, *grad_parts = run(
        branch_kernel,
        [
            shaped((tok_rows, width), jnp.float32),
            shaped((seq_count + 1, tok_rows, local_width)),
            shaped((2, width), jnp.float32),
        ]
        + [shaped((tok_rows, local_width))] * 3,
        [info, modulation, after(middle, mlp_near), out_grad, gh_near, gh_core, gh_chip]
        + out_blocks,
        2 * tok_rows * width * width,
        scratch=[pltpu.VMEM((seq_count, width, local_width), jnp.bfloat16)],
        name="branch",
    )
    grad_parts, mlp_core = lax.optimization_barrier((grad_parts, mlp_core))
    core_branch = hop(branch, 1)
    grad_att = [grad_parts[0], hop(grad_parts[1], 2), core_branch, hop(grad_parts[2], 3)]
    out_sums = run(
        out_grad_kernel,
        [shaped((2, width, local_width))],
        [info, att_ordered, core_attended, branch, core_branch],
        2 * tok_rows * width * width,
        name="out_grad",
    )[0]
    grad_mod = jnp.concatenate([grad_sums, grad_gate], axis=0)

    if ringed:
        del grad_att[2]
        grad_att, out_sums, grad_mod, mlp_taken, mlp_carried = lax.optimization_barrier(
            (grad_att, out_sums, grad_mod, mlp_taken, mlp_carried)
        )
        grad_att.insert(2, core_branch)
        mlp_ring = low(wide(mlp_keep[2]) + wide(mlp_taken) + wide(mlp_carried))
        mlp_carried = onward(mlp_ring)
        mlp_taken = pair(after(mlp_give[3], mlp_ring))
    out_chip = hop(out_sums[1:], 2)
    mod_core = hop(grad_mod, 1)
    grad_qkv = run(
        functools.partial(attend_back_kernel, heads_local, tok_rows),
        [shaped((group_rows, padded))],
        [info, cos_table, sin_table, marked, keys, values] + att_parts + grad_att,
        10 * group_rows * group_rows * head_columns,
        scratch=[
            pltpu.VMEM((group_rows, HEAD_TILE), jnp.bfloat16),
            pltpu.VMEM((HEAD_TILE, group_rows), jnp.float32),
            pltpu.VMEM((group_rows, head_columns), jnp.float32),
            pltpu.VMEM((group_rows, head_columns), jnp.float32),
            pltpu.VMEM((group_rows, head_columns), jnp.float32),
        ],
        name="attend_back",
    )[0]
    grad_qkv, out_chip, mod_core = lax.optimization_barrier((grad_qkv, out_chip, mod_core))
    grad_mod = grad_mod + mod_core
    mod_chip = hop(grad_mod, 2)
    mlp_send = low(wide(after(mlp_near[tok_rows:], grad_qkv)) + wide(mlp_core[tok_rows:]))
    if ringed:
        grad_qkv, mlp_taken, mlp_carried = lax.optimization_barrier(
            (grad_qkv, mlp_taken, mlp_carried)
        )
    qkv_sums = run(
        functools.partial(qkv_grad_kernel, data_count, 3 * local_width),
        [shaped((rows, 4 * local_width))] * count
        if ringed
        else [shaped((data_count, rows, 4 * local_width))],
        [info, hidden_one, grad_qkv, out_sums, out_chip],
        2 * group_rows * width * padded,
        scratch=[pltpu.VMEM((data_count, rows, 4 * local_width), jnp.bfloat16)],
        name="qkv_grad",
    )
    gq_near, gq_far = run(
        hidden_grad_kernel,
        [half, half],
        [info, after(grad_qkv, qkv_sums[0]), qkv_weight],
        2 * group_rows * width * padded,
        name="hidden_grad",
    )
    if ringed:
        qkv_keep, qkv_give = list(qkv_sums[0::2]), list(qkv_sums[1::2])
        qkv_taken = pair(qkv_give[1])
        mlp_ring = low(wide(mlp_keep[3]) + wide(mlp_taken) + wide(mlp_carried))
        mlp_carried = onward(mlp_ring)
        mlp_taken = pair(after(mlp_give[0], mlp_ring))
        gq_far, qkv_taken = lax.optimization_barrier((gq_far, qkv_taken))
        qkv_ring = low(wide(qkv_keep[1]) + wide(qkv_taken))
        qkv_carried = onward(qkv_ring)
        qkv_taken = pair(after(qkv_give[2], qkv_ring))
    gq_core = hop(gq_far, 1)
    gq_send = low(wide(gq_near[tok_rows:]) + wide(gq_core[tok_rows:]))
    gq_chip = hop(gq_send, 2)
    grad_mod = grad_mod + after(mod_chip, gq_send)
    grad_mods = double_to_all(grad_mod).reshape(data_count, 3 * width)
    if ringed:
        qkv_carried, qkv_taken, mlp_carried, mlp_taken, gq_send = lax.optimization_barrier(
            (qkv_carried, qkv_taken, mlp_carried, mlp_taken, gq_send)
        )
        qkv_ring = low(wide(qkv_keep[2]) + wide(qkv_taken) + wide(qkv_carried))
        qkv_carried = onward(qkv_ring)
        qkv_taken = pair(after(qkv_give[3], qkv_ring))
        sum_mlp = low(wide(mlp_keep[0]) + wide(mlp_taken) + wide(mlp_carried))
    else:
        sum_mlp = low(dp_sum_direct(grad_weights[0]))
    grad_inputs = run(
        input_kernel,
        [shaped((tok_rows, width))],
        [info, gain, tokens, grad_middle, gq_near, gq_core, gq_chip],
        20 * tok_rows * width,
        name="input",
    )[0]
    if ringed:
        qkv_carried, qkv_taken, gq_chip, sum_mlp = lax.optimization_barrier(
            (qkv_carried, qkv_taken, gq_chip, sum_mlp)
        )
        qkv_ring = low(wide(qkv_keep[3]) + wide(qkv_taken) + wide(qkv_carried))
        qkv_carried = onward(qkv_ring)
        qkv_taken = pair(after(qkv_give[0], qkv_ring))
    mlp_blocks = four(sum_mlp)
    if ringed:
        qkv_carried, qkv_taken, mlp_blocks = lax.optimization_barrier(
            (qkv_carried, qkv_taken, mlp_blocks)
        )
        sum_qkv = low(wide(qkv_keep[0]) + wide(qkv_taken) + wide(qkv_carried))
    else:
        sum_qkv = low(dp_sum_direct(qkv_sums[0]))
    mlp_chip = hop(after(mlp_send, gq_chip), 2)
    mlp_out = wide(mlp_near[:tok_rows]) + wide(mlp_core[:tok_rows]) + wide(mlp_chip)
    result = low(middle + modulation[2:3] * mlp_out)
    final_ada = lax.dot_general(
        wide(embeds), grad_mods, (((0,), (0,)), ((), ())), precision=lax.Precision.HIGHEST
    )

    final_up, final_down = run(
        functools.partial(finish_mlp_kernel, data_count),
        [shaped(w_up.shape, jnp.float32), shaped(w_down.shape, jnp.float32)],
        [info] + mlp_blocks,
        0,
        scratch=[pltpu.VMEM((seq_count,) + block_shape, jnp.bfloat16)],
        name="finish_mlp",
    )
    final_qkv, final_out, final_gain = run(
        finish_qkv_kernel,
        [
            shaped(w_qkv.shape, jnp.float32),
            shaped(w_out.shape, jnp.float32),
            shaped((1, rows), jnp.float32),
        ],
        [info] + four(sum_qkv) + [w_qkv, wide(ln1_gain).reshape(1, rows)],
        0,
        scratch=[pltpu.VMEM((seq_count, rows, 4 * local_width), jnp.bfloat16)],
        name="finish_qkv",
    )
    return (
        result,
        grad_inputs,
        final_gain.reshape(-1),
        final_qkv,
        final_out,
        final_ada,
        final_up,
        final_down,
    )


def solution(mesh):
    placed = (
        P(("dp", "seq"), None),
        P("dp"),
        P("dp", None),
        P("dp", None),
        P("dp", None),
        P("dp", None),
        P("dp", None),
        P(("dp", "seq"), None),
        P("dp", None),
        P("dp"),
    )
    return jax.shard_map(
        body,
        mesh=mesh,
        in_specs=placed,
        out_specs=(
            P(("dp", "seq"), None),
            P(("dp", "seq"), None),
            P("dp"),
            P("dp", None),
            P("dp", None),
            P("dp", None),
            P("dp", None),
            P("dp", None),
        ),
        check_vma=False,
    )
```

```python
import functools
import math

import jax
import jax.numpy as jnp
from jax import lax
from jax.experimental import pallas as pl
from jax.experimental.pallas import tpu as pltpu
from jax.sharding import PartitionSpec as P

HEADS = 12
HEAD_DIM = 64

eps = 1e-05

MASKS = (0, 2, 1, 3)


def time_table(time_steps, model_width):
    half_dim = model_width // 2
    frequency = jnp.exp(-math.log(10000.0) * jnp.arange(half_dim, dtype=jnp.float32) / half_dim)
    angles = time_steps[:, None] * frequency[None, :]
    return jnp.concatenate([jnp.cos(angles), jnp.sin(angles)], axis=1)


def low(values_in):
    return values_in.astype(jnp.bfloat16)


def wide(values_in):
    return values_in.astype(jnp.float32)


HEAD_TILE = 128
COST = 1.0
VMEM_GRANT = 16 * 1024 * 1024
MASK_FILL = -1e30
GELU_IN = math.sqrt(2.0 / math.pi)
GELU_CUBE = 0.044715


def rope_tables(positions):
    half_dim = HEAD_DIM // 2
    column = jnp.arange(2 * HEAD_DIM, dtype=jnp.int32)
    frequency = jnp.exp(
        -math.log(10000.0) * 2.0 * (column % half_dim).astype(jnp.float32) / HEAD_DIM
    )
    angles = positions.astype(jnp.float32)[:, None] * frequency[None, :]
    sign = jnp.where(column % HEAD_DIM < half_dim, -1.0, 1.0)
    return (jnp.cos(angles), jnp.sin(angles) * sign[None, :])


def dot_nn(left, right):
    return lax.dot_general(
        left, right, (((1,), (0,)), ((), ())), preferred_element_type=jnp.float32
    )


def dot_nt(left, right):
    return lax.dot_general(
        left, right, (((1,), (1,)), ((), ())), preferred_element_type=jnp.float32
    )


def dot_tn(left, right):
    return lax.dot_general(
        left, right, (((0,), (0,)), ((), ())), preferred_element_type=jnp.float32
    )


def norm_rows(values_in):
    average = jnp.mean(values_in, axis=-1, keepdims=True)
    centred = values_in - average
    variance = jnp.mean(centred * centred, axis=-1, keepdims=True)
    scaling = lax.rsqrt(variance + eps)
    return (centred * scaling, scaling)


def swap_halves(values_in):
    column = lax.broadcasted_iota(jnp.int32, values_in.shape, 1)
    ahead = pltpu.roll(values_in, HEAD_TILE - HEAD_DIM // 2, 1)
    behind = pltpu.roll(values_in, HEAD_DIM // 2, 1)
    return jnp.where(column % HEAD_DIM < HEAD_DIM // 2, ahead, behind)


def whole(count):
    return [pl.BlockSpec(memory_space=pltpu.VMEM)] * count


def scalars():
    return [pl.BlockSpec(memory_space=pltpu.SMEM)]


def run(kernel, out_shapes, args, flops, scratch=(), name=None):
    nbytes = sum(a.size * a.dtype.itemsize for a in args)
    nbytes += sum(math.prod(o.shape) * o.dtype.itemsize for o in out_shapes)
    call = pl.pallas_call(
        kernel,
        out_shape=out_shapes,
        in_specs=scalars() + whole(len(args) - 1),
        out_specs=whole(len(out_shapes)),
        scratch_shapes=list(scratch),
        cost_estimate=pl.CostEstimate(flops=int(flops * COST), bytes_accessed=int(nbytes * COST), transcendentals=0),
        compiler_params=pltpu.CompilerParams(vmem_limit_bytes=VMEM_GRANT),
        name=name,
    )
    return call(*args)


def shaped(shape, kind=jnp.bfloat16):
    return jax.ShapeDtypeStruct(shape, kind)


FIRST, OWNER, PLACE = 2, 6, 10


def block_segment(info, block, rows, axis):
    shape = (rows, 1) if axis == 0 else (1, rows)
    position = info[FIRST + block] + lax.broadcasted_iota(jnp.int32, shape, axis)
    return (position >= info[0]).astype(jnp.int32) + (position >= info[1]).astype(jnp.int32)


def place_rows(info, chunks, first, rows, dest):
    for index, chunk in enumerate(chunks):
        at = pl.multiple_of(info[PLACE + index] * rows, rows)
        dest[pl.ds(at, rows), : chunk.shape[1]] = chunk[first : first + rows, :]


def store_blocks(info, sums_ref, outs):
    if len(outs) == 1:
        outs[0][...] = sums_ref[...]
    else:
        for index, dest in enumerate(outs):
            dest[...] = sums_ref[info[PLACE + index]]


def first_part_kernel(info, qkv_ref, out_ref, dest):
    span = dest.shape[1] // 4
    for part in range(4):

        @pl.when(info[0] == part)
        def _():
            for third in range(3):
                at = (third * 4 + part) * span
                dest[:, third * span : (third + 1) * span] = qkv_ref[:, at : at + span]
            dest[:, 3 * span :] = out_ref[:, part * span : (part + 1) * span]


def modulation_kernel(info, embed_ref, weight_ref, out_ref):
    width = out_ref.shape[2]
    for third in range(3):
        part = dot_nn(embed_ref[...], weight_ref[:, third * width : (third + 1) * width])
        for group in range(out_ref.shape[0]):
            out_ref[group, third : third + 1, :] = part[group : group + 1, :]


def second_part_kernel(count, info, up_ref, down_ref, dest):
    rows = up_ref.shape[0]
    piece = down_ref.shape[0] // 4
    for part in range(4):

        @pl.when(info[0] == part)
        def _():
            for index in range(count):
                at = (index * 4 + part) * piece
                dest[:rows, index * piece : (index + 1) * piece] = up_ref[:, at : at + piece]
            dest[rows:, :] = down_ref[part * piece : (part + 1) * piece, :]


def qkv_kernel(heads, count, info, *refs):
    gain, cos_ref, sin_ref = refs[:3]
    tok_refs = refs[3:7]
    chunks = refs[7 : 7 + count]
    hidden_ref, weight_ref, own_ref, q_ref, k_ref, v_ref = refs[7 + count :]
    rows, width = tok_refs[0].shape
    lw = heads * HEAD_DIM
    place_rows(info, chunks, 0, width // count, weight_ref)
    own_ref[...] = weight_ref[:, 3 * lw : 4 * lw]
    gain_row = gain[...]
    for block in range(4):
        normed, _ = norm_rows(wide(tok_refs[block][...]))
        hidden = low(normed * gain_row)
        here = slice(block * rows, (block + 1) * rows)
        hidden_ref[here, :] = hidden
        both = dot_nn(hidden, weight_ref[:, : 2 * lw])
        last = dot_nn(hidden, weight_ref[:, 2 * lw : 2 * lw + 2 * HEAD_TILE])
        cos_part = cos_ref[here, :]
        sin_part = sin_ref[here, :]
        turned = []
        for tile in range(2 * lw // HEAD_TILE):
            piece = both[:, tile * HEAD_TILE : (tile + 1) * HEAD_TILE]
            turned.append(piece * cos_part + swap_halves(piece) * sin_part)
        column = lax.broadcasted_iota(jnp.int32, (rows, HEAD_TILE), 1)
        segment = block_segment(info, block, rows, 0)
        first_fill = jnp.where(segment == 1, 0.0, MASK_FILL)
        second_fill = jnp.where(segment == 2, 0.0, MASK_FILL)
        q_mark = jnp.where(
            column == HEAD_DIM, first_fill, jnp.where(column == HEAD_DIM + 1, second_fill, 0.0)
        )
        first_mark = jnp.where(segment == 1, 1.0, 0.0)
        second_mark = jnp.where(segment == 2, 1.0, 0.0)
        k_mark = jnp.where(
            column == HEAD_DIM,
            first_mark,
            jnp.where(
                column == HEAD_DIM + 1, second_mark, jnp.where(column < HEAD_DIM + 5, 1.0, 0.0)
            ),
        )
        v_mark = jnp.where(column < HEAD_DIM + 2, 1.0, 0.0)
        for head in range(heads):
            q_at, k_at = head, heads + head
            q_tile = turned[q_at // 2]
            k_tile = turned[k_at // 2]
            v_tile = last[:, HEAD_TILE * (head // 2) : HEAD_TILE * (head // 2 + 1)]
            if q_at % 2:
                q_tile = pltpu.roll(q_tile, HEAD_DIM, 1)
            if k_at % 2:
                k_tile = pltpu.roll(k_tile, HEAD_DIM, 1)
            if head % 2:
                v_tile = pltpu.roll(v_tile, HEAD_DIM, 1)
            there = slice(head * HEAD_TILE, (head + 1) * HEAD_TILE)
            q_ref[here, there] = low(jnp.where(column < HEAD_DIM, q_tile * 0.125, q_mark))
            k_ref[here, there] = low(jnp.where(column < HEAD_DIM, k_tile, k_mark))
            v_ref[here, there] = low(jnp.where(column < HEAD_DIM, v_tile, v_mark))


def attend_kernel(heads, rows, info, q_ref, k_ref, v_ref, *outs):
    att_refs = outs[:4]
    stat_ref = outs[4]
    for block in range(4):
        here = slice(block * rows, (block + 1) * rows)
        column = lax.broadcasted_iota(jnp.int32, (rows, HEAD_TILE), 1)
        results = []
        for head in range(heads):
            there = slice(head * HEAD_TILE, (head + 1) * HEAD_TILE)
            queries = q_ref[here, there]
            scores = dot_nt(queries, k_ref[:, there])
            row_max = jnp.max(scores, axis=-1, keepdims=True)
            weights = low(jnp.exp(scores - row_max))
            summed = dot_nn(weights, v_ref[:, there])
            row_sum = summed[:, HEAD_DIM : HEAD_DIM + 1]
            results.append(summed / row_sum)
            minus = -(row_max + jnp.log(row_sum))
            first = low(minus)
            second = low(minus - wide(first))
            third = low(minus - wide(first) - wide(second))
            stat_ref[here, there] = jnp.where(
                column == HEAD_DIM + 2,
                first,
                jnp.where(
                    column == HEAD_DIM + 3, second, jnp.where(column == HEAD_DIM + 4, third, queries)
                ),
            )
        for head in range(0, heads, 2):
            if head + 1 < heads:
                both = jnp.where(
                    column < HEAD_DIM, results[head], pltpu.roll(results[head + 1], HEAD_DIM, 1)
                )
                att_refs[block][:, head * HEAD_DIM : (head + 2) * HEAD_DIM] = low(both)
            else:
                att_refs[block][:, head * HEAD_DIM :] = low(results[head][:, :HEAD_DIM])


def natural(info, blocks, dest):
    for block in range(4):
        dest[info[OWNER + block]] = blocks[block][...]


def middle_kernel(info, tok_ref, mod_ref, *refs):
    middle_ref, hidden_ref, att_ref, weight_ref = refs[8:]
    natural(info, refs[:4], weight_ref)
    natural(info, refs[4:8], att_ref)
    span = weight_ref.shape[2]
    for columns in range(4):
        there = slice(columns * span, (columns + 1) * span)
        total = wide(tok_ref[:, there])
        for part in range(4):
            total = total + dot_nn(
                att_ref[part], weight_ref[columns, part * span : (part + 1) * span, :]
            )
        middle_ref[:, there] = total
    normed, _ = norm_rows(middle_ref[...])
    hidden_ref[...] = low(normed * (1.0 + mod_ref[0:1, :]) + mod_ref[1:2, :])


def act_grad_kernel(count, skip, info, mod_ref, *refs):
    dy_refs = refs[:4]
    chunks = refs[4 : 4 + count]
    mlp_ref, act_ref, weight_ref = refs[4 + count :]
    rows = dy_refs[0].shape[0]
    place_rows(info, chunks, skip, weight_ref.shape[0] // count, weight_ref)
    gate = mod_ref[2:3, :]
    for block in range(4):
        here = slice(block * rows, (block + 1) * rows)
        grad_mlp = low(gate * wide(dy_refs[block][...]))
        mlp_ref[here, :] = grad_mlp
        act_ref[here, :] = low(dot_nt(grad_mlp, weight_ref[...]))


def forward_kernel(count, info, act_grad, *refs):
    hid_refs = refs[:4]
    chunks = refs[4 : 4 + count]
    act_ref, pre_ref, near_ref, far_ref, weight_ref = refs[4 + count :]
    rows = hid_refs[0].shape[0]
    place_rows(info, chunks, 0, weight_ref.shape[0] // count, weight_ref)
    for block in (2, 3, 1, 0):
        here = slice(block * rows, (block + 1) * rows)
        pre = dot_nn(hid_refs[block][...], weight_ref[...])
        square = pre * pre
        inner = jnp.tanh(GELU_IN * (pre + GELU_CUBE * (square * pre)))
        half = 0.5 * (1.0 + inner)
        act_ref[here, :] = low(pre * half)
        slope = half + 0.5 * pre * (1.0 - inner * inner) * (
            GELU_IN * (1.0 + 3.0 * GELU_CUBE * square)
        )
        grad_pre = low(wide(act_grad[here, :]) * slope)
        pre_ref[here, :] = grad_pre
        dest = near_ref if block < 2 else far_ref
        dest[(block % 2) * rows : (block % 2 + 1) * rows, :] = low(
            dot_nt(grad_pre, weight_ref[...])
        )


def weight_grad_kernel(count, info, act_ref, mlp_ref, pre_ref, *refs):
    hid_refs = refs[:4]
    outs, sums_ref = refs[4:-1], refs[-1]
    rows = hid_refs[0].shape[0]
    per = act_ref.shape[1] // count
    up = dot_tn(hid_refs[0][...], pre_ref[:rows, :])
    for block in range(1, 4):
        up = up + dot_tn(hid_refs[block][...], pre_ref[block * rows : (block + 1) * rows, :])
    for index in range(count):
        sums_ref[index, :per, :] = low(up[index * per : (index + 1) * per, :])
    down = dot_tn(act_ref[...], mlp_ref[...])
    for index in range(count):
        sums_ref[index, per:, :] = low(down[index * per : (index + 1) * per, :])
    store_blocks(info, sums_ref, outs)


def down_kernel(count, skip, info, act_ref, *refs):
    dy_refs = refs[:4]
    chunks = refs[4 : 4 + count]
    near_ref, far_ref, gate_ref, weight_ref = refs[4 + count :]
    rows = dy_refs[0].shape[0]
    place_rows(info, chunks, skip, weight_ref.shape[0] // count, weight_ref)
    total = jnp.zeros(gate_ref.shape, jnp.float32)
    for block in (2, 3, 1, 0):
        here = slice(block * rows, (block + 1) * rows)
        part = dot_nn(act_ref[here, :], weight_ref[...])
        total = total + jnp.sum(wide(dy_refs[block][...]) * part, axis=0, keepdims=True)
        dest = near_ref if block < 2 else far_ref
        dest[(block % 2) * rows : (block % 2 + 1) * rows, :] = low(part)
    gate_ref[...] = total


def branch_kernel(info, mod_ref, middle_ref, dy_ref, own_ref, core_ref, chip_ref, gate_ref, *refs):
    mid_ref, branch_ref, sums_ref = refs[4:7]
    att_refs = (refs[7], refs[8], None, refs[9])
    weight_ref, parts_ref = refs[10:]
    natural(info, refs[:4], weight_ref)
    rows, width = dy_ref.shape
    grad_hidden = wide(own_ref[:rows, :]) + wide(core_ref[:rows, :]) + wide(chip_ref[...])
    normed, scaling = norm_rows(middle_ref[...])
    sums_ref[0:1, :] = jnp.sum(grad_hidden * normed, axis=0, keepdims=True)
    sums_ref[1:2, :] = jnp.sum(grad_hidden, axis=0, keepdims=True)
    sums_ref[2:3, :] = gate_ref[...]
    grad_normed = grad_hidden * (1.0 + mod_ref[0:1, :])
    first_mean = jnp.mean(grad_normed, axis=-1, keepdims=True)
    second_mean = jnp.mean(grad_normed * normed, axis=-1, keepdims=True)
    mid_ref[...] = wide(dy_ref[...]) + scaling * (grad_normed - first_mean - normed * second_mean)
    span = weight_ref.shape[2]
    branch_ref[:, :width] = low(mid_ref[...])
    branch_ref[:, width + span :] = jnp.zeros(
        (rows, branch_ref.shape[1] - width - span), jnp.bfloat16
    )
    for columns in range(4):
        parts_ref[columns] = low(mid_ref[:, columns * span : (columns + 1) * span])
    for block, dest in enumerate(att_refs):
        at = pl.multiple_of(info[OWNER + block] * span, HEAD_DIM)
        total = dot_nt(parts_ref[0], weight_ref[0, pl.ds(at, span), :])
        for columns in range(1, 4):
            total = total + dot_nt(parts_ref[columns], weight_ref[columns, pl.ds(at, span), :])
        if dest is None:
            branch_ref[:, width : width + span] = low(total)
        else:
            dest[...] = low(total)


def out_grad_kernel(info, att_ref, core_att_ref, branch_ref, core_branch_ref, near_ref, parts_ref):
    span = att_ref.shape[2]
    for columns in range(4):
        here = slice(columns * span, (columns + 1) * span)
        parts_ref[columns] = branch_ref[:, here]
        parts_ref[4 + columns] = core_branch_ref[:, here]
    for block in range(2):
        owner = info[OWNER + block]
        branch, core_branch = parts_ref[owner], parts_ref[4 + owner]
        for part in range(4):
            near_ref[block, part * span : (part + 1) * span, :] = low(
                dot_tn(att_ref[part], branch) + dot_tn(core_att_ref[part], core_branch)
            )


def attend_back_kernel(heads, rows, info, cos_ref, sin_ref, q_ref, k_ref, v_ref, *refs):
    att = refs[:4]
    span = heads * HEAD_DIM
    width = 4 * span
    grads = ((refs[4], 0), (refs[5], 0), (refs[6], width), (refs[7], 0))
    out_ref, gx_ref, turn_ref, dq_ref, dk_ref, dv_ref = refs[8:]
    column = lax.broadcasted_iota(jnp.int32, (rows, HEAD_TILE), 1)

    def tile_of(ref, base, head):
        at = base + HEAD_TILE * (head // 2)
        if base or head % 2 or head + 1 < heads:
            tile = wide(ref[:, at : at + HEAD_TILE])
            return pltpu.roll(tile, HEAD_DIM, 1) if head % 2 else tile
        last = wide(ref[:, at:])
        return jnp.concatenate([last, jnp.zeros_like(last)], axis=1)

    for head in range(heads):
        there = slice(head * HEAD_TILE, (head + 1) * HEAD_TILE)
        for block in range(4):
            here = slice(block * rows, (block + 1) * rows)
            grad = jnp.where(column < HEAD_DIM, tile_of(*grads[block], head), 0.0)
            minus = -jnp.sum(grad * tile_of(att[block], 0, head), axis=-1, keepdims=True)
            first = wide(low(minus))
            gx_ref[here, :] = low(
                jnp.where(
                    column == HEAD_DIM,
                    first,
                    jnp.where(column == HEAD_DIM + 1, minus - first, grad),
                )
            )
        for block in range(4):
            here = slice(block * rows, (block + 1) * rows)
            keys = k_ref[here, there]
            probs = jnp.exp(dot_nt(keys, q_ref[:, there]))
            prob_grad = dot_nt(v_ref[here, there], gx_ref[...])
            score_grad = low(probs * prob_grad)
            dv_ref[here, there] = dot_nn(low(probs), gx_ref[...])
            dk_ref[here, there] = dot_nn(score_grad, q_ref[:, there])
            part = dot_tn(keys, score_grad)
            if block == 0:
                turn_ref[...] = part
            else:
                turn_ref[...] += part
        dq_ref[:, there] = jnp.transpose(turn_ref[...]) * 0.125

    for block in range(4):
        here = slice(block * rows, (block + 1) * rows)
        heads_of = [dq_ref[here, h * HEAD_TILE : (h + 1) * HEAD_TILE] for h in range(heads)]
        heads_of += [dk_ref[here, h * HEAD_TILE : (h + 1) * HEAD_TILE] for h in range(heads)]
        heads_of += [dv_ref[here, h * HEAD_TILE : (h + 1) * HEAD_TILE] for h in range(heads)]
        heads_of.append(jnp.zeros((rows, HEAD_TILE), jnp.float32))
        for tile in range((3 * heads + 1) // 2):
            both = jnp.where(
                column < HEAD_DIM,
                heads_of[2 * tile],
                pltpu.roll(heads_of[2 * tile + 1], HEAD_DIM, 1),
            )
            if tile < heads:
                both = both * cos_ref[here, :] - swap_halves(both) * sin_ref[here, :]
            out_ref[here, tile * HEAD_TILE : (tile + 1) * HEAD_TILE] = low(both)


def hidden_grad_kernel(rows, info, grad_ref, weight_ref, sums_ref, near_ref, far_ref):
    span = grad_ref.shape[1]
    for block in (2, 3, 1, 0):
        dest = near_ref if block < 2 else far_ref
        at = (block % 2) * rows
        here = slice(block * rows, (block + 1) * rows)
        dest[at : at + rows, :] = low(dot_nt(grad_ref[here, :], weight_ref[:, :span]))
    extra = near_ref.shape[0] - 2 * rows
    sums = jnp.concatenate(
        [sums_ref[...], jnp.zeros((extra - 3, sums_ref.shape[1]), jnp.float32)], axis=0
    )
    near_ref[2 * rows :, :] = low(sums)
    far_ref[2 * rows :, :] = low(sums)


def qkv_grad_kernel(count, used, info, hidden_ref, grad_ref, near_ref, chip_ref, *refs):
    outs, sums_ref = refs[:-1], refs[-1]
    total = dot_tn(hidden_ref[...], grad_ref[...])
    out_total = wide(near_ref[0]) + wide(chip_ref[0])
    per = total.shape[0] // count
    for index in range(count):
        here = slice(index * per, (index + 1) * per)
        sums_ref[index, :, :used] = low(total[here, :used])
        sums_ref[index, :, used:] = low(out_total[here, :])
    store_blocks(info, sums_ref, outs)


def input_kernel(info, gain, tok_ref, mid_ref, own_ref, core_ref, chip_ref, out_ref):
    rows = tok_ref.shape[0]
    grad_hidden = wide(own_ref[:rows, :]) + wide(core_ref[:rows, :]) + wide(chip_ref[:rows, :])
    normed, scaling = norm_rows(wide(tok_ref[...]))
    grad_normed = grad_hidden * gain[...]
    first_mean = jnp.mean(grad_normed, axis=-1, keepdims=True)
    second_mean = jnp.mean(grad_normed * normed, axis=-1, keepdims=True)
    out_ref[...] = low(
        mid_ref[...] + scaling * (grad_normed - first_mean - normed * second_mean)
    )


def finish_mlp_kernel(count, info, *refs):
    blocks = refs[:4]
    up_ref, down_ref, all_ref = refs[4:]
    natural(info, blocks, all_ref)
    rows = up_ref.shape[0]
    piece = down_ref.shape[0] // 4
    for part in range(4):
        value = wide(all_ref[part])
        for index in range(count):
            at = (index * 4 + part) * piece
            up_ref[:, at : at + piece] = value[:rows, index * piece : (index + 1) * piece]
        down_ref[part * piece : (part + 1) * piece, :] = value[rows:, :]


def finish_qkv_kernel(info, *refs):
    blocks = refs[:4]
    weight_ref, gain_ref, out_ref, own_ref, sums_ref, all_ref = refs[4:]
    natural(info, blocks, all_ref)
    span = all_ref.shape[2] // 4
    total = jnp.zeros((out_ref.shape[0], 1), jnp.float32)
    for part in range(4):
        value = wide(all_ref[part])
        for third in range(3):
            at = (third * 4 + part) * span
            piece = value[:, third * span : (third + 1) * span]
            total = total + jnp.sum(
                wide(weight_ref[:, at : at + span]) * piece, axis=1, keepdims=True
            )
            out_ref[:, at : at + span] = piece
        own_ref[:, part * span : (part + 1) * span] = value[:, 3 * span :]
    turned = jnp.transpose(jnp.broadcast_to(total, (total.shape[0], HEAD_TILE)))
    sums_ref[...] = turned[0:1, :] / gain_ref[...]


def hop(values_in, mask):
    return lax.ppermute(values_in, "seq", [(i, i ^ mask) for i in range(lax.axis_size("seq"))])


def ring_of(count):
    return [0] + list(range(1, count, 2)) + [i for i in range(count - 1, 0, -1) if i % 2 == 0]


def ring_next(data_count):
    outer = data_count // 2
    ring = ring_of(outer)
    follow = {ring[i]: ring[(i + 1) % outer] for i in range(outer)}
    return [(z * 2 + y, follow[z] * 2 + y) for z in range(outer) for y in range(2)]


def pair(values_in):
    return lax.ppermute(values_in, "dp", [(i, i ^ 1) for i in range(lax.axis_size("dp"))])


def dp_sum_direct(blocks):
    data_count = lax.axis_size("dp")
    if data_count != 8:
        return wide(lax.psum_scatter(blocks, "dp", scatter_dimension=0, tiled=False))
    return jnp.sum(wide(lax.all_to_all(blocks, "dp", 0, 0, tiled=True)), axis=0)


def after(values_in, *earlier):
    return lax.optimization_barrier((values_in,) + earlier)[0]


def onward(values_in):
    return lax.ppermute(values_in, "dp", ring_next(lax.axis_size("dp")))


def kernel_info(layout, rank, index, tok_rows):
    data_count = lax.axis_size("dp")
    column = jnp.arange(PLACE + 8, dtype=jnp.int32)

    def owner(block):
        return rank ^ ((block & 1) * 2 + (block >> 1))

    values = jnp.where(column == 0, layout[0, 0], layout[0, 1])
    values = jnp.where(column >= FIRST, owner(column - FIRST) * tok_rows, values)
    values = jnp.where(column >= OWNER, owner(column - OWNER), values)
    if data_count == 8:
        step = column - PLACE
        at = index >> 1
        at = ((at ^ (at >> 1)) - (step >> 1)) & 3
        place = (at ^ (at >> 1)) * 2 + ((index + step) & 1)
    else:
        place = jnp.zeros_like(column)
    return jnp.where(column >= PLACE, place, values)


def gathered_whole(chunk, sizes):
    gathered = lax.all_gather(chunk, "dp", axis=0)
    parts = []
    at = 0
    for size in sizes:
        parts.append(gathered[:, at : at + size].reshape(-1, chunk.shape[1]))
        at += size
    return [jnp.concatenate(parts, axis=0)]


def four(values_in):
    chip = hop(values_in, 2)
    return [values_in, chip, hop(values_in, 1), hop(chip, 1)]


def beyond(values_in, mask):
    return lax.ppermute(values_in, "dp", [(i, i ^ mask) for i in range(lax.axis_size("dp"))])


def double_to_all(row, high):
    parts = row[None]
    for place, bit in enumerate(high):
        other = beyond(parts, 1 << place)
        parts = jnp.where(
            bit,
            jnp.concatenate([other, parts], axis=0),
            jnp.concatenate([parts, other], axis=0),
        )
    return parts


def body(tokens, ln1_gain, w_qkv, w_out, w_ada, w_up, w_down, out_grad, layout, timestep):
    seq_count = lax.axis_size("seq")
    data_count = lax.axis_size("dp")
    ringed = data_count == 8
    rank = lax.axis_index("seq")
    index = lax.axis_index("dp")
    high = [(index >> place) & 1 == 1 for place in range(data_count.bit_length() - 1)]
    tokens, rank, index, high = lax.optimization_barrier((tokens, rank, index, high))
    tok_rows, width = tokens.shape
    group_rows = tok_rows * seq_count
    heads_local = HEADS // seq_count
    local_width = heads_local * HEAD_DIM
    head_columns = heads_local * HEAD_TILE
    padded = (3 * heads_local + 1) // 2 * HEAD_TILE
    rows = w_qkv.shape[0]
    hidden = w_up.shape[1] // seq_count
    down_piece = w_down.shape[0] // seq_count
    rank_word = rank.reshape(1).astype(jnp.int32)

    tok_chip = hop(tokens, 2)
    first = run(
        first_part_kernel,
        [shaped((rows, 4 * local_width))],
        [rank_word, w_qkv, w_out],
        0,
        name="first_part",
    )[0]
    if ringed:
        held = [first, onward(first)]
        beside = [pair(first)]
        held[1], beside[0], tokens = lax.optimization_barrier((held[1], beside[0], tokens))
        held.append(onward(held[1]))
        beside.append(pair(held[1]))
        tok_core = hop(tokens, 1)
        held[2], beside[1], tok_chip, tok_core = lax.optimization_barrier(
            (held[2], beside[1], tok_chip, tok_core)
        )
        held.append(onward(held[2]))
        beside.append(pair(held[2]))
        tok_both = hop(tok_chip, 1)
    else:
        tok_core, tok_both = hop(tokens, 1), hop(tok_chip, 1)
    tok_blocks = [tokens, tok_chip, tok_core, tok_both]

    embed = low(time_table(wide(timestep), width))
    sent = jnp.stack(
        [embed.reshape(data_count, rows), jnp.broadcast_to(ln1_gain, (data_count, rows))], axis=1
    )
    taken = lax.all_to_all(sent, "dp", 0, 0, tiled=True)
    embeds = taken[:, 0]
    gain = wide(taken[:, 1].reshape(1, width))
    mod_parts = run(
        modulation_kernel,
        [shaped((data_count, 3, width), jnp.float32)],
        [rank_word, after(embeds, held[1]) if ringed else embeds, w_ada],
        2 * data_count * rows * w_ada.shape[1],
        name="modulation",
    )[0]

    def halved(parts, place):
        half = parts.shape[0] // 2
        kept = jnp.where(high[place], parts[half:], parts[:half])
        given = jnp.where(high[place], parts[:half], parts[half:])
        return kept + beyond(given, 1 << place)

    modulation = mod_parts
    for place in range(len(high) - 1, 1, -1):
        modulation = halved(modulation, place)

    info = kernel_info(layout, rank, index, tok_rows)
    starts = info[FIRST:OWNER]
    if ringed:
        starts = after(starts, held[2])
    positions = (starts[:, None] + jnp.arange(tok_rows, dtype=jnp.int32)[None, :]).reshape(-1)
    cos_table, sin_table = rope_tables(positions)

    second = run(
        functools.partial(second_part_kernel, data_count),
        [shaped((rows + down_piece, width))],
        [rank_word, w_up, w_down],
        0,
        name="second_part",
    )[0]
    if ringed:
        dy_core = hop(after(out_grad, held[2]), 1)
        held[3], beside[2], second, dy_core, *rest = lax.optimization_barrier(
            (
                held[3],
                beside[2],
                second,
                dy_core,
                modulation,
                gain,
                info,
                cos_table,
                sin_table,
                tok_blocks,
            )
        )
        modulation, gain, info, cos_table, sin_table, tok_blocks = rest
        beside.append(pair(held[3]))
        first_chunks = [part for both in zip(held, beside) for part in both]
        held = [second, onward(second)]
        beside = [pair(after(second, beside[3]))]
        dy_chip = hop(after(out_grad, held[0]), 2)
    else:
        first_chunks = gathered_whole(first, [rows])
        second_chunks = gathered_whole(second, [rows, down_piece])
        dy_chip, dy_core = hop(out_grad, 2), hop(out_grad, 1)
    modulation = halved(modulation, 1)
    if ringed:
        gain, modulation = lax.optimization_barrier((gain, modulation))
    modulation = halved(modulation, 0)
    count = len(first_chunks)
    up_rows = rows * (data_count // count)

    hidden_one, qkv_weight, own_out, queries, keys, values = run(
        functools.partial(qkv_kernel, heads_local, count),
        [
            shaped((group_rows, width)),
            shaped((width, 4 * local_width)),
            shaped((width, local_width)),
            shaped((group_rows, head_columns)),
            shaped((group_rows, head_columns)),
            shaped((group_rows, head_columns)),
        ],
        [info, gain, cos_table, sin_table] + tok_blocks + first_chunks,
        2 * group_rows * width * padded,
        name="qkv",
    )
    if ringed:
        queries, own_out, held[1], beside[0], modulation = lax.optimization_barrier(
            (queries, own_out, held[1], beside[0], modulation)
        )
        beside.append(pair(held[1]))
        held.append(onward(held[1]))
    chip_out = hop(own_out, 2)
    core_out = hop(own_out, 1)
    *att_parts, marked = run(
        functools.partial(attend_kernel, heads_local, tok_rows),
        [shaped((tok_rows, local_width))] * 4 + [shaped((group_rows, head_columns))],
        [info, queries, keys, values],
        4 * group_rows * group_rows * head_columns,
        name="attend",
    )
    if ringed:
        att_parts, held[2], beside[1], chip_out, core_out, dy_chip, modulation = (
            lax.optimization_barrier(
                (att_parts, held[2], beside[1], chip_out, core_out, dy_chip, modulation)
            )
        )
        beside.append(pair(held[2]))
        held.append(onward(held[2]))
    modulation = modulation[0]
    att_own = [att_parts[0]] + [hop(att_parts[j], MASKS[j]) for j in (1, 2, 3)]
    out_blocks = [own_out, chip_out, core_out, hop(after(chip_out, att_own[2]), 1)]
    if ringed:
        att_own = lax.optimization_barrier(att_own)
    middle, hidden_two, att_ordered = run(
        middle_kernel,
        [
            shaped((tok_rows, width), jnp.float32),
            shaped((tok_rows, width)),
            shaped((seq_count, tok_rows, local_width)),
        ],
        [info, tokens, modulation] + out_blocks + att_own,
        2 * tok_rows * width * width,
        scratch=[pltpu.VMEM((seq_count, width, local_width), jnp.bfloat16)],
        name="middle",
    )

    chip_hidden = hop(hidden_two, 2)
    if ringed:
        beside.append(pair(held[3]))
        second_chunks = [part for both in zip(held, beside) for part in both]
    dy_blocks = [out_grad, dy_chip, dy_core, hop(dy_chip, 1)]
    grad_mlp, grad_act = run(
        functools.partial(act_grad_kernel, count, up_rows),
        [shaped((group_rows, width)), shaped((group_rows, hidden))],
        [info, modulation] + dy_blocks + second_chunks,
        2 * group_rows * width * hidden,
        scratch=[pltpu.VMEM((hidden, width), jnp.bfloat16)],
        name="act_grad",
    )
    hid_blocks = [
        hidden_two,
        chip_hidden,
        hop(hidden_two, 1),
        hop(after(chip_hidden, grad_act), 1),
    ]
    half = shaped((group_rows // 2, width))
    activated, grad_pre, gh_near, gh_far = run(
        functools.partial(forward_kernel, count),
        [shaped((group_rows, hidden)), shaped((group_rows, hidden)), half, half],
        [info, grad_act] + hid_blocks + second_chunks,
        4 * group_rows * width * hidden,
        scratch=[pltpu.VMEM((width, hidden), jnp.bfloat16)],
        name="forward",
    )
    block_shape = (rows + down_piece, width)
    grad_weights = run(
        functools.partial(weight_grad_kernel, data_count),
        [shaped(block_shape)] * count if ringed else [shaped((data_count,) + block_shape)],
        [info, activated, grad_mlp, grad_pre] + hid_blocks,
        4 * group_rows * width * hidden,
        scratch=[pltpu.VMEM((data_count,) + block_shape, jnp.bfloat16)],
        name="weight_grad",
    )
    gh_core = hop(gh_far, 1)
    gh_core, grad_weights = lax.optimization_barrier((gh_core, grad_weights))
    gh_send = low(wide(gh_near[tok_rows:]) + wide(gh_core[tok_rows:]))
    gh_chip = hop(gh_send, 2)
    mlp_near, mlp_far, grad_gate = run(
        functools.partial(down_kernel, count, up_rows),
        [half, half, shaped((1, width), jnp.float32)],
        [info, after(activated, gh_send)] + dy_blocks + second_chunks,
        2 * group_rows * width * hidden,
        scratch=[pltpu.VMEM((hidden, width), jnp.bfloat16)],
        name="down",
    )
    if ringed:
        mlp_keep, mlp_give = list(grad_weights[0::2]), list(grad_weights[1::2])
        mlp_taken = pair(after(mlp_give[1], gh_send))
        gh_chip, mlp_far, mlp_taken = lax.optimization_barrier((gh_chip, mlp_far, mlp_taken))
        mlp_ring = low(wide(mlp_keep[1]) + wide(mlp_taken))
        gh_chip, mlp_ring = lax.optimization_barrier((gh_chip, mlp_ring))
        mlp_carried = onward(mlp_ring)
        mlp_taken = pair(after(mlp_give[2], mlp_ring))
    else:
        gh_chip, mlp_far = lax.optimization_barrier((gh_chip, mlp_far))
    mlp_core = hop(mlp_far, 1)
    core_attended = hop(after(att_ordered, gh_chip), 1)

    branch_columns = -(-(width + local_width) // HEAD_TILE) * HEAD_TILE
    grad_middle, branch, grad_mod, *grad_parts = run(
        branch_kernel,
        [
            shaped((tok_rows, width), jnp.float32),
            shaped((tok_rows, branch_columns)),
            shaped((3, width), jnp.float32),
        ]
        + [shaped((tok_rows, local_width))] * 3,
        [info, modulation, after(middle, mlp_near), out_grad, gh_near, gh_core, gh_chip]
        + [grad_gate]
        + out_blocks,
        2 * tok_rows * width * width,
        scratch=[
            pltpu.VMEM((seq_count, width, local_width), jnp.bfloat16),
            pltpu.VMEM((seq_count, tok_rows, local_width), jnp.bfloat16),
        ],
        name="branch",
    )
    grad_parts, mlp_core = lax.optimization_barrier((grad_parts, mlp_core))
    core_branch = hop(branch, 1)
    grad_att = [grad_parts[0], hop(grad_parts[1], 2), core_branch, hop(grad_parts[2], 3)]
    out_sums = run(
        out_grad_kernel,
        [shaped((2, width, local_width))],
        [info, att_ordered, core_attended, branch, core_branch],
        2 * tok_rows * width * width,
        scratch=[pltpu.VMEM((2 * seq_count, tok_rows, local_width), jnp.bfloat16)],
        name="out_grad",
    )[0]

    if ringed:
        del grad_att[2]
        grad_att, out_sums, mlp_taken, mlp_carried = lax.optimization_barrier(
            (grad_att, out_sums, mlp_taken, mlp_carried)
        )
        grad_att.insert(2, core_branch)
        mlp_ring = low(wide(mlp_keep[2]) + wide(mlp_taken) + wide(mlp_carried))
        mlp_carried = onward(mlp_ring)
        mlp_taken = pair(after(mlp_give[3], mlp_ring))
    out_chip = hop(out_sums[1:], 2)
    grad_qkv = run(
        functools.partial(attend_back_kernel, heads_local, tok_rows),
        [shaped((group_rows, padded))],
        [info, cos_table, sin_table, marked, keys, values] + att_parts + grad_att,
        10 * group_rows * group_rows * head_columns,
        scratch=[
            pltpu.VMEM((group_rows, HEAD_TILE), jnp.bfloat16),
            pltpu.VMEM((HEAD_TILE, group_rows), jnp.float32),
            pltpu.VMEM((group_rows, head_columns), jnp.float32),
            pltpu.VMEM((group_rows, head_columns), jnp.float32),
            pltpu.VMEM((group_rows, head_columns), jnp.float32),
        ],
        name="attend_back",
    )[0]
    grad_qkv, out_chip = lax.optimization_barrier((grad_qkv, out_chip))
    if ringed:
        grad_qkv, mlp_taken, mlp_carried = lax.optimization_barrier(
            (grad_qkv, mlp_taken, mlp_carried)
        )
    qkv_sums = run(
        functools.partial(qkv_grad_kernel, data_count, 3 * local_width),
        [shaped((rows, 4 * local_width))] * count
        if ringed
        else [shaped((data_count, rows, 4 * local_width))],
        [info, hidden_one, grad_qkv, out_sums, out_chip],
        2 * group_rows * width * padded,
        scratch=[pltpu.VMEM((data_count, rows, 4 * local_width), jnp.bfloat16)],
        name="qkv_grad",
    )
    half_extra = shaped((group_rows // 2 + 16, width))
    gq_near, gq_far = run(
        functools.partial(hidden_grad_kernel, tok_rows),
        [half_extra, half_extra],
        [info, after(grad_qkv, qkv_sums[0]), qkv_weight, grad_mod],
        2 * group_rows * width * padded,
        name="hidden_grad",
    )
    if ringed:
        qkv_keep, qkv_give = list(qkv_sums[0::2]), list(qkv_sums[1::2])
        qkv_taken = pair(qkv_give[1])
        gq_far, qkv_taken = lax.optimization_barrier((gq_far, qkv_taken))
        qkv_ring = low(wide(qkv_keep[1]) + wide(qkv_taken))
        qkv_carried = onward(qkv_ring)
        qkv_taken = pair(after(qkv_give[2], qkv_ring))
    gq_core = hop(gq_far, 1)
    gq_send = low(wide(gq_near[tok_rows:]) + wide(gq_core[tok_rows:]))
    if ringed:
        qkv_carried, qkv_taken, gq_send = lax.optimization_barrier(
            (qkv_carried, qkv_taken, gq_send)
        )
        qkv_ring = low(wide(qkv_keep[2]) + wide(qkv_taken) + wide(qkv_carried))
        qkv_carried = onward(qkv_ring)
        qkv_taken = pair(after(qkv_give[3], qkv_ring))
        mlp_ring = low(wide(after(mlp_keep[3], gq_send)) + wide(mlp_taken) + wide(mlp_carried))
        mlp_carried = onward(mlp_ring)
        mlp_taken = pair(after(mlp_give[0], mlp_ring))
    gq_chip = hop(gq_send, 2)
    if ringed:
        qkv_ring = low(wide(qkv_keep[3]) + wide(qkv_taken) + wide(qkv_carried))
        qkv_carried = onward(qkv_ring)
        qkv_taken = pair(after(qkv_give[0], qkv_ring))
        sum_mlp = low(wide(mlp_keep[0]) + wide(mlp_taken) + wide(mlp_carried))
    else:
        sum_mlp = low(dp_sum_direct(grad_weights[0]))
    sum_mlp, gq_chip = lax.optimization_barrier((sum_mlp, gq_chip))
    mlp_blocks = four(sum_mlp)
    grad_inputs = run(
        input_kernel,
        [shaped((tok_rows, width))],
        [info, gain, tokens, grad_middle, gq_near, gq_core, gq_chip],
        20 * tok_rows * width,
        name="input",
    )[0]
    grad_mod = (wide(gq_send[tok_rows:]) + wide(gq_chip[tok_rows:]))[:3]
    grad_mods = double_to_all(grad_mod, high).reshape(data_count, 3 * width)
    if ringed:
        qkv_carried, qkv_taken, grad_inputs = lax.optimization_barrier(
            (qkv_carried, qkv_taken, grad_inputs)
        )
        sum_qkv = low(wide(qkv_keep[0]) + wide(qkv_taken) + wide(qkv_carried))
    else:
        sum_qkv = low(dp_sum_direct(qkv_sums[0]))
    mlp_send = low(wide(after(mlp_near[tok_rows:], gq_chip)) + wide(mlp_core[tok_rows:]))
    mlp_chip = hop(mlp_send, 2)
    mlp_out = wide(mlp_near[:tok_rows]) + wide(mlp_core[:tok_rows]) + wide(mlp_chip)
    result = low(middle + modulation[2:3] * mlp_out)
    final_ada = lax.dot_general(
        wide(embeds), grad_mods, (((0,), (0,)), ((), ())), precision=lax.Precision.HIGHEST
    )

    final_up, final_down = run(
        functools.partial(finish_mlp_kernel, data_count),
        [shaped(w_up.shape, jnp.float32), shaped(w_down.shape, jnp.float32)],
        [info] + mlp_blocks,
        0,
        scratch=[pltpu.VMEM((seq_count,) + block_shape, jnp.bfloat16)],
        name="finish_mlp",
    )
    final_qkv, final_out, final_gain = run(
        finish_qkv_kernel,
        [
            shaped(w_qkv.shape, jnp.float32),
            shaped(w_out.shape, jnp.float32),
            shaped((1, rows), jnp.float32),
        ],
        [info] + four(sum_qkv) + [w_qkv, wide(ln1_gain).reshape(1, rows)],
        0,
        scratch=[pltpu.VMEM((seq_count, rows, 4 * local_width), jnp.bfloat16)],
        name="finish_qkv",
    )
    return (
        result,
        grad_inputs,
        final_gain.reshape(-1),
        final_qkv,
        final_out,
        final_ada,
        final_up,
        final_down,
    )


def solution(mesh):
    placed = (
        P(("dp", "seq"), None),
        P("dp"),
        P("dp", None),
        P("dp", None),
        P("dp", None),
        P("dp", None),
        P("dp", None),
        P(("dp", "seq"), None),
        P("dp", None),
        P("dp"),
    )
    return jax.shard_map(
        body,
        mesh=mesh,
        in_specs=placed,
        out_specs=(
            P(("dp", "seq"), None),
            P(("dp", "seq"), None),
            P("dp"),
            P("dp", None),
            P("dp", None),
            P("dp", None),
            P("dp", None),
            P("dp", None),
        ),
        check_vma=False,
    )
```

```python
import functools
import math

import jax
import jax.numpy as jnp
from jax import lax
from jax.experimental import pallas as pl
from jax.experimental.pallas import tpu as pltpu
from jax.sharding import PartitionSpec as P

HEADS = 12
HEAD_DIM = 64

eps = 1e-05

MASKS = (0, 2, 1, 3)


def time_table(time_steps, model_width):
    half_dim = model_width // 2
    frequency = jnp.exp(-math.log(10000.0) * jnp.arange(half_dim, dtype=jnp.float32) / half_dim)
    angles = time_steps[:, None] * frequency[None, :]
    return jnp.concatenate([jnp.cos(angles), jnp.sin(angles)], axis=1)


def low(values_in):
    return values_in.astype(jnp.bfloat16)


def wide(values_in):
    return values_in.astype(jnp.float32)


HEAD_TILE = 128
COST = 1.0
VMEM_GRANT = 16 * 1024 * 1024
MASK_FILL = -1e30
GELU_IN = math.sqrt(2.0 / math.pi)
GELU_CUBE = 0.044715


def rope_tables(positions):
    half_dim = HEAD_DIM // 2
    column = jnp.arange(2 * HEAD_DIM, dtype=jnp.int32)
    frequency = jnp.exp(
        -math.log(10000.0) * 2.0 * (column % half_dim).astype(jnp.float32) / HEAD_DIM
    )
    angles = positions.astype(jnp.float32)[:, None] * frequency[None, :]
    sign = jnp.where(column % HEAD_DIM < half_dim, -1.0, 1.0)
    return (jnp.cos(angles), jnp.sin(angles) * sign[None, :])


def dot_nn(left, right):
    return lax.dot_general(
        left, right, (((1,), (0,)), ((), ())), preferred_element_type=jnp.float32
    )


def dot_nt(left, right):
    return lax.dot_general(
        left, right, (((1,), (1,)), ((), ())), preferred_element_type=jnp.float32
    )


def dot_tn(left, right):
    return lax.dot_general(
        left, right, (((0,), (0,)), ((), ())), preferred_element_type=jnp.float32
    )


def norm_rows(values_in):
    average = jnp.mean(values_in, axis=-1, keepdims=True)
    centred = values_in - average
    variance = jnp.mean(centred * centred, axis=-1, keepdims=True)
    scaling = lax.rsqrt(variance + eps)
    return (centred * scaling, scaling)


def swap_halves(values_in):
    column = lax.broadcasted_iota(jnp.int32, values_in.shape, 1)
    ahead = pltpu.roll(values_in, HEAD_TILE - HEAD_DIM // 2, 1)
    behind = pltpu.roll(values_in, HEAD_DIM // 2, 1)
    return jnp.where(column % HEAD_DIM < HEAD_DIM // 2, ahead, behind)


def whole(count):
    return [pl.BlockSpec(memory_space=pltpu.VMEM)] * count


def scalars():
    return [pl.BlockSpec(memory_space=pltpu.SMEM)]


def run(kernel, out_shapes, args, flops, scratch=(), name=None):
    nbytes = sum(a.size * a.dtype.itemsize for a in args)
    nbytes += sum(math.prod(o.shape) * o.dtype.itemsize for o in out_shapes)
    call = pl.pallas_call(
        kernel,
        out_shape=out_shapes,
        in_specs=scalars() + whole(len(args) - 1),
        out_specs=whole(len(out_shapes)),
        scratch_shapes=list(scratch),
        cost_estimate=pl.CostEstimate(flops=int(flops * COST), bytes_accessed=int(nbytes * COST), transcendentals=0),
        compiler_params=pltpu.CompilerParams(vmem_limit_bytes=VMEM_GRANT),
        name=name,
    )
    return call(*args)


def shaped(shape, kind=jnp.bfloat16):
    return jax.ShapeDtypeStruct(shape, kind)


FIRST, OWNER, PLACE = 2, 6, 10


def block_segment(info, block, rows, axis):
    shape = (rows, 1) if axis == 0 else (1, rows)
    position = info[FIRST + block] + lax.broadcasted_iota(jnp.int32, shape, axis)
    return (position >= info[0]).astype(jnp.int32) + (position >= info[1]).astype(jnp.int32)


def place_rows(info, chunks, first, rows, dest):
    for index, chunk in enumerate(chunks):
        at = pl.multiple_of(info[PLACE + index] * rows, rows)
        dest[pl.ds(at, rows), : chunk.shape[1]] = chunk[first : first + rows, :]


def store_blocks(info, sums_ref, outs):
    if len(outs) == 1:
        outs[0][...] = sums_ref[...]
    else:
        for index, dest in enumerate(outs):
            dest[...] = sums_ref[info[PLACE + index]]


def first_part_kernel(info, qkv_ref, out_ref, dest):
    span = dest.shape[1] // 4
    for part in range(4):

        @pl.when(info[0] == part)
        def _():
            for third in range(3):
                at = (third * 4 + part) * span
                dest[:, third * span : (third + 1) * span] = qkv_ref[:, at : at + span]
            dest[:, 3 * span :] = out_ref[:, part * span : (part + 1) * span]


def modulation_kernel(info, embed_ref, weight_ref, out_ref):
    width = out_ref.shape[2]
    for third in range(3):
        part = dot_nn(embed_ref[...], weight_ref[:, third * width : (third + 1) * width])
        for group in range(out_ref.shape[0]):
            out_ref[group, third : third + 1, :] = part[group : group + 1, :]


def second_part_kernel(count, info, up_ref, down_ref, dest):
    rows = up_ref.shape[0]
    piece = down_ref.shape[0] // 4
    for part in range(4):

        @pl.when(info[0] == part)
        def _():
            for index in range(count):
                at = (index * 4 + part) * piece
                dest[:rows, index * piece : (index + 1) * piece] = up_ref[:, at : at + piece]
            dest[rows:, :] = down_ref[part * piece : (part + 1) * piece, :]


def qkv_kernel(heads, count, info, *refs):
    gain, cos_ref, sin_ref = refs[:3]
    tok_refs = refs[3:7]
    chunks = refs[7 : 7 + count]
    hidden_ref, weight_ref, own_ref, q_ref, k_ref, v_ref, all_ref = refs[7 + count :]
    rows, width = tok_refs[0].shape
    lw = heads * HEAD_DIM
    place_rows(info, chunks, 0, width // count, weight_ref)
    own_ref[...] = weight_ref[:, 3 * lw : 4 * lw]
    gain_row = gain[...]
    for block in range(4):
        all_ref[block] = tok_refs[block][...]

    @pl.loop(0, 4)
    def _(block):
        normed, _ = norm_rows(wide(all_ref[block]))
        hidden = low(normed * gain_row)
        here = pl.ds(pl.multiple_of(block * rows, rows), rows)
        hidden_ref[here, :] = hidden
        both = dot_nn(hidden, weight_ref[:, : 2 * lw])
        last = dot_nn(hidden, weight_ref[:, 2 * lw : 2 * lw + 2 * HEAD_TILE])
        cos_part = cos_ref[here, :]
        sin_part = sin_ref[here, :]
        turned = []
        for tile in range(2 * lw // HEAD_TILE):
            piece = both[:, tile * HEAD_TILE : (tile + 1) * HEAD_TILE]
            turned.append(piece * cos_part + swap_halves(piece) * sin_part)
        column = lax.broadcasted_iota(jnp.int32, (rows, HEAD_TILE), 1)
        segment = block_segment(info, block, rows, 0)
        first_fill = jnp.where(segment == 1, 0.0, MASK_FILL)
        second_fill = jnp.where(segment == 2, 0.0, MASK_FILL)
        q_mark = jnp.where(
            column == HEAD_DIM, first_fill, jnp.where(column == HEAD_DIM + 1, second_fill, 0.0)
        )
        first_mark = jnp.where(segment == 1, 1.0, 0.0)
        second_mark = jnp.where(segment == 2, 1.0, 0.0)
        k_mark = jnp.where(
            column == HEAD_DIM,
            first_mark,
            jnp.where(
                column == HEAD_DIM + 1, second_mark, jnp.where(column < HEAD_DIM + 5, 1.0, 0.0)
            ),
        )
        v_mark = jnp.where(column < HEAD_DIM + 2, 1.0, 0.0)
        for head in range(heads):
            q_at, k_at = head, heads + head
            q_tile = turned[q_at // 2]
            k_tile = turned[k_at // 2]
            v_tile = last[:, HEAD_TILE * (head // 2) : HEAD_TILE * (head // 2 + 1)]
            if q_at % 2:
                q_tile = pltpu.roll(q_tile, HEAD_DIM, 1)
            if k_at % 2:
                k_tile = pltpu.roll(k_tile, HEAD_DIM, 1)
            if head % 2:
                v_tile = pltpu.roll(v_tile, HEAD_DIM, 1)
            there = slice(head * HEAD_TILE, (head + 1) * HEAD_TILE)
            q_ref[here, there] = low(jnp.where(column < HEAD_DIM, q_tile * 0.125, q_mark))
            k_ref[here, there] = low(jnp.where(column < HEAD_DIM, k_tile, k_mark))
            v_ref[here, there] = low(jnp.where(column < HEAD_DIM, v_tile, v_mark))


def attend_kernel(heads, rows, info, q_ref, k_ref, v_ref, *outs):
    att_refs = outs[:4]
    stat_ref, all_ref = outs[4:]
    column = lax.broadcasted_iota(jnp.int32, (rows, HEAD_TILE), 1)

    @pl.loop(0, 4)
    def _(block):
        here = pl.ds(pl.multiple_of(block * rows, rows), rows)
        results = []
        for head in range(heads):
            there = slice(head * HEAD_TILE, (head + 1) * HEAD_TILE)
            queries = q_ref[here, there]
            scores = dot_nt(queries, k_ref[:, there])
            row_max = jnp.max(scores, axis=-1, keepdims=True)
            weights = low(jnp.exp(scores - row_max))
            summed = dot_nn(weights, v_ref[:, there])
            row_sum = summed[:, HEAD_DIM : HEAD_DIM + 1]
            results.append(summed / row_sum)
            minus = -(row_max + jnp.log(row_sum))
            first = low(minus)
            second = low(minus - wide(first))
            third = low(minus - wide(first) - wide(second))
            stat_ref[here, there] = jnp.where(
                column == HEAD_DIM + 2,
                first,
                jnp.where(
                    column == HEAD_DIM + 3, second, jnp.where(column == HEAD_DIM + 4, third, queries)
                ),
            )
        for head in range(0, heads, 2):
            if head + 1 < heads:
                both = jnp.where(
                    column < HEAD_DIM, results[head], pltpu.roll(results[head + 1], HEAD_DIM, 1)
                )
                all_ref[here, head * HEAD_DIM : (head + 2) * HEAD_DIM] = low(both)
            else:
                all_ref[here, head * HEAD_DIM :] = low(results[head][:, :HEAD_DIM])

    for block in range(4):
        att_refs[block][...] = all_ref[block * rows : (block + 1) * rows, :]


def natural(info, blocks, dest):
    for block in range(4):
        dest[info[OWNER + block]] = blocks[block][...]


def middle_kernel(info, tok_ref, mod_ref, *refs):
    middle_ref, hidden_ref, att_ref, weight_ref = refs[8:]
    natural(info, refs[:4], weight_ref)
    natural(info, refs[4:8], att_ref)
    span = weight_ref.shape[2]
    for columns in range(4):
        there = slice(columns * span, (columns + 1) * span)
        total = wide(tok_ref[:, there])
        for part in range(4):
            total = total + dot_nn(
                att_ref[part], weight_ref[columns, part * span : (part + 1) * span, :]
            )
        middle_ref[:, there] = total
    normed, _ = norm_rows(middle_ref[...])
    hidden_ref[...] = low(normed * (1.0 + mod_ref[0:1, :]) + mod_ref[1:2, :])


def act_grad_kernel(count, skip, info, mod_ref, *refs):
    dy_refs = refs[:4]
    chunks = refs[4 : 4 + count]
    mlp_ref, act_ref, weight_ref = refs[4 + count :]
    rows = dy_refs[0].shape[0]
    place_rows(info, chunks, skip, weight_ref.shape[0] // count, weight_ref)
    gate = mod_ref[2:3, :]
    for block in range(4):
        here = slice(block * rows, (block + 1) * rows)
        mlp_ref[here, :] = low(gate * wide(dy_refs[block][...]))

    @pl.loop(0, 2)
    def _(turn):
        here = pl.ds(pl.multiple_of(turn * 2 * rows, 2 * rows), 2 * rows)
        act_ref[here, :] = low(dot_nt(mlp_ref[here, :], weight_ref[...]))


def forward_kernel(count, info, act_grad, *refs):
    hid_refs = refs[:4]
    chunks = refs[4 : 4 + count]
    act_ref, pre_ref, near_ref, far_ref, weight_ref, all_ref = refs[4 + count :]
    rows = hid_refs[0].shape[0]
    place_rows(info, chunks, 0, weight_ref.shape[0] // count, weight_ref)
    for block in range(4):
        all_ref[block] = hid_refs[block][...]

    @pl.loop(0, 2)
    def _(turn):
        there = pl.ds(pl.multiple_of(turn * rows, rows), rows)
        for half, dest in ((1, far_ref), (0, near_ref)):
            here = pl.ds(pl.multiple_of((2 * half + turn) * rows, rows), rows)
            pre = dot_nn(all_ref[2 * half + turn], weight_ref[...])
            square = pre * pre
            inner = jnp.tanh(GELU_IN * (pre + GELU_CUBE * (square * pre)))
            side = 0.5 * (1.0 + inner)
            act_ref[here, :] = low(pre * side)
            slope = side + 0.5 * pre * (1.0 - inner * inner) * (
                GELU_IN * (1.0 + 3.0 * GELU_CUBE * square)
            )
            grad_pre = low(wide(act_grad[here, :]) * slope)
            pre_ref[here, :] = grad_pre
            dest[there, :] = low(dot_nt(grad_pre, weight_ref[...]))


def weight_grad_kernel(count, info, act_ref, mlp_ref, pre_ref, *refs):
    hid_refs = refs[:4]
    outs, sums_ref = refs[4:-1], refs[-1]
    rows = hid_refs[0].shape[0]
    per = act_ref.shape[1] // count
    up = dot_tn(hid_refs[0][...], pre_ref[:rows, :])
    for block in range(1, 4):
        up = up + dot_tn(hid_refs[block][...], pre_ref[block * rows : (block + 1) * rows, :])
    for index in range(count):
        sums_ref[index, :per, :] = low(up[index * per : (index + 1) * per, :])
    down = dot_tn(act_ref[...], mlp_ref[...])
    for index in range(count):
        sums_ref[index, per:, :] = low(down[index * per : (index + 1) * per, :])
    store_blocks(info, sums_ref, outs)


def down_kernel(count, skip, info, act_ref, *refs):
    dy_refs = refs[:4]
    chunks = refs[4 : 4 + count]
    near_ref, far_ref, gate_ref, weight_ref = refs[4 + count :]
    rows = dy_refs[0].shape[0]
    place_rows(info, chunks, skip, weight_ref.shape[0] // count, weight_ref)
    total = jnp.zeros(gate_ref.shape, jnp.float32)
    for block in (2, 3, 1, 0):
        here = slice(block * rows, (block + 1) * rows)
        part = dot_nn(act_ref[here, :], weight_ref[...])
        total = total + jnp.sum(wide(dy_refs[block][...]) * part, axis=0, keepdims=True)
        dest = near_ref if block < 2 else far_ref
        dest[(block % 2) * rows : (block % 2 + 1) * rows, :] = low(part)
    gate_ref[...] = total


def branch_kernel(info, mod_ref, middle_ref, dy_ref, own_ref, core_ref, chip_ref, gate_ref, *refs):
    mid_ref, branch_ref, sums_ref = refs[4:7]
    att_refs = (refs[7], refs[8], None, refs[9])
    weight_ref, parts_ref = refs[10:]
    natural(info, refs[:4], weight_ref)
    rows, width = dy_ref.shape
    grad_hidden = wide(own_ref[:rows, :]) + wide(core_ref[:rows, :]) + wide(chip_ref[...])
    normed, scaling = norm_rows(middle_ref[...])
    sums_ref[0:1, :] = jnp.sum(grad_hidden * normed, axis=0, keepdims=True)
    sums_ref[1:2, :] = jnp.sum(grad_hidden, axis=0, keepdims=True)
    sums_ref[2:3, :] = gate_ref[...]
    grad_normed = grad_hidden * (1.0 + mod_ref[0:1, :])
    first_mean = jnp.mean(grad_normed, axis=-1, keepdims=True)
    second_mean = jnp.mean(grad_normed * normed, axis=-1, keepdims=True)
    mid_ref[...] = wide(dy_ref[...]) + scaling * (grad_normed - first_mean - normed * second_mean)
    span = weight_ref.shape[2]
    branch_ref[:, :width] = low(mid_ref[...])
    branch_ref[:, width + span :] = jnp.zeros(
        (rows, branch_ref.shape[1] - width - span), jnp.bfloat16
    )
    for columns in range(4):
        parts_ref[columns] = low(mid_ref[:, columns * span : (columns + 1) * span])
    for block, dest in enumerate(att_refs):
        at = pl.multiple_of(info[OWNER + block] * span, HEAD_DIM)
        total = dot_nt(parts_ref[0], weight_ref[0, pl.ds(at, span), :])
        for columns in range(1, 4):
            total = total + dot_nt(parts_ref[columns], weight_ref[columns, pl.ds(at, span), :])
        if dest is None:
            branch_ref[:, width : width + span] = low(total)
        else:
            dest[...] = low(total)


def out_grad_kernel(info, att_ref, core_att_ref, branch_ref, core_branch_ref, near_ref, parts_ref):
    span = att_ref.shape[2]
    for columns in range(4):
        here = slice(columns * span, (columns + 1) * span)
        parts_ref[columns] = branch_ref[:, here]
        parts_ref[4 + columns] = core_branch_ref[:, here]
    for block in range(2):
        owner = info[OWNER + block]
        branch, core_branch = parts_ref[owner], parts_ref[4 + owner]
        for part in range(4):
            near_ref[block, part * span : (part + 1) * span, :] = low(
                dot_tn(att_ref[part], branch) + dot_tn(core_att_ref[part], core_branch)
            )


def attend_back_kernel(heads, rows, info, cos_ref, sin_ref, q_ref, k_ref, v_ref, *refs):
    att = refs[:4]
    span = heads * HEAD_DIM
    width = 4 * span
    grads = ((refs[4], 0), (refs[5], 0), (refs[6], width), (refs[7], 0))
    out_ref, gx_ref, turn_ref, dq_ref, dk_ref, dv_ref = refs[8:]
    column = lax.broadcasted_iota(jnp.int32, (rows, HEAD_TILE), 1)

    def tile_of(ref, base, head):
        at = base + HEAD_TILE * (head // 2)
        if base or head % 2 or head + 1 < heads:
            tile = wide(ref[:, at : at + HEAD_TILE])
            return pltpu.roll(tile, HEAD_DIM, 1) if head % 2 else tile
        last = wide(ref[:, at:])
        return jnp.concatenate([last, jnp.zeros_like(last)], axis=1)

    for head in range(heads):
        there = slice(head * HEAD_TILE, (head + 1) * HEAD_TILE)
        for block in range(4):
            here = slice(block * rows, (block + 1) * rows)
            grad = jnp.where(column < HEAD_DIM, tile_of(*grads[block], head), 0.0)
            minus = -jnp.sum(grad * tile_of(att[block], 0, head), axis=-1, keepdims=True)
            first = wide(low(minus))
            gx_ref[here, :] = low(
                jnp.where(
                    column == HEAD_DIM,
                    first,
                    jnp.where(column == HEAD_DIM + 1, minus - first, grad),
                )
            )
        for block in range(4):
            here = slice(block * rows, (block + 1) * rows)
            keys = k_ref[here, there]
            probs = jnp.exp(dot_nt(keys, q_ref[:, there]))
            prob_grad = dot_nt(v_ref[here, there], gx_ref[...])
            score_grad = low(probs * prob_grad)
            dv_ref[here, there] = dot_nn(low(probs), gx_ref[...])
            dk_ref[here, there] = dot_nn(score_grad, q_ref[:, there])
            part = dot_tn(keys, score_grad)
            if block == 0:
                turn_ref[...] = part
            else:
                turn_ref[...] += part
        dq_ref[:, there] = jnp.transpose(turn_ref[...]) * 0.125

    for block in range(4):
        here = slice(block * rows, (block + 1) * rows)
        heads_of = [dq_ref[here, h * HEAD_TILE : (h + 1) * HEAD_TILE] for h in range(heads)]
        heads_of += [dk_ref[here, h * HEAD_TILE : (h + 1) * HEAD_TILE] for h in range(heads)]
        heads_of += [dv_ref[here, h * HEAD_TILE : (h + 1) * HEAD_TILE] for h in range(heads)]
        heads_of.append(jnp.zeros((rows, HEAD_TILE), jnp.float32))
        for tile in range((3 * heads + 1) // 2):
            both = jnp.where(
                column < HEAD_DIM,
                heads_of[2 * tile],
                pltpu.roll(heads_of[2 * tile + 1], HEAD_DIM, 1),
            )
            if tile < heads:
                both = both * cos_ref[here, :] - swap_halves(both) * sin_ref[here, :]
            out_ref[here, tile * HEAD_TILE : (tile + 1) * HEAD_TILE] = low(both)


def hidden_grad_kernel(rows, info, grad_ref, weight_ref, near_ref, far_ref):
    span = grad_ref.shape[1]

    @pl.loop(0, 2)
    def _(turn):
        there = pl.ds(pl.multiple_of(turn * rows, rows), rows)
        for half, dest in ((1, far_ref), (0, near_ref)):
            here = pl.ds(pl.multiple_of((2 * half + turn) * rows, rows), rows)
            dest[there, :] = low(dot_nt(grad_ref[here, :], weight_ref[:, :span]))


def qkv_grad_kernel(count, used, info, hidden_ref, grad_ref, near_ref, chip_ref, *refs):
    outs, sums_ref = refs[:-1], refs[-1]
    total = dot_tn(hidden_ref[...], grad_ref[...])
    out_total = wide(near_ref[0]) + wide(chip_ref[0])
    per = total.shape[0] // count
    for index in range(count):
        here = slice(index * per, (index + 1) * per)
        sums_ref[index, :, :used] = low(total[here, :used])
        sums_ref[index, :, used:] = low(out_total[here, :])
    store_blocks(info, sums_ref, outs)


def input_kernel(info, gain, tok_ref, mid_ref, own_ref, core_ref, chip_ref, out_ref):
    rows = tok_ref.shape[0]
    grad_hidden = wide(own_ref[:rows, :]) + wide(core_ref[:rows, :]) + wide(chip_ref[:rows, :])
    normed, scaling = norm_rows(wide(tok_ref[...]))
    grad_normed = grad_hidden * gain[...]
    first_mean = jnp.mean(grad_normed, axis=-1, keepdims=True)
    second_mean = jnp.mean(grad_normed * normed, axis=-1, keepdims=True)
    out_ref[...] = low(
        mid_ref[...] + scaling * (grad_normed - first_mean - normed * second_mean)
    )


def finish_mlp_kernel(count, info, *refs):
    blocks = refs[:4]
    up_ref, down_ref, all_ref = refs[4:]
    natural(info, blocks, all_ref)
    rows = up_ref.shape[0]
    piece = down_ref.shape[0] // 4
    for part in range(4):
        value = wide(all_ref[part])
        for index in range(count):
            at = (index * 4 + part) * piece
            up_ref[:, at : at + piece] = value[:rows, index * piece : (index + 1) * piece]
        down_ref[part * piece : (part + 1) * piece, :] = value[rows:, :]


def finish_qkv_kernel(info, *refs):
    blocks = refs[:4]
    weight_ref, gain_ref, out_ref, own_ref, sums_ref, all_ref = refs[4:]
    natural(info, blocks, all_ref)
    span = all_ref.shape[2] // 4
    total = jnp.zeros((out_ref.shape[0], 1), jnp.float32)
    for part in range(4):
        value = wide(all_ref[part])
        for third in range(3):
            at = (third * 4 + part) * span
            piece = value[:, third * span : (third + 1) * span]
            total = total + jnp.sum(
                wide(weight_ref[:, at : at + span]) * piece, axis=1, keepdims=True
            )
            out_ref[:, at : at + span] = piece
        own_ref[:, part * span : (part + 1) * span] = value[:, 3 * span :]
    turned = jnp.transpose(jnp.broadcast_to(total, (total.shape[0], HEAD_TILE)))
    sums_ref[...] = turned[0:1, :] / gain_ref[...]


def hop(values_in, mask):
    return lax.ppermute(values_in, "seq", [(i, i ^ mask) for i in range(lax.axis_size("seq"))])


def ring_of(count):
    return [0] + list(range(1, count, 2)) + [i for i in range(count - 1, 0, -1) if i % 2 == 0]


def ring_next(data_count):
    outer = data_count // 2
    ring = ring_of(outer)
    follow = {ring[i]: ring[(i + 1) % outer] for i in range(outer)}
    return [(z * 2 + y, follow[z] * 2 + y) for z in range(outer) for y in range(2)]


def pair(values_in):
    return lax.ppermute(values_in, "dp", [(i, i ^ 1) for i in range(lax.axis_size("dp"))])


def dp_sum_direct(blocks):
    data_count = lax.axis_size("dp")
    if data_count != 8:
        return wide(lax.psum_scatter(blocks, "dp", scatter_dimension=0, tiled=False))
    return jnp.sum(wide(lax.all_to_all(blocks, "dp", 0, 0, tiled=True)), axis=0)


def after(values_in, *earlier):
    return lax.optimization_barrier((values_in,) + earlier)[0]


def onward(values_in):
    return lax.ppermute(values_in, "dp", ring_next(lax.axis_size("dp")))


def kernel_info(layout, rank, index, tok_rows):
    data_count = lax.axis_size("dp")
    column = jnp.arange(PLACE + 8, dtype=jnp.int32)

    def owner(block):
        return rank ^ ((block & 1) * 2 + (block >> 1))

    values = jnp.where(column == 0, layout[0, 0], layout[0, 1])
    values = jnp.where(column >= FIRST, owner(column - FIRST) * tok_rows, values)
    values = jnp.where(column >= OWNER, owner(column - OWNER), values)
    if data_count == 8:
        step = column - PLACE
        at = index >> 1
        at = ((at ^ (at >> 1)) - (step >> 1)) & 3
        place = (at ^ (at >> 1)) * 2 + ((index + step) & 1)
    else:
        place = jnp.zeros_like(column)
    return jnp.where(column >= PLACE, place, values)


def gathered_whole(chunk, sizes):
    gathered = lax.all_gather(chunk, "dp", axis=0)
    parts = []
    at = 0
    for size in sizes:
        parts.append(gathered[:, at : at + size].reshape(-1, chunk.shape[1]))
        at += size
    return [jnp.concatenate(parts, axis=0)]


def four(values_in):
    chip = hop(values_in, 2)
    return [values_in, chip, hop(values_in, 1), hop(chip, 1)]


def beyond(values_in, mask):
    return lax.ppermute(values_in, "dp", [(i, i ^ mask) for i in range(lax.axis_size("dp"))])


def doubled(parts, other, bit):
    return jnp.where(
        bit, jnp.concatenate([other, parts], axis=0), jnp.concatenate([parts, other], axis=0)
    )


def body(tokens, ln1_gain, w_qkv, w_out, w_ada, w_up, w_down, out_grad, layout, timestep):
    seq_count = lax.axis_size("seq")
    data_count = lax.axis_size("dp")
    ringed = data_count == 8
    rank = lax.axis_index("seq")
    index = lax.axis_index("dp")
    high = [(index >> place) & 1 == 1 for place in range(data_count.bit_length() - 1)]
    tokens, rank, index, high = lax.optimization_barrier((tokens, rank, index, high))
    tok_rows, width = tokens.shape
    group_rows = tok_rows * seq_count
    heads_local = HEADS // seq_count
    local_width = heads_local * HEAD_DIM
    head_columns = heads_local * HEAD_TILE
    padded = (3 * heads_local + 1) // 2 * HEAD_TILE
    rows = w_qkv.shape[0]
    hidden = w_up.shape[1] // seq_count
    down_piece = w_down.shape[0] // seq_count
    rank_word = rank.reshape(1).astype(jnp.int32)

    tok_chip = hop(tokens, 2)
    first = run(
        first_part_kernel,
        [shaped((rows, 4 * local_width))],
        [rank_word, w_qkv, w_out],
        0,
        name="first_part",
    )[0]
    if ringed:
        held = [first, onward(first)]
        beside = [pair(first)]
        held[1], beside[0], tokens = lax.optimization_barrier((held[1], beside[0], tokens))
        held.append(onward(held[1]))
        beside.append(pair(held[1]))
        tok_core = hop(tokens, 1)
        held[2], beside[1], tok_chip, tok_core = lax.optimization_barrier(
            (held[2], beside[1], tok_chip, tok_core)
        )
        held.append(onward(held[2]))
        beside.append(pair(held[2]))
        tok_both = hop(tok_chip, 1)
    else:
        tok_core, tok_both = hop(tokens, 1), hop(tok_chip, 1)
    tok_blocks = [tokens, tok_chip, tok_core, tok_both]

    embed = low(time_table(wide(timestep), width))
    sent = jnp.stack(
        [embed.reshape(data_count, rows), jnp.broadcast_to(ln1_gain, (data_count, rows))], axis=1
    )
    if ringed:
        sent = after(sent, held[1])
    taken = lax.all_to_all(sent, "dp", 0, 0, tiled=True)
    embeds = taken[:, 0]
    gain = wide(taken[:, 1].reshape(1, width))
    mod_parts = run(
        modulation_kernel,
        [shaped((data_count, 3, width), jnp.float32)],
        [rank_word, after(embeds, held[2]) if ringed else embeds, w_ada],
        2 * data_count * rows * w_ada.shape[1],
        name="modulation",
    )[0]

    def halves(parts, place):
        half = parts.shape[0] // 2
        kept = jnp.where(high[place], parts[half:], parts[:half])
        given = jnp.where(high[place], parts[:half], parts[half:])
        return kept, beyond(given, 1 << place)

    modulation = mod_parts
    for place in range(len(high) - 1, 2, -1):
        modulation = sum(halves(modulation, place))

    info = kernel_info(layout, rank, index, tok_rows)
    starts = info[FIRST:OWNER]
    if ringed:
        starts = after(starts, held[2])
    positions = (starts[:, None] + jnp.arange(tok_rows, dtype=jnp.int32)[None, :]).reshape(-1)
    cos_table, sin_table = rope_tables(positions)

    second = run(
        functools.partial(second_part_kernel, data_count),
        [shaped((rows + down_piece, width))],
        [rank_word, w_up, w_down],
        0,
        name="second_part",
    )[0]
    if ringed:
        dy_core = hop(after(out_grad, held[2]), 1)
        held[3], beside[2], second, dy_core, *rest = lax.optimization_barrier(
            (
                held[3],
                beside[2],
                second,
                dy_core,
                gain,
                info,
                cos_table,
                sin_table,
                tok_blocks,
            )
        )
        gain, info, cos_table, sin_table, tok_blocks = rest
        beside.append(pair(held[3]))
        first_chunks = [part for both in zip(held, beside) for part in both]
        held = [second, onward(second)]
        beside = [pair(after(second, beside[3]))]
        dy_chip = hop(after(out_grad, held[0]), 2)
    else:
        first_chunks = gathered_whole(first, [rows])
        second_chunks = gathered_whole(second, [rows, down_piece])
        dy_chip, dy_core = hop(out_grad, 2), hop(out_grad, 1)
    kept, sums = halves(modulation, 2)
    if ringed:
        gain, sums = lax.optimization_barrier((gain, sums))
    kept, sums = halves(kept + sums, 1)
    count = len(first_chunks)
    up_rows = rows * (data_count // count)

    hidden_one, qkv_weight, own_out, queries, keys, values = run(
        functools.partial(qkv_kernel, heads_local, count),
        [
            shaped((group_rows, width)),
            shaped((width, 4 * local_width)),
            shaped((width, local_width)),
            shaped((group_rows, head_columns)),
            shaped((group_rows, head_columns)),
            shaped((group_rows, head_columns)),
        ],
        [info, gain, cos_table, sin_table] + tok_blocks + first_chunks,
        2 * group_rows * width * padded,
        scratch=[pltpu.VMEM((seq_count, tok_rows, width), jnp.bfloat16)],
        name="qkv",
    )
    if ringed:
        queries, own_out, held[1], beside[0], sums = lax.optimization_barrier(
            (queries, own_out, held[1], beside[0], sums)
        )
        beside.append(pair(held[1]))
        held.append(onward(held[1]))
    kept, sums = halves(kept + sums, 0)
    chip_out = hop(own_out, 2)
    core_out = hop(own_out, 1)
    *att_parts, marked = run(
        functools.partial(attend_kernel, heads_local, tok_rows),
        [shaped((tok_rows, local_width))] * 4 + [shaped((group_rows, head_columns))],
        [info, queries, keys, values],
        4 * group_rows * group_rows * head_columns,
        scratch=[pltpu.VMEM((group_rows, local_width), jnp.bfloat16)],
        name="attend",
    )
    if ringed:
        att_parts, held[2], beside[1], chip_out, core_out, dy_chip, sums = lax.optimization_barrier(
            (att_parts, held[2], beside[1], chip_out, core_out, dy_chip, sums)
        )
        beside.append(pair(held[2]))
        held.append(onward(held[2]))
    modulation = (kept + sums)[0]
    att_own = [att_parts[0]] + [hop(att_parts[j], MASKS[j]) for j in (1, 2, 3)]
    out_blocks = [own_out, chip_out, core_out, hop(after(chip_out, att_own[2]), 1)]
    if ringed:
        att_own = lax.optimization_barrier(att_own)
    middle, hidden_two, att_ordered = run(
        middle_kernel,
        [
            shaped((tok_rows, width), jnp.float32),
            shaped((tok_rows, width)),
            shaped((seq_count, tok_rows, local_width)),
        ],
        [info, tokens, modulation] + out_blocks + att_own,
        2 * tok_rows * width * width,
        scratch=[pltpu.VMEM((seq_count, width, local_width), jnp.bfloat16)],
        name="middle",
    )

    chip_hidden = hop(hidden_two, 2)
    if ringed:
        beside.append(pair(held[3]))
        second_chunks = [part for both in zip(held, beside) for part in both]
    dy_blocks = [out_grad, dy_chip, dy_core, hop(after(dy_chip, hidden_two), 1)]
    grad_mlp, grad_act = run(
        functools.partial(act_grad_kernel, count, up_rows),
        [shaped((group_rows, width)), shaped((group_rows, hidden))],
        [info, modulation] + dy_blocks + second_chunks,
        2 * group_rows * width * hidden,
        scratch=[pltpu.VMEM((hidden, width), jnp.bfloat16)],
        name="act_grad",
    )
    hid_blocks = [
        hidden_two,
        chip_hidden,
        hop(hidden_two, 1),
        hop(after(chip_hidden, grad_act), 1),
    ]
    half = shaped((group_rows // 2, width))
    activated, grad_pre, gh_near, gh_far = run(
        functools.partial(forward_kernel, count),
        [shaped((group_rows, hidden)), shaped((group_rows, hidden)), half, half],
        [info, grad_act] + hid_blocks + second_chunks,
        4 * group_rows * width * hidden,
        scratch=[
            pltpu.VMEM((width, hidden), jnp.bfloat16),
            pltpu.VMEM((seq_count, tok_rows, width), jnp.bfloat16),
        ],
        name="forward",
    )
    block_shape = (rows + down_piece, width)
    grad_weights = run(
        functools.partial(weight_grad_kernel, data_count),
        [shaped(block_shape)] * count if ringed else [shaped((data_count,) + block_shape)],
        [info, activated, grad_mlp, grad_pre] + hid_blocks,
        4 * group_rows * width * hidden,
        scratch=[pltpu.VMEM((data_count,) + block_shape, jnp.bfloat16)],
        name="weight_grad",
    )
    gh_core = hop(gh_far, 1)
    gh_core, grad_weights = lax.optimization_barrier((gh_core, grad_weights))
    gh_send = low(wide(gh_near[tok_rows:]) + wide(gh_core[tok_rows:]))
    gh_chip = hop(gh_send, 2)
    mlp_near, mlp_far, grad_gate = run(
        functools.partial(down_kernel, count, up_rows),
        [half, half, shaped((1, width), jnp.float32)],
        [info, after(activated, gh_send)] + dy_blocks + second_chunks,
        2 * group_rows * width * hidden,
        scratch=[pltpu.VMEM((hidden, width), jnp.bfloat16)],
        name="down",
    )
    if ringed:
        mlp_keep, mlp_give = list(grad_weights[0::2]), list(grad_weights[1::2])
        mlp_taken = pair(after(mlp_give[1], gh_send))
        gh_chip, mlp_far, mlp_taken = lax.optimization_barrier((gh_chip, mlp_far, mlp_taken))
        mlp_ring = low(wide(mlp_keep[1]) + wide(mlp_taken))
        gh_chip, mlp_ring = lax.optimization_barrier((gh_chip, mlp_ring))
        mlp_carried = onward(mlp_ring)
        mlp_taken = pair(after(mlp_give[2], mlp_ring))
    else:
        gh_chip, mlp_far = lax.optimization_barrier((gh_chip, mlp_far))
    mlp_core = hop(mlp_far, 1)
    core_attended = hop(after(att_ordered, gh_chip), 1)

    branch_columns = -(-(width + local_width) // HEAD_TILE) * HEAD_TILE
    grad_middle, branch, grad_mod, *grad_parts = run(
        branch_kernel,
        [
            shaped((tok_rows, width), jnp.float32),
            shaped((tok_rows, branch_columns)),
            shaped((3, width), jnp.float32),
        ]
        + [shaped((tok_rows, local_width))] * 3,
        [info, modulation, after(middle, mlp_near), out_grad, gh_near, gh_core, gh_chip]
        + [grad_gate]
        + out_blocks,
        2 * tok_rows * width * width,
        scratch=[
            pltpu.VMEM((seq_count, width, local_width), jnp.bfloat16),
            pltpu.VMEM((seq_count, tok_rows, local_width), jnp.bfloat16),
        ],
        name="branch",
    )
    grad_parts, mlp_core = lax.optimization_barrier((grad_parts, mlp_core))
    core_branch = hop(branch, 1)
    grad_att = [grad_parts[0], hop(grad_parts[1], 2), core_branch, hop(grad_parts[2], 3)]
    out_sums = run(
        out_grad_kernel,
        [shaped((2, width, local_width))],
        [info, att_ordered, core_attended, branch, core_branch],
        2 * tok_rows * width * width,
        scratch=[pltpu.VMEM((2 * seq_count, tok_rows, local_width), jnp.bfloat16)],
        name="out_grad",
    )[0]

    if ringed:
        del grad_att[2]
        grad_att, out_sums, mlp_taken, mlp_carried = lax.optimization_barrier(
            (grad_att, out_sums, mlp_taken, mlp_carried)
        )
        grad_att.insert(2, core_branch)
        mlp_ring = low(wide(mlp_keep[2]) + wide(mlp_taken) + wide(mlp_carried))
        mlp_carried = onward(mlp_ring)
        mlp_taken = pair(after(mlp_give[3], mlp_ring))
    out_chip = hop(out_sums[1:], 2)
    mod_core = hop(grad_mod, 1)
    grad_qkv = run(
        functools.partial(attend_back_kernel, heads_local, tok_rows),
        [shaped((group_rows, padded))],
        [info, cos_table, sin_table, marked, keys, values] + att_parts + grad_att,
        10 * group_rows * group_rows * head_columns,
        scratch=[
            pltpu.VMEM((group_rows, HEAD_TILE), jnp.bfloat16),
            pltpu.VMEM((HEAD_TILE, group_rows), jnp.float32),
            pltpu.VMEM((group_rows, head_columns), jnp.float32),
            pltpu.VMEM((group_rows, head_columns), jnp.float32),
            pltpu.VMEM((group_rows, head_columns), jnp.float32),
        ],
        name="attend_back",
    )[0]
    grad_qkv, out_chip, mod_core = lax.optimization_barrier((grad_qkv, out_chip, mod_core))
    grad_mod = grad_mod + mod_core
    mod_chip = hop(grad_mod, 2)
    mlp_send = low(wide(after(mlp_near[tok_rows:], grad_qkv)) + wide(mlp_core[tok_rows:]))
    mlp_chip = hop(mlp_send, 2)
    if ringed:
        grad_qkv, mlp_taken, mlp_carried = lax.optimization_barrier(
            (grad_qkv, mlp_taken, mlp_carried)
        )
    qkv_sums = run(
        functools.partial(qkv_grad_kernel, data_count, 3 * local_width),
        [shaped((rows, 4 * local_width))] * count
        if ringed
        else [shaped((data_count, rows, 4 * local_width))],
        [info, hidden_one, grad_qkv, out_sums, out_chip],
        2 * group_rows * width * padded,
        scratch=[pltpu.VMEM((data_count, rows, 4 * local_width), jnp.bfloat16)],
        name="qkv_grad",
    )
    gq_near, gq_far = run(
        functools.partial(hidden_grad_kernel, tok_rows),
        [half, half],
        [info, after(grad_qkv, qkv_sums[0]), qkv_weight],
        2 * group_rows * width * padded,
        name="hidden_grad",
    )
    if ringed:
        qkv_keep, qkv_give = list(qkv_sums[0::2]), list(qkv_sums[1::2])
        qkv_taken = pair(qkv_give[1])
        mlp_ring = low(wide(after(mlp_keep[3], qkv_sums[0])) + wide(mlp_taken) + wide(mlp_carried))
        mlp_carried = onward(mlp_ring)
        mlp_taken = pair(after(mlp_give[0], mlp_ring))
        gq_far, qkv_taken, mod_chip = lax.optimization_barrier((gq_far, qkv_taken, mod_chip))
        qkv_ring = low(wide(qkv_keep[1]) + wide(qkv_taken))
        qkv_carried = onward(qkv_ring)
        qkv_taken = pair(after(qkv_give[2], qkv_ring))
    grad_mod = (grad_mod + mod_chip)[None]
    mod_other = beyond(grad_mod, 1)
    gq_core = hop(gq_far, 1)
    gq_send = low(wide(gq_near[tok_rows:]) + wide(gq_core[tok_rows:]))
    if ringed:
        qkv_carried, qkv_taken, gq_send, mlp_carried, mlp_taken = lax.optimization_barrier(
            (qkv_carried, qkv_taken, gq_send, mlp_carried, mlp_taken)
        )
        qkv_ring = low(wide(qkv_keep[2]) + wide(qkv_taken) + wide(qkv_carried))
        qkv_carried = onward(qkv_ring)
        qkv_taken = pair(after(qkv_give[3], qkv_ring))
    gq_chip = hop(gq_send, 2)
    if ringed:
        sum_mlp = low(wide(mlp_keep[0]) + wide(mlp_taken) + wide(mlp_carried))
        qkv_carried, qkv_taken, mlp_chip, mod_other = lax.optimization_barrier(
            (qkv_carried, qkv_taken, mlp_chip, mod_other)
        )
        qkv_ring = low(wide(qkv_keep[3]) + wide(qkv_taken) + wide(qkv_carried))
        qkv_carried = onward(qkv_ring)
        qkv_taken = pair(after(qkv_give[0], qkv_ring))
    else:
        sum_mlp = low(dp_sum_direct(grad_weights[0]))
    grad_mod = doubled(grad_mod, mod_other, high[0])
    sum_mlp, gq_chip = lax.optimization_barrier((sum_mlp, gq_chip))
    mlp_blocks = four(sum_mlp)
    grad_inputs = run(
        input_kernel,
        [shaped((tok_rows, width))],
        [info, gain, tokens, grad_middle, gq_near, gq_core, gq_chip],
        20 * tok_rows * width,
        name="input",
    )[0]
    for place in range(1, len(high)):
        grad_mod = doubled(grad_mod, beyond(grad_mod, 1 << place), high[place])
    grad_mods = grad_mod.reshape(data_count, 3 * width)
    if ringed:
        qkv_carried, qkv_taken, grad_inputs = lax.optimization_barrier(
            (qkv_carried, qkv_taken, grad_inputs)
        )
        sum_qkv = low(wide(qkv_keep[0]) + wide(qkv_taken) + wide(qkv_carried))
    else:
        sum_qkv = low(dp_sum_direct(qkv_sums[0]))
    mlp_out = wide(mlp_near[:tok_rows]) + wide(mlp_core[:tok_rows]) + wide(mlp_chip)
    result = low(middle + modulation[2:3] * mlp_out)
    final_ada = lax.dot_general(
        wide(embeds), grad_mods, (((0,), (0,)), ((), ())), precision=lax.Precision.HIGHEST
    )

    final_up, final_down = run(
        functools.partial(finish_mlp_kernel, data_count),
        [shaped(w_up.shape, jnp.float32), shaped(w_down.shape, jnp.float32)],
        [info] + mlp_blocks,
        0,
        scratch=[pltpu.VMEM((seq_count,) + block_shape, jnp.bfloat16)],
        name="finish_mlp",
    )
    final_qkv, final_out, final_gain = run(
        finish_qkv_kernel,
        [
            shaped(w_qkv.shape, jnp.float32),
            shaped(w_out.shape, jnp.float32),
            shaped((1, rows), jnp.float32),
        ],
        [info] + four(sum_qkv) + [w_qkv, wide(ln1_gain).reshape(1, rows)],
        0,
        scratch=[pltpu.VMEM((seq_count, rows, 4 * local_width), jnp.bfloat16)],
        name="finish_qkv",
    )
    return (
        result,
        grad_inputs,
        final_gain.reshape(-1),
        final_qkv,
        final_out,
        final_ada,
        final_up,
        final_down,
    )


def solution(mesh):
    placed = (
        P(("dp", "seq"), None),
        P("dp"),
        P("dp", None),
        P("dp", None),
        P("dp", None),
        P("dp", None),
        P("dp", None),
        P(("dp", "seq"), None),
        P("dp", None),
        P("dp"),
    )
    return jax.shard_map(
        body,
        mesh=mesh,
        in_specs=placed,
        out_specs=(
            P(("dp", "seq"), None),
            P(("dp", "seq"), None),
            P("dp"),
            P("dp", None),
            P("dp", None),
            P("dp", None),
            P("dp", None),
            P("dp", None),
        ),
        check_vma=False,
    )
```

```python
import functools
import math

import jax
import jax.numpy as jnp
from jax import lax
from jax.experimental import pallas as pl
from jax.experimental.pallas import tpu as pltpu
from jax.sharding import PartitionSpec as P

HEADS = 12
HEAD_DIM = 64

eps = 1e-05

MASKS = (0, 2, 1, 3)


def time_table(time_steps, model_width):
    half_dim = model_width // 2
    frequency = jnp.exp(-math.log(10000.0) * jnp.arange(half_dim, dtype=jnp.float32) / half_dim)
    angles = time_steps[:, None] * frequency[None, :]
    return jnp.concatenate([jnp.cos(angles), jnp.sin(angles)], axis=1)


def low(values_in):
    return values_in.astype(jnp.bfloat16)


def wide(values_in):
    return values_in.astype(jnp.float32)


HEAD_TILE = 128
COST = 1.0
VMEM_GRANT = 16 * 1024 * 1024
MASK_FILL = -1e30
GELU_IN = math.sqrt(2.0 / math.pi)
GELU_CUBE = 0.044715


def rope_tables(positions):
    half_dim = HEAD_DIM // 2
    column = jnp.arange(2 * HEAD_DIM, dtype=jnp.int32)
    frequency = jnp.exp(
        -math.log(10000.0) * 2.0 * (column % half_dim).astype(jnp.float32) / HEAD_DIM
    )
    angles = positions.astype(jnp.float32)[:, None] * frequency[None, :]
    sign = jnp.where(column % HEAD_DIM < half_dim, -1.0, 1.0)
    return (jnp.cos(angles), jnp.sin(angles) * sign[None, :])


def dot_nn(left, right):
    return lax.dot_general(
        left, right, (((1,), (0,)), ((), ())), preferred_element_type=jnp.float32
    )


def dot_nt(left, right):
    return lax.dot_general(
        left, right, (((1,), (1,)), ((), ())), preferred_element_type=jnp.float32
    )


def dot_tn(left, right):
    return lax.dot_general(
        left, right, (((0,), (0,)), ((), ())), preferred_element_type=jnp.float32
    )


def norm_rows(values_in):
    average = jnp.mean(values_in, axis=-1, keepdims=True)
    centred = values_in - average
    variance = jnp.mean(centred * centred, axis=-1, keepdims=True)
    scaling = lax.rsqrt(variance + eps)
    return (centred * scaling, scaling)


def swap_halves(values_in):
    column = lax.broadcasted_iota(jnp.int32, values_in.shape, 1)
    ahead = pltpu.roll(values_in, HEAD_TILE - HEAD_DIM // 2, 1)
    behind = pltpu.roll(values_in, HEAD_DIM // 2, 1)
    return jnp.where(column % HEAD_DIM < HEAD_DIM // 2, ahead, behind)


def whole(count):
    return [pl.BlockSpec(memory_space=pltpu.VMEM)] * count


def scalars():
    return [pl.BlockSpec(memory_space=pltpu.SMEM)]


def run(kernel, out_shapes, args, flops, scratch=(), name=None):
    nbytes = sum(a.size * a.dtype.itemsize for a in args)
    nbytes += sum(math.prod(o.shape) * o.dtype.itemsize for o in out_shapes)
    call = pl.pallas_call(
        kernel,
        out_shape=out_shapes,
        in_specs=scalars() + whole(len(args) - 1),
        out_specs=whole(len(out_shapes)),
        scratch_shapes=list(scratch),
        cost_estimate=pl.CostEstimate(flops=int(flops * COST), bytes_accessed=int(nbytes * COST), transcendentals=0),
        compiler_params=pltpu.CompilerParams(vmem_limit_bytes=VMEM_GRANT),
        name=name,
    )
    return call(*args)


def shaped(shape, kind=jnp.bfloat16):
    return jax.ShapeDtypeStruct(shape, kind)


FIRST, OWNER, PLACE = 2, 6, 10


def block_segment(info, block, rows, axis):
    shape = (rows, 1) if axis == 0 else (1, rows)
    position = info[FIRST + block] + lax.broadcasted_iota(jnp.int32, shape, axis)
    return (position >= info[0]).astype(jnp.int32) + (position >= info[1]).astype(jnp.int32)


def place_rows(info, chunks, first, rows, dest):
    for index, chunk in enumerate(chunks):
        at = pl.multiple_of(info[PLACE + index] * rows, rows)
        dest[pl.ds(at, rows), : chunk.shape[1]] = chunk[first : first + rows, :]


def store_blocks(info, sums_ref, outs):
    if len(outs) == 1:
        outs[0][...] = sums_ref[...]
    else:
        for index, dest in enumerate(outs):
            dest[...] = sums_ref[info[PLACE + index]]


def first_part_kernel(info, qkv_ref, out_ref, dest):
    span = dest.shape[1] // 4
    for part in range(4):

        @pl.when(info[0] == part)
        def _():
            for third in range(3):
                at = (third * 4 + part) * span
                dest[:, third * span : (third + 1) * span] = qkv_ref[:, at : at + span]
            dest[:, 3 * span :] = out_ref[:, part * span : (part + 1) * span]


def modulation_kernel(info, embed_ref, weight_ref, out_ref):
    width = out_ref.shape[2]
    for third in range(3):
        part = dot_nn(embed_ref[...], weight_ref[:, third * width : (third + 1) * width])
        for group in range(out_ref.shape[0]):
            out_ref[group, third : third + 1, :] = part[group : group + 1, :]


def second_part_kernel(count, info, up_ref, down_ref, dest):
    rows = up_ref.shape[0]
    piece = down_ref.shape[0] // 4
    for part in range(4):

        @pl.when(info[0] == part)
        def _():
            for index in range(count):
                at = (index * 4 + part) * piece
                dest[:rows, index * piece : (index + 1) * piece] = up_ref[:, at : at + piece]
            dest[rows:, :] = down_ref[part * piece : (part + 1) * piece, :]


def qkv_kernel(heads, count, info, *refs):
    gain, cos_ref, sin_ref = refs[:3]
    tok_refs = refs[3:7]
    chunks = refs[7 : 7 + count]
    hidden_ref, weight_ref, own_ref, q_ref, k_ref, v_ref, all_ref = refs[7 + count :]
    rows, width = tok_refs[0].shape
    lw = heads * HEAD_DIM
    place_rows(info, chunks, 0, width // count, weight_ref)
    own_ref[...] = weight_ref[:, 3 * lw : 4 * lw]
    gain_row = gain[...]
    for block in range(4):
        all_ref[block] = tok_refs[block][...]

    @pl.loop(0, 4)
    def _(block):
        normed, _ = norm_rows(wide(all_ref[block]))
        hidden = low(normed * gain_row)
        here = pl.ds(pl.multiple_of(block * rows, rows), rows)
        hidden_ref[here, :] = hidden
        both = dot_nn(hidden, weight_ref[:, : 2 * lw])
        last = dot_nn(hidden, weight_ref[:, 2 * lw : 2 * lw + 2 * HEAD_TILE])
        cos_part = cos_ref[here, :]
        sin_part = sin_ref[here, :]
        turned = []
        for tile in range(2 * lw // HEAD_TILE):
            piece = both[:, tile * HEAD_TILE : (tile + 1) * HEAD_TILE]
            turned.append(piece * cos_part + swap_halves(piece) * sin_part)
        column = lax.broadcasted_iota(jnp.int32, (rows, HEAD_TILE), 1)
        segment = block_segment(info, block, rows, 0)
        first_fill = jnp.where(segment == 1, 0.0, MASK_FILL)
        second_fill = jnp.where(segment == 2, 0.0, MASK_FILL)
        q_mark = jnp.where(
            column == HEAD_DIM, first_fill, jnp.where(column == HEAD_DIM + 1, second_fill, 0.0)
        )
        first_mark = jnp.where(segment == 1, 1.0, 0.0)
        second_mark = jnp.where(segment == 2, 1.0, 0.0)
        k_mark = jnp.where(
            column == HEAD_DIM,
            first_mark,
            jnp.where(
                column == HEAD_DIM + 1, second_mark, jnp.where(column < HEAD_DIM + 5, 1.0, 0.0)
            ),
        )
        v_mark = jnp.where(column < HEAD_DIM + 2, 1.0, 0.0)
        for head in range(heads):
            q_at, k_at = head, heads + head
            q_tile = turned[q_at // 2]
            k_tile = turned[k_at // 2]
            v_tile = last[:, HEAD_TILE * (head // 2) : HEAD_TILE * (head // 2 + 1)]
            if q_at % 2:
                q_tile = pltpu.roll(q_tile, HEAD_DIM, 1)
            if k_at % 2:
                k_tile = pltpu.roll(k_tile, HEAD_DIM, 1)
            if head % 2:
                v_tile = pltpu.roll(v_tile, HEAD_DIM, 1)
            there = slice(head * HEAD_TILE, (head + 1) * HEAD_TILE)
            q_ref[here, there] = low(jnp.where(column < HEAD_DIM, q_tile * 0.125, q_mark))
            k_ref[here, there] = low(jnp.where(column < HEAD_DIM, k_tile, k_mark))
            v_ref[here, there] = low(jnp.where(column < HEAD_DIM, v_tile, v_mark))


def attend_kernel(heads, rows, info, q_ref, k_ref, v_ref, *outs):
    att_refs = outs[:4]
    stat_ref, all_ref = outs[4:]
    column = lax.broadcasted_iota(jnp.int32, (rows, HEAD_TILE), 1)

    @pl.loop(0, 4)
    def _(block):
        here = pl.ds(pl.multiple_of(block * rows, rows), rows)
        results = []
        for head in range(heads):
            there = slice(head * HEAD_TILE, (head + 1) * HEAD_TILE)
            queries = q_ref[here, there]
            scores = dot_nt(queries, k_ref[:, there])
            row_max = jnp.max(scores, axis=-1, keepdims=True)
            weights = low(jnp.exp(scores - row_max))
            summed = dot_nn(weights, v_ref[:, there])
            row_sum = summed[:, HEAD_DIM : HEAD_DIM + 1]
            results.append(summed / row_sum)
            minus = -(row_max + jnp.log(row_sum))
            first = low(minus)
            second = low(minus - wide(first))
            third = low(minus - wide(first) - wide(second))
            stat_ref[here, there] = jnp.where(
                column == HEAD_DIM + 2,
                first,
                jnp.where(
                    column == HEAD_DIM + 3, second, jnp.where(column == HEAD_DIM + 4, third, queries)
                ),
            )
        for head in range(0, heads, 2):
            if head + 1 < heads:
                both = jnp.where(
                    column < HEAD_DIM, results[head], pltpu.roll(results[head + 1], HEAD_DIM, 1)
                )
                all_ref[here, head * HEAD_DIM : (head + 2) * HEAD_DIM] = low(both)
            else:
                all_ref[here, head * HEAD_DIM :] = low(results[head][:, :HEAD_DIM])

    for block in range(4):
        att_refs[block][...] = all_ref[block * rows : (block + 1) * rows, :]


def natural(info, blocks, dest):
    for block in range(4):
        dest[info[OWNER + block]] = blocks[block][...]


def middle_kernel(info, tok_ref, mod_ref, *refs):
    middle_ref, hidden_ref, att_ref, weight_ref = refs[8:]
    natural(info, refs[:4], weight_ref)
    natural(info, refs[4:8], att_ref)
    span = weight_ref.shape[2]
    for columns in range(4):
        there = slice(columns * span, (columns + 1) * span)
        total = wide(tok_ref[:, there])
        for part in range(4):
            total = total + dot_nn(
                att_ref[part], weight_ref[columns, part * span : (part + 1) * span, :]
            )
        middle_ref[:, there] = total
    normed, _ = norm_rows(middle_ref[...])
    hidden_ref[...] = low(normed * (1.0 + mod_ref[0:1, :]) + mod_ref[1:2, :])


def act_grad_kernel(count, skip, info, mod_ref, *refs):
    dy_refs = refs[:4]
    chunks = refs[4 : 4 + count]
    mlp_ref, act_ref, weight_ref = refs[4 + count :]
    rows = dy_refs[0].shape[0]
    place_rows(info, chunks, skip, weight_ref.shape[0] // count, weight_ref)
    gate = mod_ref[2:3, :]
    for block in range(4):
        here = slice(block * rows, (block + 1) * rows)
        mlp_ref[here, :] = low(gate * wide(dy_refs[block][...]))

    @pl.loop(0, 2)
    def _(turn):
        here = pl.ds(pl.multiple_of(turn * 2 * rows, 2 * rows), 2 * rows)
        act_ref[here, :] = low(dot_nt(mlp_ref[here, :], weight_ref[...]))


def forward_kernel(count, info, act_grad, *refs):
    hid_refs = refs[:4]
    chunks = refs[4 : 4 + count]
    act_ref, pre_ref, near_ref, far_ref, weight_ref, all_ref = refs[4 + count :]
    rows = hid_refs[0].shape[0]
    place_rows(info, chunks, 0, weight_ref.shape[0] // count, weight_ref)
    for block in range(4):
        all_ref[block] = hid_refs[block][...]

    @pl.loop(0, 2)
    def _(turn):
        there = pl.ds(pl.multiple_of(turn * rows, rows), rows)
        for half, dest in ((1, far_ref), (0, near_ref)):
            here = pl.ds(pl.multiple_of((2 * half + turn) * rows, rows), rows)
            pre = dot_nn(all_ref[2 * half + turn], weight_ref[...])
            square = pre * pre
            inner = jnp.tanh(GELU_IN * (pre + GELU_CUBE * (square * pre)))
            side = 0.5 * (1.0 + inner)
            act_ref[here, :] = low(pre * side)
            slope = side + 0.5 * pre * (1.0 - inner * inner) * (
                GELU_IN * (1.0 + 3.0 * GELU_CUBE * square)
            )
            grad_pre = low(wide(act_grad[here, :]) * slope)
            pre_ref[here, :] = grad_pre
            dest[there, :] = low(dot_nt(grad_pre, weight_ref[...]))


def weight_grad_kernel(count, info, act_ref, mlp_ref, pre_ref, *refs):
    hid_refs = refs[:4]
    outs, sums_ref = refs[4:-1], refs[-1]
    rows = hid_refs[0].shape[0]
    per = act_ref.shape[1] // count
    up = dot_tn(hid_refs[0][...], pre_ref[:rows, :])
    for block in range(1, 4):
        up = up + dot_tn(hid_refs[block][...], pre_ref[block * rows : (block + 1) * rows, :])
    for index in range(count):
        sums_ref[index, :per, :] = low(up[index * per : (index + 1) * per, :])
    down = dot_tn(act_ref[...], mlp_ref[...])
    for index in range(count):
        sums_ref[index, per:, :] = low(down[index * per : (index + 1) * per, :])
    store_blocks(info, sums_ref, outs)


def down_kernel(count, skip, info, act_ref, *refs):
    dy_refs = refs[:4]
    chunks = refs[4 : 4 + count]
    near_ref, far_ref, gate_ref, weight_ref = refs[4 + count :]
    rows = dy_refs[0].shape[0]
    place_rows(info, chunks, skip, weight_ref.shape[0] // count, weight_ref)
    total = jnp.zeros(gate_ref.shape, jnp.float32)
    for block in (2, 3, 1, 0):
        here = slice(block * rows, (block + 1) * rows)
        part = dot_nn(act_ref[here, :], weight_ref[...])
        total = total + jnp.sum(wide(dy_refs[block][...]) * part, axis=0, keepdims=True)
        dest = near_ref if block < 2 else far_ref
        dest[(block % 2) * rows : (block % 2 + 1) * rows, :] = low(part)
    gate_ref[...] = total


def branch_kernel(info, mod_ref, middle_ref, dy_ref, own_ref, core_ref, chip_ref, gate_ref, *refs):
    mid_ref, branch_ref, sums_ref = refs[4:7]
    att_refs = (refs[7], refs[8], None, refs[9])
    weight_ref, parts_ref = refs[10:]
    natural(info, refs[:4], weight_ref)
    rows, width = dy_ref.shape
    grad_hidden = wide(own_ref[:rows, :]) + wide(core_ref[:rows, :]) + wide(chip_ref[...])
    normed, scaling = norm_rows(middle_ref[...])
    sums_ref[0:1, :] = jnp.sum(grad_hidden * normed, axis=0, keepdims=True)
    sums_ref[1:2, :] = jnp.sum(grad_hidden, axis=0, keepdims=True)
    sums_ref[2:3, :] = gate_ref[...]
    grad_normed = grad_hidden * (1.0 + mod_ref[0:1, :])
    first_mean = jnp.mean(grad_normed, axis=-1, keepdims=True)
    second_mean = jnp.mean(grad_normed * normed, axis=-1, keepdims=True)
    mid_ref[...] = wide(dy_ref[...]) + scaling * (grad_normed - first_mean - normed * second_mean)
    span = weight_ref.shape[2]
    branch_ref[:, :width] = low(mid_ref[...])
    branch_ref[:, width + span :] = jnp.zeros(
        (rows, branch_ref.shape[1] - width - span), jnp.bfloat16
    )
    for columns in range(4):
        parts_ref[columns] = low(mid_ref[:, columns * span : (columns + 1) * span])
    for block, dest in enumerate(att_refs):
        at = pl.multiple_of(info[OWNER + block] * span, HEAD_DIM)
        total = dot_nt(parts_ref[0], weight_ref[0, pl.ds(at, span), :])
        for columns in range(1, 4):
            total = total + dot_nt(parts_ref[columns], weight_ref[columns, pl.ds(at, span), :])
        if dest is None:
            branch_ref[:, width : width + span] = low(total)
        else:
            dest[...] = low(total)


def out_grad_kernel(info, att_ref, core_att_ref, branch_ref, core_branch_ref, near_ref, parts_ref):
    span = att_ref.shape[2]
    for columns in range(4):
        here = slice(columns * span, (columns + 1) * span)
        parts_ref[columns] = branch_ref[:, here]
        parts_ref[4 + columns] = core_branch_ref[:, here]
    for block in range(2):
        owner = info[OWNER + block]
        branch, core_branch = parts_ref[owner], parts_ref[4 + owner]
        for part in range(4):
            near_ref[block, part * span : (part + 1) * span, :] = low(
                dot_tn(att_ref[part], branch) + dot_tn(core_att_ref[part], core_branch)
            )


def attend_back_kernel(heads, rows, info, cos_ref, sin_ref, q_ref, k_ref, v_ref, *refs):
    att = refs[:4]
    span = heads * HEAD_DIM
    width = 4 * span
    grads = ((refs[4], 0), (refs[5], 0), (refs[6], width), (refs[7], 0))
    out_ref, gx_ref, turn_ref, dq_ref, dk_ref, dv_ref = refs[8:]
    column = lax.broadcasted_iota(jnp.int32, (rows, HEAD_TILE), 1)

    def tile_of(ref, base, head):
        at = base + HEAD_TILE * (head // 2)
        if base or head % 2 or head + 1 < heads:
            tile = wide(ref[:, at : at + HEAD_TILE])
            return pltpu.roll(tile, HEAD_DIM, 1) if head % 2 else tile
        last = wide(ref[:, at:])
        return jnp.concatenate([last, jnp.zeros_like(last)], axis=1)

    for head in range(heads):
        there = slice(head * HEAD_TILE, (head + 1) * HEAD_TILE)
        for block in range(4):
            here = slice(block * rows, (block + 1) * rows)
            grad = jnp.where(column < HEAD_DIM, tile_of(*grads[block], head), 0.0)
            minus = -jnp.sum(grad * tile_of(att[block], 0, head), axis=-1, keepdims=True)
            first = wide(low(minus))
            gx_ref[here, :] = low(
                jnp.where(
                    column == HEAD_DIM,
                    first,
                    jnp.where(column == HEAD_DIM + 1, minus - first, grad),
                )
            )
        for block in range(4):
            here = slice(block * rows, (block + 1) * rows)
            keys = k_ref[here, there]
            probs = jnp.exp(dot_nt(keys, q_ref[:, there]))
            prob_grad = dot_nt(v_ref[here, there], gx_ref[...])
            score_grad = low(probs * prob_grad)
            dv_ref[here, there] = dot_nn(low(probs), gx_ref[...])
            dk_ref[here, there] = dot_nn(score_grad, q_ref[:, there])
            part = dot_tn(keys, score_grad)
            if block == 0:
                turn_ref[...] = part
            else:
                turn_ref[...] += part
        dq_ref[:, there] = jnp.transpose(turn_ref[...]) * 0.125

    for block in range(4):
        here = slice(block * rows, (block + 1) * rows)
        heads_of = [dq_ref[here, h * HEAD_TILE : (h + 1) * HEAD_TILE] for h in range(heads)]
        heads_of += [dk_ref[here, h * HEAD_TILE : (h + 1) * HEAD_TILE] for h in range(heads)]
        heads_of += [dv_ref[here, h * HEAD_TILE : (h + 1) * HEAD_TILE] for h in range(heads)]
        heads_of.append(jnp.zeros((rows, HEAD_TILE), jnp.float32))
        for tile in range((3 * heads + 1) // 2):
            both = jnp.where(
                column < HEAD_DIM,
                heads_of[2 * tile],
                pltpu.roll(heads_of[2 * tile + 1], HEAD_DIM, 1),
            )
            if tile < heads:
                both = both * cos_ref[here, :] - swap_halves(both) * sin_ref[here, :]
            out_ref[here, tile * HEAD_TILE : (tile + 1) * HEAD_TILE] = low(both)


def hidden_grad_kernel(rows, info, grad_ref, weight_ref, near_ref, far_ref):
    span = grad_ref.shape[1]

    @pl.loop(0, 2)
    def _(turn):
        there = pl.ds(pl.multiple_of(turn * rows, rows), rows)
        for half, dest in ((1, far_ref), (0, near_ref)):
            here = pl.ds(pl.multiple_of((2 * half + turn) * rows, rows), rows)
            dest[there, :] = low(dot_nt(grad_ref[here, :], weight_ref[:, :span]))


def qkv_grad_kernel(count, used, info, hidden_ref, grad_ref, near_ref, chip_ref, *refs):
    outs, sums_ref = refs[:-1], refs[-1]
    total = dot_tn(hidden_ref[...], grad_ref[...])
    out_total = wide(near_ref[0]) + wide(chip_ref[0])
    per = total.shape[0] // count
    for index in range(count):
        here = slice(index * per, (index + 1) * per)
        sums_ref[index, :, :used] = low(total[here, :used])
        sums_ref[index, :, used:] = low(out_total[here, :])
    store_blocks(info, sums_ref, outs)


def input_kernel(info, gain, tok_ref, mid_ref, own_ref, core_ref, chip_ref, out_ref):
    rows = tok_ref.shape[0]
    grad_hidden = wide(own_ref[:rows, :]) + wide(core_ref[:rows, :]) + wide(chip_ref[:rows, :])
    normed, scaling = norm_rows(wide(tok_ref[...]))
    grad_normed = grad_hidden * gain[...]
    first_mean = jnp.mean(grad_normed, axis=-1, keepdims=True)
    second_mean = jnp.mean(grad_normed * normed, axis=-1, keepdims=True)
    out_ref[...] = low(
        mid_ref[...] + scaling * (grad_normed - first_mean - normed * second_mean)
    )


def finish_mlp_kernel(count, info, *refs):
    blocks = refs[:4]
    up_ref, down_ref, all_ref = refs[4:]
    natural(info, blocks, all_ref)
    rows = up_ref.shape[0]
    piece = down_ref.shape[0] // 4
    for part in range(4):
        value = wide(all_ref[part])
        for index in range(count):
            at = (index * 4 + part) * piece
            up_ref[:, at : at + piece] = value[:rows, index * piece : (index + 1) * piece]
        down_ref[part * piece : (part + 1) * piece, :] = value[rows:, :]


def finish_qkv_kernel(info, *refs):
    blocks = refs[:4]
    weight_ref, gain_ref, out_ref, own_ref, sums_ref, all_ref = refs[4:]
    natural(info, blocks, all_ref)
    span = all_ref.shape[2] // 4
    total = jnp.zeros((out_ref.shape[0], 1), jnp.float32)
    for part in range(4):
        value = wide(all_ref[part])
        for third in range(3):
            at = (third * 4 + part) * span
            piece = value[:, third * span : (third + 1) * span]
            total = total + jnp.sum(
                wide(weight_ref[:, at : at + span]) * piece, axis=1, keepdims=True
            )
            out_ref[:, at : at + span] = piece
        own_ref[:, part * span : (part + 1) * span] = value[:, 3 * span :]
    turned = jnp.transpose(jnp.broadcast_to(total, (total.shape[0], HEAD_TILE)))
    sums_ref[...] = turned[0:1, :] / gain_ref[...]


def hop(values_in, mask):
    return lax.ppermute(values_in, "seq", [(i, i ^ mask) for i in range(lax.axis_size("seq"))])


def ring_of(count):
    return [0] + list(range(1, count, 2)) + [i for i in range(count - 1, 0, -1) if i % 2 == 0]


def ring_next(data_count):
    outer = data_count // 2
    ring = ring_of(outer)
    follow = {ring[i]: ring[(i + 1) % outer] for i in range(outer)}
    return [(z * 2 + y, follow[z] * 2 + y) for z in range(outer) for y in range(2)]


def pair(values_in):
    return lax.ppermute(values_in, "dp", [(i, i ^ 1) for i in range(lax.axis_size("dp"))])


def dp_sum_direct(blocks):
    data_count = lax.axis_size("dp")
    if data_count != 8:
        return wide(lax.psum_scatter(blocks, "dp", scatter_dimension=0, tiled=False))
    return jnp.sum(wide(lax.all_to_all(blocks, "dp", 0, 0, tiled=True)), axis=0)


def after(values_in, *earlier):
    return lax.optimization_barrier((values_in,) + earlier)[0]


def onward(values_in):
    return lax.ppermute(values_in, "dp", ring_next(lax.axis_size("dp")))


def kernel_info(layout, rank, index, tok_rows):
    data_count = lax.axis_size("dp")
    column = jnp.arange(PLACE + 8, dtype=jnp.int32)

    def owner(block):
        return rank ^ ((block & 1) * 2 + (block >> 1))

    values = jnp.where(column == 0, layout[0, 0], layout[0, 1])
    values = jnp.where(column >= FIRST, owner(column - FIRST) * tok_rows, values)
    values = jnp.where(column >= OWNER, owner(column - OWNER), values)
    if data_count == 8:
        step = column - PLACE
        at = index >> 1
        at = ((at ^ (at >> 1)) - (step >> 1)) & 3
        place = (at ^ (at >> 1)) * 2 + ((index + step) & 1)
    else:
        place = jnp.zeros_like(column)
    return jnp.where(column >= PLACE, place, values)


def gathered_whole(chunk, sizes):
    gathered = lax.all_gather(chunk, "dp", axis=0)
    parts = []
    at = 0
    for size in sizes:
        parts.append(gathered[:, at : at + size].reshape(-1, chunk.shape[1]))
        at += size
    return [jnp.concatenate(parts, axis=0)]


def four(values_in):
    chip = hop(values_in, 2)
    return [values_in, chip, hop(values_in, 1), hop(chip, 1)]


def beyond(values_in, mask):
    return lax.ppermute(values_in, "dp", [(i, i ^ mask) for i in range(lax.axis_size("dp"))])


def doubled(parts, other, bit):
    return jnp.where(
        bit, jnp.concatenate([other, parts], axis=0), jnp.concatenate([parts, other], axis=0)
    )


def body(tokens, ln1_gain, w_qkv, w_out, w_ada, w_up, w_down, out_grad, layout, timestep):
    seq_count = lax.axis_size("seq")
    data_count = lax.axis_size("dp")
    ringed = data_count == 8
    rank = lax.axis_index("seq")
    index = lax.axis_index("dp")
    high = [(index >> place) & 1 == 1 for place in range(data_count.bit_length() - 1)]
    tokens, rank, index, high = lax.optimization_barrier((tokens, rank, index, high))
    tok_rows, width = tokens.shape
    group_rows = tok_rows * seq_count
    heads_local = HEADS // seq_count
    local_width = heads_local * HEAD_DIM
    head_columns = heads_local * HEAD_TILE
    padded = (3 * heads_local + 1) // 2 * HEAD_TILE
    rows = w_qkv.shape[0]
    hidden = w_up.shape[1] // seq_count
    down_piece = w_down.shape[0] // seq_count
    rank_word = rank.reshape(1).astype(jnp.int32)

    tok_chip = hop(tokens, 2)
    first = run(
        first_part_kernel,
        [shaped((rows, 4 * local_width))],
        [rank_word, w_qkv, w_out],
        0,
        name="first_part",
    )[0]
    if ringed:
        held = [first, onward(first)]
        beside = [pair(first)]
        held[1], beside[0], tokens = lax.optimization_barrier((held[1], beside[0], tokens))
        held.append(onward(held[1]))
        beside.append(pair(held[1]))
        tok_core = hop(tokens, 1)
        held[2], beside[1], tok_chip, tok_core = lax.optimization_barrier(
            (held[2], beside[1], tok_chip, tok_core)
        )
        held.append(onward(held[2]))
        beside.append(pair(held[2]))
        tok_both = hop(tok_chip, 1)
    else:
        tok_core, tok_both = hop(tokens, 1), hop(tok_chip, 1)
    tok_blocks = [tokens, tok_chip, tok_core, tok_both]

    embed = low(time_table(wide(timestep), width))
    sent = jnp.stack(
        [embed.reshape(data_count, rows), jnp.broadcast_to(ln1_gain, (data_count, rows))], axis=1
    )
    if ringed:
        sent = after(sent, held[1])
    taken = lax.all_to_all(sent, "dp", 0, 0, tiled=True)
    embeds = taken[:, 0]
    gain = wide(taken[:, 1].reshape(1, width))
    mod_parts = run(
        modulation_kernel,
        [shaped((data_count, 3, width), jnp.float32)],
        [rank_word, after(embeds, held[2]) if ringed else embeds, w_ada],
        2 * data_count * rows * w_ada.shape[1],
        name="modulation",
    )[0]

    def halves(parts, place):
        half = parts.shape[0] // 2
        kept = jnp.where(high[place], parts[half:], parts[:half])
        given = jnp.where(high[place], parts[:half], parts[half:])
        return kept, beyond(given, 1 << place)

    modulation = mod_parts
    for place in range(len(high) - 1, 2, -1):
        modulation = sum(halves(modulation, place))

    info = kernel_info(layout, rank, index, tok_rows)
    starts = info[FIRST:OWNER]
    if ringed:
        starts = after(starts, held[2])
    positions = (starts[:, None] + jnp.arange(tok_rows, dtype=jnp.int32)[None, :]).reshape(-1)
    cos_table, sin_table = rope_tables(positions)

    second = run(
        functools.partial(second_part_kernel, data_count),
        [shaped((rows + down_piece, width))],
        [rank_word, w_up, w_down],
        0,
        name="second_part",
    )[0]
    if ringed:
        dy_core = hop(after(out_grad, held[2]), 1)
        held[3], beside[2], second, dy_core, *rest = lax.optimization_barrier(
            (
                held[3],
                beside[2],
                second,
                dy_core,
                gain,
                info,
                cos_table,
                sin_table,
                tok_blocks,
            )
        )
        gain, info, cos_table, sin_table, tok_blocks = rest
        beside.append(pair(held[3]))
        first_chunks = [part for both in zip(held, beside) for part in both]
        held = [second, onward(second)]
        beside = [pair(after(second, beside[3]))]
        dy_chip = hop(after(out_grad, held[0]), 2)
    else:
        first_chunks = gathered_whole(first, [rows])
        second_chunks = gathered_whole(second, [rows, down_piece])
        dy_chip, dy_core = hop(out_grad, 2), hop(out_grad, 1)
    kept, sums = halves(modulation, 2)
    if ringed:
        gain, sums = lax.optimization_barrier((gain, sums))
    kept, sums = halves(kept + sums, 1)
    count = len(first_chunks)
    up_rows = rows * (data_count // count)

    hidden_one, qkv_weight, own_out, queries, keys, values = run(
        functools.partial(qkv_kernel, heads_local, count),
        [
            shaped((group_rows, width)),
            shaped((width, 4 * local_width)),
            shaped((width, local_width)),
            shaped((group_rows, head_columns)),
            shaped((group_rows, head_columns)),
            shaped((group_rows, head_columns)),
        ],
        [info, gain, cos_table, sin_table] + tok_blocks + first_chunks,
        2 * group_rows * width * padded,
        scratch=[pltpu.VMEM((seq_count, tok_rows, width), jnp.bfloat16)],
        name="qkv",
    )
    if ringed:
        queries, own_out, held[1], beside[0], sums = lax.optimization_barrier(
            (queries, own_out, held[1], beside[0], sums)
        )
        beside.append(pair(held[1]))
        held.append(onward(held[1]))
    kept, sums = halves(kept + sums, 0)
    chip_out = hop(own_out, 2)
    core_out = hop(own_out, 1)
    *att_parts, marked = run(
        functools.partial(attend_kernel, heads_local, tok_rows),
        [shaped((tok_rows, local_width))] * 4 + [shaped((group_rows, head_columns))],
        [info, queries, keys, values],
        4 * group_rows * group_rows * head_columns,
        scratch=[pltpu.VMEM((group_rows, local_width), jnp.bfloat16)],
        name="attend",
    )
    if ringed:
        att_parts, held[2], beside[1], chip_out, core_out, dy_chip, sums = lax.optimization_barrier(
            (att_parts, held[2], beside[1], chip_out, core_out, dy_chip, sums)
        )
        beside.append(pair(held[2]))
        held.append(onward(held[2]))
    modulation = (kept + sums)[0]
    att_own = [att_parts[0]] + [hop(att_parts[j], MASKS[j]) for j in (1, 2, 3)]
    out_blocks = [own_out, chip_out, core_out, hop(after(chip_out, att_own[2]), 1)]
    if ringed:
        att_own, held[3], beside[2] = lax.optimization_barrier((att_own, held[3], beside[2]))
    middle, hidden_two, att_ordered = run(
        middle_kernel,
        [
            shaped((tok_rows, width), jnp.float32),
            shaped((tok_rows, width)),
            shaped((seq_count, tok_rows, local_width)),
        ],
        [info, tokens, modulation] + out_blocks + att_own,
        2 * tok_rows * width * width,
        scratch=[pltpu.VMEM((seq_count, width, local_width), jnp.bfloat16)],
        name="middle",
    )

    chip_hidden = hop(hidden_two, 2)
    if ringed:
        beside.append(pair(held[3]))
        second_chunks = [part for both in zip(held, beside) for part in both]
    dy_blocks = [out_grad, dy_chip, dy_core, hop(after(dy_chip, hidden_two), 1)]
    grad_mlp, grad_act = run(
        functools.partial(act_grad_kernel, count, up_rows),
        [shaped((group_rows, width)), shaped((group_rows, hidden))],
        [info, modulation] + dy_blocks + second_chunks,
        2 * group_rows * width * hidden,
        scratch=[pltpu.VMEM((hidden, width), jnp.bfloat16)],
        name="act_grad",
    )
    hid_blocks = [
        hidden_two,
        chip_hidden,
        hop(hidden_two, 1),
        hop(after(chip_hidden, grad_act), 1),
    ]
    half = shaped((group_rows // 2, width))
    activated, grad_pre, gh_near, gh_far = run(
        functools.partial(forward_kernel, count),
        [shaped((group_rows, hidden)), shaped((group_rows, hidden)), half, half],
        [info, grad_act] + hid_blocks + second_chunks,
        4 * group_rows * width * hidden,
        scratch=[
            pltpu.VMEM((width, hidden), jnp.bfloat16),
            pltpu.VMEM((seq_count, tok_rows, width), jnp.bfloat16),
        ],
        name="forward",
    )
    block_shape = (rows + down_piece, width)
    grad_weights = run(
        functools.partial(weight_grad_kernel, data_count),
        [shaped(block_shape)] * count if ringed else [shaped((data_count,) + block_shape)],
        [info, activated, grad_mlp, grad_pre] + hid_blocks,
        4 * group_rows * width * hidden,
        scratch=[pltpu.VMEM((data_count,) + block_shape, jnp.bfloat16)],
        name="weight_grad",
    )
    gh_core = hop(gh_far, 1)
    gh_core, grad_weights = lax.optimization_barrier((gh_core, grad_weights))
    gh_send = low(wide(gh_near[tok_rows:]) + wide(gh_core[tok_rows:]))
    gh_chip = hop(gh_send, 2)
    mlp_near, mlp_far, grad_gate = run(
        functools.partial(down_kernel, count, up_rows),
        [half, half, shaped((1, width), jnp.float32)],
        [info, after(activated, gh_send)] + dy_blocks + second_chunks,
        2 * group_rows * width * hidden,
        scratch=[pltpu.VMEM((hidden, width), jnp.bfloat16)],
        name="down",
    )
    if ringed:
        mlp_keep, mlp_give = list(grad_weights[0::2]), list(grad_weights[1::2])
        mlp_taken = pair(after(mlp_give[1], gh_send))
        gh_chip, mlp_far, mlp_taken = lax.optimization_barrier((gh_chip, mlp_far, mlp_taken))
        mlp_ring = low(wide(mlp_keep[1]) + wide(mlp_taken))
        gh_chip, mlp_ring = lax.optimization_barrier((gh_chip, mlp_ring))
        mlp_carried = onward(mlp_ring)
        mlp_taken = pair(after(mlp_give[2], mlp_ring))
    else:
        gh_chip, mlp_far = lax.optimization_barrier((gh_chip, mlp_far))
    mlp_core = hop(mlp_far, 1)
    core_attended = hop(after(att_ordered, gh_chip), 1)

    branch_columns = -(-(width + local_width) // HEAD_TILE) * HEAD_TILE
    grad_middle, branch, grad_mod, *grad_parts = run(
        branch_kernel,
        [
            shaped((tok_rows, width), jnp.float32),
            shaped((tok_rows, branch_columns)),
            shaped((3, width), jnp.float32),
        ]
        + [shaped((tok_rows, local_width))] * 3,
        [info, modulation, after(middle, mlp_near), out_grad, gh_near, gh_core, gh_chip]
        + [grad_gate]
        + out_blocks,
        2 * tok_rows * width * width,
        scratch=[
            pltpu.VMEM((seq_count, width, local_width), jnp.bfloat16),
            pltpu.VMEM((seq_count, tok_rows, local_width), jnp.bfloat16),
        ],
        name="branch",
    )
    grad_parts, mlp_core = lax.optimization_barrier((grad_parts, mlp_core))
    core_branch = hop(branch, 1)
    grad_att = [grad_parts[0], hop(grad_parts[1], 2), core_branch, hop(grad_parts[2], 3)]
    out_sums = run(
        out_grad_kernel,
        [shaped((2, width, local_width))],
        [info, att_ordered, core_attended, branch, core_branch],
        2 * tok_rows * width * width,
        scratch=[pltpu.VMEM((2 * seq_count, tok_rows, local_width), jnp.bfloat16)],
        name="out_grad",
    )[0]

    if ringed:
        del grad_att[2]
        grad_att, out_sums, mlp_taken, mlp_carried = lax.optimization_barrier(
            (grad_att, out_sums, mlp_taken, mlp_carried)
        )
        grad_att.insert(2, core_branch)
        mlp_ring = low(wide(mlp_keep[2]) + wide(mlp_taken) + wide(mlp_carried))
        mlp_carried = onward(mlp_ring)
        mlp_taken = pair(after(mlp_give[3], mlp_ring))
    out_chip = hop(out_sums[1:], 2)
    mod_core = hop(grad_mod, 1)
    grad_qkv = run(
        functools.partial(attend_back_kernel, heads_local, tok_rows),
        [shaped((group_rows, padded))],
        [info, cos_table, sin_table, marked, keys, values] + att_parts + grad_att,
        10 * group_rows * group_rows * head_columns,
        scratch=[
            pltpu.VMEM((group_rows, HEAD_TILE), jnp.bfloat16),
            pltpu.VMEM((HEAD_TILE, group_rows), jnp.float32),
            pltpu.VMEM((group_rows, head_columns), jnp.float32),
            pltpu.VMEM((group_rows, head_columns), jnp.float32),
            pltpu.VMEM((group_rows, head_columns), jnp.float32),
        ],
        name="attend_back",
    )[0]
    grad_qkv, out_chip, mod_core = lax.optimization_barrier((grad_qkv, out_chip, mod_core))
    grad_mod = grad_mod + mod_core
    mod_chip = hop(grad_mod, 2)
    mlp_send = low(wide(after(mlp_near[tok_rows:], grad_qkv)) + wide(mlp_core[tok_rows:]))
    mlp_chip = hop(mlp_send, 2)
    if ringed:
        grad_qkv, mlp_taken, mlp_carried = lax.optimization_barrier(
            (grad_qkv, mlp_taken, mlp_carried)
        )
    qkv_sums = run(
        functools.partial(qkv_grad_kernel, data_count, 3 * local_width),
        [shaped((rows, 4 * local_width))] * count
        if ringed
        else [shaped((data_count, rows, 4 * local_width))],
        [info, hidden_one, grad_qkv, out_sums, out_chip],
        2 * group_rows * width * padded,
        scratch=[pltpu.VMEM((data_count, rows, 4 * local_width), jnp.bfloat16)],
        name="qkv_grad",
    )
    gq_near, gq_far = run(
        functools.partial(hidden_grad_kernel, tok_rows),
        [half, half],
        [info, after(grad_qkv, qkv_sums[0]), qkv_weight],
        2 * group_rows * width * padded,
        name="hidden_grad",
    )
    if ringed:
        qkv_keep, qkv_give = list(qkv_sums[0::2]), list(qkv_sums[1::2])
        qkv_taken = pair(qkv_give[1])
        mlp_ring = low(wide(after(mlp_keep[3], qkv_sums[0])) + wide(mlp_taken) + wide(mlp_carried))
        mlp_carried = onward(mlp_ring)
        mlp_taken = pair(after(mlp_give[0], mlp_ring))
        gq_far, qkv_taken, mod_chip = lax.optimization_barrier((gq_far, qkv_taken, mod_chip))
        qkv_ring = low(wide(qkv_keep[1]) + wide(qkv_taken))
        qkv_carried = onward(qkv_ring)
        qkv_taken = pair(after(qkv_give[2], qkv_ring))
    grad_mod = (grad_mod + mod_chip)[None]
    mod_other = beyond(grad_mod, 1)
    gq_core = hop(gq_far, 1)
    gq_send = low(wide(gq_near[tok_rows:]) + wide(gq_core[tok_rows:]))
    if ringed:
        qkv_carried, qkv_taken, gq_send, mlp_carried, mlp_taken = lax.optimization_barrier(
            (qkv_carried, qkv_taken, gq_send, mlp_carried, mlp_taken)
        )
        qkv_ring = low(wide(qkv_keep[2]) + wide(qkv_taken) + wide(qkv_carried))
        qkv_carried = onward(qkv_ring)
        qkv_taken = pair(after(qkv_give[3], qkv_ring))
    if ringed:
        sum_mlp = low(wide(mlp_keep[0]) + wide(mlp_taken) + wide(mlp_carried))
        qkv_carried, qkv_taken, mlp_chip, mod_other, gq_send = lax.optimization_barrier(
            (qkv_carried, qkv_taken, mlp_chip, mod_other, gq_send)
        )
        qkv_ring = low(wide(qkv_keep[3]) + wide(qkv_taken) + wide(qkv_carried))
        qkv_carried = onward(qkv_ring)
        qkv_taken = pair(after(qkv_give[0], qkv_ring))
    else:
        sum_mlp = low(dp_sum_direct(grad_weights[0]))
    gq_chip = hop(gq_send, 2)
    grad_mod = doubled(grad_mod, mod_other, high[0])
    mlp_blocks = four(sum_mlp)
    grad_inputs = run(
        input_kernel,
        [shaped((tok_rows, width))],
        [info, gain, tokens, grad_middle, gq_near, gq_core, gq_chip],
        20 * tok_rows * width,
        name="input",
    )[0]
    for place in range(1, len(high)):
        grad_mod = doubled(grad_mod, beyond(grad_mod, 1 << place), high[place])
    grad_mods = grad_mod.reshape(data_count, 3 * width)
    if ringed:
        qkv_carried, qkv_taken, gq_chip = lax.optimization_barrier(
            (qkv_carried, qkv_taken, gq_chip)
        )
        sum_qkv = low(wide(qkv_keep[0]) + wide(qkv_taken) + wide(qkv_carried))
    else:
        sum_qkv = low(dp_sum_direct(qkv_sums[0]))
    mlp_out = wide(mlp_near[:tok_rows]) + wide(mlp_core[:tok_rows]) + wide(mlp_chip)
    result = low(middle + modulation[2:3] * mlp_out)
    final_ada = lax.dot_general(
        wide(embeds), grad_mods, (((0,), (0,)), ((), ())), precision=lax.Precision.HIGHEST
    )

    final_up, final_down = run(
        functools.partial(finish_mlp_kernel, data_count),
        [shaped(w_up.shape, jnp.float32), shaped(w_down.shape, jnp.float32)],
        [info] + mlp_blocks,
        0,
        scratch=[pltpu.VMEM((seq_count,) + block_shape, jnp.bfloat16)],
        name="finish_mlp",
    )
    qkv_far, final_up, grad_inputs = lax.optimization_barrier(
        (hop(sum_qkv, 2), final_up, grad_inputs)
    )
    qkv_blocks = [sum_qkv, qkv_far, hop(after(sum_qkv, qkv_far), 1), hop(qkv_far, 1)]
    final_qkv, final_out, final_gain = run(
        finish_qkv_kernel,
        [
            shaped(w_qkv.shape, jnp.float32),
            shaped(w_out.shape, jnp.float32),
            shaped((1, rows), jnp.float32),
        ],
        [info] + qkv_blocks + [w_qkv, wide(ln1_gain).reshape(1, rows)],
        0,
        scratch=[pltpu.VMEM((seq_count, rows, 4 * local_width), jnp.bfloat16)],
        name="finish_qkv",
    )
    return (
        result,
        grad_inputs,
        final_gain.reshape(-1),
        final_qkv,
        final_out,
        final_ada,
        final_up,
        final_down,
    )


def solution(mesh):
    placed = (
        P(("dp", "seq"), None),
        P("dp"),
        P("dp", None),
        P("dp", None),
        P("dp", None),
        P("dp", None),
        P("dp", None),
        P(("dp", "seq"), None),
        P("dp", None),
        P("dp"),
    )
    return jax.shard_map(
        body,
        mesh=mesh,
        in_specs=placed,
        out_specs=(
            P(("dp", "seq"), None),
            P(("dp", "seq"), None),
            P("dp"),
            P("dp", None),
            P("dp", None),
            P("dp", None),
            P("dp", None),
            P("dp", None),
        ),
        check_vma=False,
    )
```

```python
import functools
import math

import jax
import jax.numpy as jnp
from jax import lax
from jax.experimental import pallas as pl
from jax.experimental.pallas import tpu as pltpu
from jax.sharding import PartitionSpec as P

HEADS = 12
HEAD_DIM = 64

eps = 1e-05

MASKS = (0, 2, 1, 3)


def time_table(time_steps, model_width):
    half_dim = model_width // 2
    frequency = jnp.exp(-math.log(10000.0) * jnp.arange(half_dim, dtype=jnp.float32) / half_dim)
    angles = time_steps[:, None] * frequency[None, :]
    return jnp.concatenate([jnp.cos(angles), jnp.sin(angles)], axis=1)


def low(values_in):
    return values_in.astype(jnp.bfloat16)


def wide(values_in):
    return values_in.astype(jnp.float32)


HEAD_TILE = 128
COST = 1.0
VMEM_GRANT = 16 * 1024 * 1024
MASK_FILL = -1e30
GELU_IN = math.sqrt(2.0 / math.pi)
GELU_CUBE = 0.044715


def rope_tables(positions):
    half_dim = HEAD_DIM // 2
    column = jnp.arange(2 * HEAD_DIM, dtype=jnp.int32)
    frequency = jnp.exp(
        -math.log(10000.0) * 2.0 * (column % half_dim).astype(jnp.float32) / HEAD_DIM
    )
    angles = positions.astype(jnp.float32)[:, None] * frequency[None, :]
    sign = jnp.where(column % HEAD_DIM < half_dim, -1.0, 1.0)
    return (jnp.cos(angles), jnp.sin(angles) * sign[None, :])


def dot_nn(left, right):
    return lax.dot_general(
        left, right, (((1,), (0,)), ((), ())), preferred_element_type=jnp.float32
    )


def dot_nt(left, right):
    return lax.dot_general(
        left, right, (((1,), (1,)), ((), ())), preferred_element_type=jnp.float32
    )


def dot_tn(left, right):
    return lax.dot_general(
        left, right, (((0,), (0,)), ((), ())), preferred_element_type=jnp.float32
    )


def norm_rows(values_in):
    average = jnp.mean(values_in, axis=-1, keepdims=True)
    centred = values_in - average
    variance = jnp.mean(centred * centred, axis=-1, keepdims=True)
    scaling = lax.rsqrt(variance + eps)
    return (centred * scaling, scaling)


def swap_halves(values_in):
    column = lax.broadcasted_iota(jnp.int32, values_in.shape, 1)
    ahead = pltpu.roll(values_in, HEAD_TILE - HEAD_DIM // 2, 1)
    behind = pltpu.roll(values_in, HEAD_DIM // 2, 1)
    return jnp.where(column % HEAD_DIM < HEAD_DIM // 2, ahead, behind)


def whole(count):
    return [pl.BlockSpec(memory_space=pltpu.VMEM)] * count


def scalars():
    return [pl.BlockSpec(memory_space=pltpu.SMEM)]


def run(kernel, out_shapes, args, flops, scratch=(), name=None):
    nbytes = sum(a.size * a.dtype.itemsize for a in args)
    nbytes += sum(math.prod(o.shape) * o.dtype.itemsize for o in out_shapes)
    call = pl.pallas_call(
        kernel,
        out_shape=out_shapes,
        in_specs=scalars() + whole(len(args) - 1),
        out_specs=whole(len(out_shapes)),
        scratch_shapes=list(scratch),
        cost_estimate=pl.CostEstimate(flops=int(flops * COST), bytes_accessed=int(nbytes * COST), transcendentals=0),
        compiler_params=pltpu.CompilerParams(vmem_limit_bytes=VMEM_GRANT),
        name=name,
    )
    return call(*args)


def shaped(shape, kind=jnp.bfloat16):
    return jax.ShapeDtypeStruct(shape, kind)


FIRST, OWNER, PLACE = 2, 6, 10


def block_segment(info, block, rows, axis):
    shape = (rows, 1) if axis == 0 else (1, rows)
    position = info[FIRST + block] + lax.broadcasted_iota(jnp.int32, shape, axis)
    return (position >= info[0]).astype(jnp.int32) + (position >= info[1]).astype(jnp.int32)


def place_rows(info, chunks, first, rows, dest):
    for index, chunk in enumerate(chunks):
        at = pl.multiple_of(info[PLACE + index] * rows, rows)
        dest[pl.ds(at, rows), : chunk.shape[1]] = chunk[first : first + rows, :]


def store_blocks(info, sums_ref, outs):
    if len(outs) == 1:
        outs[0][...] = sums_ref[...]
    else:
        for index, dest in enumerate(outs):
            dest[...] = sums_ref[info[PLACE + index]]


def first_part_kernel(info, qkv_ref, out_ref, dest):
    span = dest.shape[1] // 4
    for part in range(4):

        @pl.when(info[0] == part)
        def _():
            for third in range(3):
                at = (third * 4 + part) * span
                dest[:, third * span : (third + 1) * span] = qkv_ref[:, at : at + span]
            dest[:, 3 * span :] = out_ref[:, part * span : (part + 1) * span]


def modulation_kernel(info, embed_ref, weight_ref, out_ref):
    width = out_ref.shape[2]
    for third in range(3):
        part = dot_nn(embed_ref[...], weight_ref[:, third * width : (third + 1) * width])
        for group in range(out_ref.shape[0]):
            out_ref[group, third : third + 1, :] = part[group : group + 1, :]


def second_part_kernel(count, info, up_ref, down_ref, dest):
    rows = up_ref.shape[0]
    piece = down_ref.shape[0] // 4
    for part in range(4):

        @pl.when(info[0] == part)
        def _():
            for index in range(count):
                at = (index * 4 + part) * piece
                dest[:rows, index * piece : (index + 1) * piece] = up_ref[:, at : at + piece]
            dest[rows:, :] = down_ref[part * piece : (part + 1) * piece, :]


def qkv_kernel(heads, count, info, *refs):
    gain, cos_ref, sin_ref = refs[:3]
    tok_refs = refs[3:7]
    chunks = refs[7 : 7 + count]
    hidden_ref, weight_ref, own_ref, q_ref, k_ref, v_ref, all_ref = refs[7 + count :]
    rows, width = tok_refs[0].shape
    lw = heads * HEAD_DIM
    place_rows(info, chunks, 0, width // count, weight_ref)
    own_ref[...] = weight_ref[:, 3 * lw : 4 * lw]
    gain_row = gain[...]
    for block in range(4):
        all_ref[block] = tok_refs[block][...]

    @pl.loop(0, 4)
    def _(block):
        normed, _ = norm_rows(wide(all_ref[block]))
        hidden = low(normed * gain_row)
        here = pl.ds(pl.multiple_of(block * rows, rows), rows)
        hidden_ref[here, :] = hidden
        both = dot_nn(hidden, weight_ref[:, : 2 * lw])
        last = dot_nn(hidden, weight_ref[:, 2 * lw : 2 * lw + 2 * HEAD_TILE])
        cos_part = cos_ref[here, :]
        sin_part = sin_ref[here, :]
        turned = []
        for tile in range(2 * lw // HEAD_TILE):
            piece = both[:, tile * HEAD_TILE : (tile + 1) * HEAD_TILE]
            turned.append(piece * cos_part + swap_halves(piece) * sin_part)
        column = lax.broadcasted_iota(jnp.int32, (rows, HEAD_TILE), 1)
        segment = block_segment(info, block, rows, 0)
        first_fill = jnp.where(segment == 1, 0.0, MASK_FILL)
        second_fill = jnp.where(segment == 2, 0.0, MASK_FILL)
        q_mark = jnp.where(
            column == HEAD_DIM, first_fill, jnp.where(column == HEAD_DIM + 1, second_fill, 0.0)
        )
        first_mark = jnp.where(segment == 1, 1.0, 0.0)
        second_mark = jnp.where(segment == 2, 1.0, 0.0)
        k_mark = jnp.where(
            column == HEAD_DIM,
            first_mark,
            jnp.where(
                column == HEAD_DIM + 1, second_mark, jnp.where(column < HEAD_DIM + 5, 1.0, 0.0)
            ),
        )
        v_mark = jnp.where(column < HEAD_DIM + 2, 1.0, 0.0)
        for head in range(heads):
            q_at, k_at = head, heads + head
            q_tile = turned[q_at // 2]
            k_tile = turned[k_at // 2]
            v_tile = last[:, HEAD_TILE * (head // 2) : HEAD_TILE * (head // 2 + 1)]
            if q_at % 2:
                q_tile = pltpu.roll(q_tile, HEAD_DIM, 1)
            if k_at % 2:
                k_tile = pltpu.roll(k_tile, HEAD_DIM, 1)
            if head % 2:
                v_tile = pltpu.roll(v_tile, HEAD_DIM, 1)
            there = slice(head * HEAD_TILE, (head + 1) * HEAD_TILE)
            q_ref[here, there] = low(jnp.where(column < HEAD_DIM, q_tile * 0.125, q_mark))
            k_ref[here, there] = low(jnp.where(column < HEAD_DIM, k_tile, k_mark))
            v_ref[here, there] = low(jnp.where(column < HEAD_DIM, v_tile, v_mark))


def attend_kernel(heads, rows, info, q_ref, k_ref, v_ref, *outs):
    att_refs = outs[:4]
    stat_ref, all_ref = outs[4:]
    column = lax.broadcasted_iota(jnp.int32, (rows, HEAD_TILE), 1)

    @pl.loop(0, 4)
    def _(block):
        here = pl.ds(pl.multiple_of(block * rows, rows), rows)
        results = []
        for head in range(heads):
            there = slice(head * HEAD_TILE, (head + 1) * HEAD_TILE)
            queries = q_ref[here, there]
            scores = dot_nt(queries, k_ref[:, there])
            row_max = jnp.max(scores, axis=-1, keepdims=True)
            weights = low(jnp.exp(scores - row_max))
            summed = dot_nn(weights, v_ref[:, there])
            row_sum = summed[:, HEAD_DIM : HEAD_DIM + 1]
            results.append(summed / row_sum)
            minus = -(row_max + jnp.log(row_sum))
            first = low(minus)
            second = low(minus - wide(first))
            third = low(minus - wide(first) - wide(second))
            stat_ref[here, there] = jnp.where(
                column == HEAD_DIM + 2,
                first,
                jnp.where(
                    column == HEAD_DIM + 3, second, jnp.where(column == HEAD_DIM + 4, third, queries)
                ),
            )
        for head in range(0, heads, 2):
            if head + 1 < heads:
                both = jnp.where(
                    column < HEAD_DIM, results[head], pltpu.roll(results[head + 1], HEAD_DIM, 1)
                )
                all_ref[here, head * HEAD_DIM : (head + 2) * HEAD_DIM] = low(both)
            else:
                all_ref[here, head * HEAD_DIM :] = low(results[head][:, :HEAD_DIM])

    for block in range(4):
        att_refs[block][...] = all_ref[block * rows : (block + 1) * rows, :]


def natural(info, blocks, dest):
    for block in range(4):
        dest[info[OWNER + block]] = blocks[block][...]


def middle_kernel(info, tok_ref, mod_ref, *refs):
    middle_ref, hidden_ref, att_ref, weight_ref = refs[8:]
    natural(info, refs[:4], weight_ref)
    natural(info, refs[4:8], att_ref)
    span = weight_ref.shape[2]
    for columns in range(4):
        there = slice(columns * span, (columns + 1) * span)
        total = wide(tok_ref[:, there])
        for part in range(4):
            total = total + dot_nn(
                att_ref[part], weight_ref[columns, part * span : (part + 1) * span, :]
            )
        middle_ref[:, there] = total
    normed, _ = norm_rows(middle_ref[...])
    hidden_ref[...] = low(normed * (1.0 + mod_ref[0:1, :]) + mod_ref[1:2, :])


def act_grad_kernel(count, skip, info, mod_ref, *refs):
    dy_refs = refs[:4]
    chunks = refs[4 : 4 + count]
    mlp_ref, act_ref, weight_ref = refs[4 + count :]
    rows = dy_refs[0].shape[0]
    place_rows(info, chunks, skip, weight_ref.shape[0] // count, weight_ref)
    gate = mod_ref[2:3, :]
    for block in range(4):
        here = slice(block * rows, (block + 1) * rows)
        mlp_ref[here, :] = low(gate * wide(dy_refs[block][...]))

    @pl.loop(0, 2)
    def _(turn):
        here = pl.ds(pl.multiple_of(turn * 2 * rows, 2 * rows), 2 * rows)
        act_ref[here, :] = low(dot_nt(mlp_ref[here, :], weight_ref[...]))


def forward_kernel(count, info, act_grad, *refs):
    hid_refs = refs[:4]
    chunks = refs[4 : 4 + count]
    act_ref, pre_ref, near_ref, far_ref, weight_ref, all_ref = refs[4 + count :]
    rows = hid_refs[0].shape[0]
    place_rows(info, chunks, 0, weight_ref.shape[0] // count, weight_ref)
    for block in range(4):
        all_ref[block] = hid_refs[block][...]

    @pl.loop(0, 2)
    def _(turn):
        there = pl.ds(pl.multiple_of(turn * rows, rows), rows)
        for half, dest in ((1, far_ref), (0, near_ref)):
            here = pl.ds(pl.multiple_of((2 * half + turn) * rows, rows), rows)
            pre = dot_nn(all_ref[2 * half + turn], weight_ref[...])
            square = pre * pre
            inner = jnp.tanh(GELU_IN * (pre + GELU_CUBE * (square * pre)))
            side = 0.5 * (1.0 + inner)
            act_ref[here, :] = low(pre * side)
            slope = side + 0.5 * pre * (1.0 - inner * inner) * (
                GELU_IN * (1.0 + 3.0 * GELU_CUBE * square)
            )
            grad_pre = low(wide(act_grad[here, :]) * slope)
            pre_ref[here, :] = grad_pre
            dest[there, :] = low(dot_nt(grad_pre, weight_ref[...]))


def weight_grad_kernel(count, info, act_ref, mlp_ref, pre_ref, *refs):
    hid_refs = refs[:4]
    outs, sums_ref = refs[4:-1], refs[-1]
    rows = hid_refs[0].shape[0]
    per = act_ref.shape[1] // count
    up = dot_tn(hid_refs[0][...], pre_ref[:rows, :])
    for block in range(1, 4):
        up = up + dot_tn(hid_refs[block][...], pre_ref[block * rows : (block + 1) * rows, :])
    for index in range(count):
        sums_ref[index, :per, :] = low(up[index * per : (index + 1) * per, :])
    down = dot_tn(act_ref[...], mlp_ref[...])
    for index in range(count):
        sums_ref[index, per:, :] = low(down[index * per : (index + 1) * per, :])
    store_blocks(info, sums_ref, outs)


def down_kernel(count, skip, info, act_ref, *refs):
    dy_refs = refs[:4]
    chunks = refs[4 : 4 + count]
    near_ref, far_ref, gate_ref, weight_ref = refs[4 + count :]
    rows = dy_refs[0].shape[0]
    place_rows(info, chunks, skip, weight_ref.shape[0] // count, weight_ref)
    total = jnp.zeros(gate_ref.shape, jnp.float32)
    for block in (2, 3, 1, 0):
        here = slice(block * rows, (block + 1) * rows)
        part = dot_nn(act_ref[here, :], weight_ref[...])
        total = total + jnp.sum(wide(dy_refs[block][...]) * part, axis=0, keepdims=True)
        dest = near_ref if block < 2 else far_ref
        dest[(block % 2) * rows : (block % 2 + 1) * rows, :] = low(part)
    gate_ref[...] = total


def branch_kernel(info, mod_ref, middle_ref, dy_ref, own_ref, core_ref, chip_ref, gate_ref, *refs):
    mid_ref, branch_ref, sums_ref = refs[4:7]
    att_refs = (refs[7], refs[8], None, refs[9])
    weight_ref, parts_ref = refs[10:]
    natural(info, refs[:4], weight_ref)
    rows, width = dy_ref.shape
    grad_hidden = wide(own_ref[:rows, :]) + wide(core_ref[:rows, :]) + wide(chip_ref[...])
    normed, scaling = norm_rows(middle_ref[...])
    sums_ref[0:1, :] = jnp.sum(grad_hidden * normed, axis=0, keepdims=True)
    sums_ref[1:2, :] = jnp.sum(grad_hidden, axis=0, keepdims=True)
    sums_ref[2:3, :] = gate_ref[...]
    grad_normed = grad_hidden * (1.0 + mod_ref[0:1, :])
    first_mean = jnp.mean(grad_normed, axis=-1, keepdims=True)
    second_mean = jnp.mean(grad_normed * normed, axis=-1, keepdims=True)
    mid_ref[...] = wide(dy_ref[...]) + scaling * (grad_normed - first_mean - normed * second_mean)
    span = weight_ref.shape[2]
    branch_ref[:, :width] = low(mid_ref[...])
    branch_ref[:, width + span :] = jnp.zeros(
        (rows, branch_ref.shape[1] - width - span), jnp.bfloat16
    )
    for columns in range(4):
        parts_ref[columns] = low(mid_ref[:, columns * span : (columns + 1) * span])
    for block, dest in enumerate(att_refs):
        at = pl.multiple_of(info[OWNER + block] * span, HEAD_DIM)
        total = dot_nt(parts_ref[0], weight_ref[0, pl.ds(at, span), :])
        for columns in range(1, 4):
            total = total + dot_nt(parts_ref[columns], weight_ref[columns, pl.ds(at, span), :])
        if dest is None:
            branch_ref[:, width : width + span] = low(total)
        else:
            dest[...] = low(total)


def out_grad_kernel(info, att_ref, core_att_ref, branch_ref, core_branch_ref, near_ref, parts_ref):
    span = att_ref.shape[2]
    for columns in range(4):
        here = slice(columns * span, (columns + 1) * span)
        parts_ref[columns] = branch_ref[:, here]
        parts_ref[4 + columns] = core_branch_ref[:, here]
    for block in range(2):
        owner = info[OWNER + block]
        branch, core_branch = parts_ref[owner], parts_ref[4 + owner]
        for part in range(4):
            near_ref[block, part * span : (part + 1) * span, :] = low(
                dot_tn(att_ref[part], branch) + dot_tn(core_att_ref[part], core_branch)
            )


def attend_back_kernel(heads, rows, info, cos_ref, sin_ref, q_ref, k_ref, v_ref, *refs):
    att = refs[:4]
    span = heads * HEAD_DIM
    width = 4 * span
    grads = ((refs[4], 0), (refs[5], 0), (refs[6], width), (refs[7], 0))
    out_ref, gx_ref, turn_ref, dq_ref, dk_ref, dv_ref = refs[8:]
    column = lax.broadcasted_iota(jnp.int32, (rows, HEAD_TILE), 1)

    def tile_of(ref, base, head):
        at = base + HEAD_TILE * (head // 2)
        if base or head % 2 or head + 1 < heads:
            tile = wide(ref[:, at : at + HEAD_TILE])
            return pltpu.roll(tile, HEAD_DIM, 1) if head % 2 else tile
        last = wide(ref[:, at:])
        return jnp.concatenate([last, jnp.zeros_like(last)], axis=1)

    for head in range(heads):
        there = slice(head * HEAD_TILE, (head + 1) * HEAD_TILE)
        for block in range(4):
            here = slice(block * rows, (block + 1) * rows)
            grad = jnp.where(column < HEAD_DIM, tile_of(*grads[block], head), 0.0)
            minus = -jnp.sum(grad * tile_of(att[block], 0, head), axis=-1, keepdims=True)
            first = wide(low(minus))
            gx_ref[here, :] = low(
                jnp.where(
                    column == HEAD_DIM,
                    first,
                    jnp.where(column == HEAD_DIM + 1, minus - first, grad),
                )
            )
        for block in range(4):
            here = slice(block * rows, (block + 1) * rows)
            keys = k_ref[here, there]
            probs = jnp.exp(dot_nt(keys, q_ref[:, there]))
            prob_grad = dot_nt(v_ref[here, there], gx_ref[...])
            score_grad = low(probs * prob_grad)
            dv_ref[here, there] = dot_nn(low(probs), gx_ref[...])
            dk_ref[here, there] = dot_nn(score_grad, q_ref[:, there])
            part = dot_tn(keys, score_grad)
            if block == 0:
                turn_ref[...] = part
            else:
                turn_ref[...] += part
        dq_ref[:, there] = jnp.transpose(turn_ref[...]) * 0.125

    for block in range(4):
        here = slice(block * rows, (block + 1) * rows)
        heads_of = [dq_ref[here, h * HEAD_TILE : (h + 1) * HEAD_TILE] for h in range(heads)]
        heads_of += [dk_ref[here, h * HEAD_TILE : (h + 1) * HEAD_TILE] for h in range(heads)]
        heads_of += [dv_ref[here, h * HEAD_TILE : (h + 1) * HEAD_TILE] for h in range(heads)]
        heads_of.append(jnp.zeros((rows, HEAD_TILE), jnp.float32))
        for tile in range((3 * heads + 1) // 2):
            both = jnp.where(
                column < HEAD_DIM,
                heads_of[2 * tile],
                pltpu.roll(heads_of[2 * tile + 1], HEAD_DIM, 1),
            )
            if tile < heads:
                both = both * cos_ref[here, :] - swap_halves(both) * sin_ref[here, :]
            out_ref[here, tile * HEAD_TILE : (tile + 1) * HEAD_TILE] = low(both)


def hidden_grad_kernel(rows, info, grad_ref, weight_ref, near_ref, far_ref):
    span = grad_ref.shape[1]

    @pl.loop(0, 2)
    def _(turn):
        there = pl.ds(pl.multiple_of(turn * rows, rows), rows)
        for half, dest in ((1, far_ref), (0, near_ref)):
            here = pl.ds(pl.multiple_of((2 * half + turn) * rows, rows), rows)
            dest[there, :] = low(dot_nt(grad_ref[here, :], weight_ref[:, :span]))


def qkv_grad_kernel(count, used, info, hidden_ref, grad_ref, near_ref, chip_ref, *refs):
    outs, sums_ref = refs[:-1], refs[-1]
    total = dot_tn(hidden_ref[...], grad_ref[...])
    out_total = wide(near_ref[0]) + wide(chip_ref[0])
    per = total.shape[0] // count
    for index in range(count):
        here = slice(index * per, (index + 1) * per)
        sums_ref[index, :, :used] = low(total[here, :used])
        sums_ref[index, :, used:] = low(out_total[here, :])
    store_blocks(info, sums_ref, outs)


def input_kernel(info, gain, tok_ref, mid_ref, own_ref, core_ref, chip_ref, out_ref):
    rows = tok_ref.shape[0]
    grad_hidden = wide(own_ref[:rows, :]) + wide(core_ref[:rows, :]) + wide(chip_ref[:rows, :])
    normed, scaling = norm_rows(wide(tok_ref[...]))
    grad_normed = grad_hidden * gain[...]
    first_mean = jnp.mean(grad_normed, axis=-1, keepdims=True)
    second_mean = jnp.mean(grad_normed * normed, axis=-1, keepdims=True)
    out_ref[...] = low(
        mid_ref[...] + scaling * (grad_normed - first_mean - normed * second_mean)
    )


def finish_mlp_kernel(count, info, *refs):
    blocks = refs[:4]
    up_ref, down_ref, all_ref = refs[4:]
    natural(info, blocks, all_ref)
    rows = up_ref.shape[0]
    piece = down_ref.shape[0] // 4
    for part in range(4):
        value = wide(all_ref[part])
        for index in range(count):
            at = (index * 4 + part) * piece
            up_ref[:, at : at + piece] = value[:rows, index * piece : (index + 1) * piece]
        down_ref[part * piece : (part + 1) * piece, :] = value[rows:, :]


def finish_qkv_kernel(info, *refs):
    blocks = refs[:4]
    weight_ref, gain_ref, out_ref, own_ref, sums_ref, all_ref = refs[4:]
    natural(info, blocks, all_ref)
    span = all_ref.shape[2] // 4
    total = jnp.zeros((out_ref.shape[0], 1), jnp.float32)
    for part in range(4):
        value = wide(all_ref[part])
        for third in range(3):
            at = (third * 4 + part) * span
            piece = value[:, third * span : (third + 1) * span]
            total = total + jnp.sum(
                wide(weight_ref[:, at : at + span]) * piece, axis=1, keepdims=True
            )
            out_ref[:, at : at + span] = piece
        own_ref[:, part * span : (part + 1) * span] = value[:, 3 * span :]
    turned = jnp.transpose(jnp.broadcast_to(total, (total.shape[0], HEAD_TILE)))
    sums_ref[...] = turned[0:1, :] / gain_ref[...]


def hop(values_in, mask):
    return lax.ppermute(values_in, "seq", [(i, i ^ mask) for i in range(lax.axis_size("seq"))])


def ring_of(count):
    return [0] + list(range(1, count, 2)) + [i for i in range(count - 1, 0, -1) if i % 2 == 0]


def ring_next(data_count):
    outer = data_count // 2
    ring = ring_of(outer)
    follow = {ring[i]: ring[(i + 1) % outer] for i in range(outer)}
    return [(z * 2 + y, follow[z] * 2 + y) for z in range(outer) for y in range(2)]


def pair(values_in):
    return lax.ppermute(values_in, "dp", [(i, i ^ 1) for i in range(lax.axis_size("dp"))])


def dp_sum_direct(blocks):
    data_count = lax.axis_size("dp")
    if data_count != 8:
        return wide(lax.psum_scatter(blocks, "dp", scatter_dimension=0, tiled=False))
    return jnp.sum(wide(lax.all_to_all(blocks, "dp", 0, 0, tiled=True)), axis=0)


def after(values_in, *earlier):
    return lax.optimization_barrier((values_in,) + earlier)[0]


def onward(values_in):
    return lax.ppermute(values_in, "dp", ring_next(lax.axis_size("dp")))


def kernel_info(layout, rank, index, tok_rows):
    data_count = lax.axis_size("dp")
    column = jnp.arange(PLACE + 8, dtype=jnp.int32)

    def owner(block):
        return rank ^ ((block & 1) * 2 + (block >> 1))

    values = jnp.where(column == 0, layout[0, 0], layout[0, 1])
    values = jnp.where(column >= FIRST, owner(column - FIRST) * tok_rows, values)
    values = jnp.where(column >= OWNER, owner(column - OWNER), values)
    if data_count == 8:
        step = column - PLACE
        at = index >> 1
        at = ((at ^ (at >> 1)) - (step >> 1)) & 3
        place = (at ^ (at >> 1)) * 2 + ((index + step) & 1)
    else:
        place = jnp.zeros_like(column)
    return jnp.where(column >= PLACE, place, values)


def gathered_whole(chunk, sizes):
    gathered = lax.all_gather(chunk, "dp", axis=0)
    parts = []
    at = 0
    for size in sizes:
        parts.append(gathered[:, at : at + size].reshape(-1, chunk.shape[1]))
        at += size
    return [jnp.concatenate(parts, axis=0)]


def four(values_in):
    chip = hop(values_in, 2)
    return [values_in, chip, hop(values_in, 1), hop(chip, 1)]


def beyond(values_in, mask):
    return lax.ppermute(values_in, "dp", [(i, i ^ mask) for i in range(lax.axis_size("dp"))])


def doubled(parts, other, bit):
    return jnp.where(
        bit, jnp.concatenate([other, parts], axis=0), jnp.concatenate([parts, other], axis=0)
    )


def body(tokens, ln1_gain, w_qkv, w_out, w_ada, w_up, w_down, out_grad, layout, timestep):
    seq_count = lax.axis_size("seq")
    data_count = lax.axis_size("dp")
    ringed = data_count == 8
    rank = lax.axis_index("seq")
    index = lax.axis_index("dp")
    high = [(index >> place) & 1 == 1 for place in range(data_count.bit_length() - 1)]
    tokens, rank, index, high = lax.optimization_barrier((tokens, rank, index, high))
    tok_rows, width = tokens.shape
    group_rows = tok_rows * seq_count
    heads_local = HEADS // seq_count
    local_width = heads_local * HEAD_DIM
    head_columns = heads_local * HEAD_TILE
    padded = (3 * heads_local + 1) // 2 * HEAD_TILE
    rows = w_qkv.shape[0]
    hidden = w_up.shape[1] // seq_count
    down_piece = w_down.shape[0] // seq_count
    rank_word = rank.reshape(1).astype(jnp.int32)

    tok_chip = hop(tokens, 2)
    first = run(
        first_part_kernel,
        [shaped((rows, 4 * local_width))],
        [rank_word, w_qkv, w_out],
        0,
        name="first_part",
    )[0]
    if ringed:
        held = [first, onward(first)]
        beside = [pair(first)]
        held[1], beside[0], tokens = lax.optimization_barrier((held[1], beside[0], tokens))
        held.append(onward(held[1]))
        beside.append(pair(held[1]))
        tok_core = hop(tokens, 1)
        held[2], beside[1], tok_chip, tok_core = lax.optimization_barrier(
            (held[2], beside[1], tok_chip, tok_core)
        )
        held.append(onward(held[2]))
        beside.append(pair(held[2]))
        tok_both = hop(tok_chip, 1)
    else:
        tok_core, tok_both = hop(tokens, 1), hop(tok_chip, 1)
    tok_blocks = [tokens, tok_chip, tok_core, tok_both]

    embed = low(time_table(wide(timestep), width))
    sent = jnp.stack(
        [embed.reshape(data_count, rows), jnp.broadcast_to(ln1_gain, (data_count, rows))], axis=1
    )
    taken = lax.all_to_all(sent, "dp", 0, 0, tiled=True)
    embeds = taken[:, 0]
    gain = wide(taken[:, 1].reshape(1, width))
    mod_parts = run(
        modulation_kernel,
        [shaped((data_count, 3, width), jnp.float32)],
        [rank_word, after(embeds, held[2]) if ringed else embeds, w_ada],
        2 * data_count * rows * w_ada.shape[1],
        name="modulation",
    )[0]

    def halves(parts, place):
        half = parts.shape[0] // 2
        kept = jnp.where(high[place], parts[half:], parts[:half])
        given = jnp.where(high[place], parts[:half], parts[half:])
        return kept, beyond(given, 1 << place)

    modulation = mod_parts
    for place in range(len(high) - 1, 2, -1):
        modulation = sum(halves(modulation, place))

    info = kernel_info(layout, rank, index, tok_rows)
    starts = info[FIRST:OWNER]

    second = run(
        functools.partial(second_part_kernel, data_count),
        [shaped((rows + down_piece, width))],
        [rank_word, w_up, w_down],
        0,
        name="second_part",
    )[0]
    if ringed:
        dy_core = hop(after(out_grad, held[2]), 1)
        held[3], beside[2], second, dy_core, *rest = lax.optimization_barrier(
            (
                held[3],
                beside[2],
                second,
                dy_core,
                gain,
                info,
                tok_blocks,
            )
        )
        gain, info, tok_blocks = rest
        modulation = after(modulation, held[3])
        beside.append(pair(held[3]))
        first_chunks = [part for both in zip(held, beside) for part in both]
        second = after(second, beside[3])
        held = [second, onward(second)]
        beside = [pair(second)]
        dy_chip = hop(after(out_grad, held[0]), 2)
    else:
        first_chunks = gathered_whole(first, [rows])
        second_chunks = gathered_whole(second, [rows, down_piece])
        dy_chip, dy_core = hop(out_grad, 2), hop(out_grad, 1)
    if ringed:
        starts = after(starts, first_chunks[6])
    positions = (starts[:, None] + jnp.arange(tok_rows, dtype=jnp.int32)[None, :]).reshape(-1)
    cos_table, sin_table = rope_tables(positions)
    kept, sums = halves(modulation, 2)
    if ringed:
        gain, sums = lax.optimization_barrier((gain, sums))
    kept, sums = halves(kept + sums, 1)
    count = len(first_chunks)
    up_rows = rows * (data_count // count)

    hidden_one, qkv_weight, own_out, queries, keys, values = run(
        functools.partial(qkv_kernel, heads_local, count),
        [
            shaped((group_rows, width)),
            shaped((width, 4 * local_width)),
            shaped((width, local_width)),
            shaped((group_rows, head_columns)),
            shaped((group_rows, head_columns)),
            shaped((group_rows, head_columns)),
        ],
        [info, gain, cos_table, sin_table] + tok_blocks + first_chunks,
        2 * group_rows * width * padded,
        scratch=[pltpu.VMEM((seq_count, tok_rows, width), jnp.bfloat16)],
        name="qkv",
    )
    if ringed:
        queries, own_out, held[1], beside[0], sums = lax.optimization_barrier(
            (queries, own_out, held[1], beside[0], sums)
        )
        beside.append(pair(held[1]))
        held.append(onward(held[1]))
    kept, sums = halves(kept + sums, 0)
    chip_out = hop(own_out, 2)
    core_out = hop(own_out, 1)
    *att_parts, marked = run(
        functools.partial(attend_kernel, heads_local, tok_rows),
        [shaped((tok_rows, local_width))] * 4 + [shaped((group_rows, head_columns))],
        [info, queries, keys, values],
        4 * group_rows * group_rows * head_columns,
        scratch=[pltpu.VMEM((group_rows, local_width), jnp.bfloat16)],
        name="attend",
    )
    if ringed:
        att_parts, held[2], beside[1], chip_out, core_out, dy_chip, sums = lax.optimization_barrier(
            (att_parts, held[2], beside[1], chip_out, core_out, dy_chip, sums)
        )
        beside.append(pair(held[2]))
        held.append(onward(held[2]))
    modulation = (kept + sums)[0]
    att_own = [att_parts[0]] + [hop(att_parts[j], MASKS[j]) for j in (1, 2, 3)]
    out_blocks = [own_out, chip_out, core_out, hop(after(chip_out, att_own[2]), 1)]
    if ringed:
        att_own, held[3], beside[2] = lax.optimization_barrier((att_own, held[3], beside[2]))
    middle, hidden_two, att_ordered = run(
        middle_kernel,
        [
            shaped((tok_rows, width), jnp.float32),
            shaped((tok_rows, width)),
            shaped((seq_count, tok_rows, local_width)),
        ],
        [info, tokens, modulation] + out_blocks + att_own,
        2 * tok_rows * width * width,
        scratch=[pltpu.VMEM((seq_count, width, local_width), jnp.bfloat16)],
        name="middle",
    )

    chip_hidden = hop(hidden_two, 2)
    if ringed:
        beside.append(pair(held[3]))
        second_chunks = [part for both in zip(held, beside) for part in both]
    dy_blocks = [out_grad, dy_chip, dy_core, hop(after(dy_chip, hidden_two), 1)]
    grad_mlp, grad_act = run(
        functools.partial(act_grad_kernel, count, up_rows),
        [shaped((group_rows, width)), shaped((group_rows, hidden))],
        [info, modulation] + dy_blocks + second_chunks,
        2 * group_rows * width * hidden,
        scratch=[pltpu.VMEM((hidden, width), jnp.bfloat16)],
        name="act_grad",
    )
    hid_blocks = [
        hidden_two,
        chip_hidden,
        hop(hidden_two, 1),
        hop(after(chip_hidden, grad_act), 1),
    ]
    half = shaped((group_rows // 2, width))
    activated, grad_pre, gh_near, gh_far = run(
        functools.partial(forward_kernel, count),
        [shaped((group_rows, hidden)), shaped((group_rows, hidden)), half, half],
        [info, grad_act] + hid_blocks + second_chunks,
        4 * group_rows * width * hidden,
        scratch=[
            pltpu.VMEM((width, hidden), jnp.bfloat16),
            pltpu.VMEM((seq_count, tok_rows, width), jnp.bfloat16),
        ],
        name="forward",
    )
    block_shape = (rows + down_piece, width)
    grad_weights = run(
        functools.partial(weight_grad_kernel, data_count),
        [shaped(block_shape)] * count if ringed else [shaped((data_count,) + block_shape)],
        [info, activated, grad_mlp, grad_pre] + hid_blocks,
        4 * group_rows * width * hidden,
        scratch=[pltpu.VMEM((data_count,) + block_shape, jnp.bfloat16)],
        name="weight_grad",
    )
    gh_core = hop(gh_far, 1)
    gh_core, grad_weights = lax.optimization_barrier((gh_core, grad_weights))
    gh_send = low(wide(gh_near[tok_rows:]) + wide(gh_core[tok_rows:]))
    gh_chip = hop(gh_send, 2)
    mlp_near, mlp_far, grad_gate = run(
        functools.partial(down_kernel, count, up_rows),
        [half, half, shaped((1, width), jnp.float32)],
        [info, after(activated, gh_send)] + dy_blocks + second_chunks,
        2 * group_rows * width * hidden,
        scratch=[pltpu.VMEM((hidden, width), jnp.bfloat16)],
        name="down",
    )
    if ringed:
        mlp_keep, mlp_give = list(grad_weights[0::2]), list(grad_weights[1::2])
        mlp_taken = pair(after(mlp_give[1], gh_send))
        gh_chip, mlp_far, mlp_taken = lax.optimization_barrier((gh_chip, mlp_far, mlp_taken))
        mlp_ring = low(wide(mlp_keep[1]) + wide(mlp_taken))
        gh_chip, mlp_ring = lax.optimization_barrier((gh_chip, mlp_ring))
        mlp_carried = onward(mlp_ring)
        mlp_taken = pair(after(mlp_give[2], mlp_ring))
    else:
        gh_chip, mlp_far = lax.optimization_barrier((gh_chip, mlp_far))
    mlp_core = hop(mlp_far, 1)
    core_attended = hop(after(att_ordered, gh_chip), 1)

    branch_columns = -(-(width + local_width) // HEAD_TILE) * HEAD_TILE
    grad_middle, branch, grad_mod, *grad_parts = run(
        branch_kernel,
        [
            shaped((tok_rows, width), jnp.float32),
            shaped((tok_rows, branch_columns)),
            shaped((3, width), jnp.float32),
        ]
        + [shaped((tok_rows, local_width))] * 3,
        [info, modulation, after(middle, mlp_near), out_grad, gh_near, gh_core, gh_chip]
        + [grad_gate]
        + out_blocks,
        2 * tok_rows * width * width,
        scratch=[
            pltpu.VMEM((seq_count, width, local_width), jnp.bfloat16),
            pltpu.VMEM((seq_count, tok_rows, local_width), jnp.bfloat16),
        ],
        name="branch",
    )
    grad_parts, mlp_core = lax.optimization_barrier((grad_parts, mlp_core))
    core_branch = hop(branch, 1)
    grad_att = [grad_parts[0], hop(grad_parts[1], 2), core_branch, hop(grad_parts[2], 3)]
    out_sums = run(
        out_grad_kernel,
        [shaped((2, width, local_width))],
        [info, att_ordered, core_attended, branch, core_branch],
        2 * tok_rows * width * width,
        scratch=[pltpu.VMEM((2 * seq_count, tok_rows, local_width), jnp.bfloat16)],
        name="out_grad",
    )[0]

    if ringed:
        del grad_att[2]
        grad_att, out_sums, mlp_taken, mlp_carried = lax.optimization_barrier(
            (grad_att, out_sums, mlp_taken, mlp_carried)
        )
        grad_att.insert(2, core_branch)
        mlp_ring = low(wide(mlp_keep[2]) + wide(mlp_taken) + wide(mlp_carried))
        mlp_carried = onward(mlp_ring)
        mlp_taken = pair(after(mlp_give[3], mlp_ring))
    out_chip = hop(out_sums[1:], 2)
    mod_core = hop(grad_mod, 1)
    grad_qkv = run(
        functools.partial(attend_back_kernel, heads_local, tok_rows),
        [shaped((group_rows, padded))],
        [info, cos_table, sin_table, marked, keys, values] + att_parts + grad_att,
        10 * group_rows * group_rows * head_columns,
        scratch=[
            pltpu.VMEM((group_rows, HEAD_TILE), jnp.bfloat16),
            pltpu.VMEM((HEAD_TILE, group_rows), jnp.float32),
            pltpu.VMEM((group_rows, head_columns), jnp.float32),
            pltpu.VMEM((group_rows, head_columns), jnp.float32),
            pltpu.VMEM((group_rows, head_columns), jnp.float32),
        ],
        name="attend_back",
    )[0]
    grad_qkv, out_chip, mod_core = lax.optimization_barrier((grad_qkv, out_chip, mod_core))
    grad_mod = grad_mod + mod_core
    mod_chip = hop(grad_mod, 2)
    mlp_send = low(wide(after(mlp_near[tok_rows:], grad_qkv)) + wide(mlp_core[tok_rows:]))
    mlp_chip = hop(mlp_send, 2)
    if ringed:
        grad_qkv, mlp_taken, mlp_carried = lax.optimization_barrier(
            (grad_qkv, mlp_taken, mlp_carried)
        )
    qkv_sums = run(
        functools.partial(qkv_grad_kernel, data_count, 3 * local_width),
        [shaped((rows, 4 * local_width))] * count
        if ringed
        else [shaped((data_count, rows, 4 * local_width))],
        [info, hidden_one, grad_qkv, out_sums, out_chip],
        2 * group_rows * width * padded,
        scratch=[pltpu.VMEM((data_count, rows, 4 * local_width), jnp.bfloat16)],
        name="qkv_grad",
    )
    gq_near, gq_far = run(
        functools.partial(hidden_grad_kernel, tok_rows),
        [half, half],
        [info, after(grad_qkv, qkv_sums[0]), qkv_weight],
        2 * group_rows * width * padded,
        name="hidden_grad",
    )
    if ringed:
        qkv_keep, qkv_give = list(qkv_sums[0::2]), list(qkv_sums[1::2])
        qkv_taken = pair(qkv_give[1])
        mlp_ring = low(wide(after(mlp_keep[3], qkv_sums[0])) + wide(mlp_taken) + wide(mlp_carried))
        mlp_carried = onward(mlp_ring)
        mlp_taken = pair(after(mlp_give[0], mlp_ring))
        gq_far, qkv_taken, mod_chip = lax.optimization_barrier((gq_far, qkv_taken, mod_chip))
        qkv_ring = low(wide(qkv_keep[1]) + wide(qkv_taken))
        qkv_carried = onward(qkv_ring)
        qkv_taken = pair(after(qkv_give[2], qkv_ring))
    grad_mod = (grad_mod + mod_chip)[None]
    mod_other = beyond(grad_mod, 1)
    gq_core = hop(gq_far, 1)
    gq_send = low(wide(gq_near[tok_rows:]) + wide(gq_core[tok_rows:]))
    if ringed:
        qkv_carried, qkv_taken, gq_send, mlp_carried, mlp_taken = lax.optimization_barrier(
            (qkv_carried, qkv_taken, gq_send, mlp_carried, mlp_taken)
        )
        qkv_ring = low(wide(qkv_keep[2]) + wide(qkv_taken) + wide(qkv_carried))
        qkv_carried = onward(qkv_ring)
        qkv_taken = pair(after(qkv_give[3], qkv_ring))
    if ringed:
        sum_mlp = low(wide(mlp_keep[0]) + wide(mlp_taken) + wide(mlp_carried))
        qkv_carried, qkv_taken, mlp_chip, mod_other = lax.optimization_barrier(
            (qkv_carried, qkv_taken, mlp_chip, mod_other)
        )
        qkv_ring = low(wide(qkv_keep[3]) + wide(qkv_taken) + wide(qkv_carried))
        qkv_carried = onward(qkv_ring)
        qkv_taken = pair(after(qkv_give[0], qkv_ring))
    else:
        sum_mlp = low(dp_sum_direct(grad_weights[0]))
    gq_chip = hop(gq_send, 2)
    grad_mod = doubled(grad_mod, mod_other, high[0])
    mlp_far = hop(sum_mlp, 2)
    grad_inputs = run(
        input_kernel,
        [shaped((tok_rows, width))],
        [info, gain, tokens, grad_middle, gq_near, gq_core, gq_chip],
        20 * tok_rows * width,
        name="input",
    )[0]
    for place in range(1, len(high)):
        grad_mod = doubled(grad_mod, beyond(grad_mod, 1 << place), high[place])
    grad_mods = grad_mod.reshape(data_count, 3 * width)
    if ringed:
        qkv_carried, qkv_taken, gq_chip = lax.optimization_barrier(
            (qkv_carried, qkv_taken, gq_chip)
        )
        sum_qkv = low(wide(qkv_keep[0]) + wide(qkv_taken) + wide(qkv_carried))
    else:
        sum_qkv = low(dp_sum_direct(qkv_sums[0]))
    mlp_out = wide(mlp_near[:tok_rows]) + wide(mlp_core[:tok_rows]) + wide(mlp_chip)
    result = low(middle + modulation[2:3] * mlp_out)
    final_ada = lax.dot_general(
        wide(embeds), grad_mods, (((0,), (0,)), ((), ())), precision=lax.Precision.HIGHEST
    )

    mlp_blocks = [sum_mlp, mlp_far, hop(sum_mlp, 1), hop(after(mlp_far, sum_qkv, grad_inputs), 1)]
    final_up, final_down = run(
        functools.partial(finish_mlp_kernel, data_count),
        [shaped(w_up.shape, jnp.float32), shaped(w_down.shape, jnp.float32)],
        [info] + mlp_blocks,
        0,
        scratch=[pltpu.VMEM((seq_count,) + block_shape, jnp.bfloat16)],
        name="finish_mlp",
    )
    qkv_far, final_up, grad_inputs = lax.optimization_barrier(
        (hop(sum_qkv, 2), final_up, grad_inputs)
    )
    qkv_blocks = [sum_qkv, qkv_far, hop(after(sum_qkv, qkv_far), 1), hop(qkv_far, 1)]
    final_qkv, final_out, final_gain = run(
        finish_qkv_kernel,
        [
            shaped(w_qkv.shape, jnp.float32),
            shaped(w_out.shape, jnp.float32),
            shaped((1, rows), jnp.float32),
        ],
        [info] + qkv_blocks + [w_qkv, wide(ln1_gain).reshape(1, rows)],
        0,
        scratch=[pltpu.VMEM((seq_count, rows, 4 * local_width), jnp.bfloat16)],
        name="finish_qkv",
    )
    return (
        result,
        grad_inputs,
        final_gain.reshape(-1),
        final_qkv,
        final_out,
        final_ada,
        final_up,
        final_down,
    )


def solution(mesh):
    placed = (
        P(("dp", "seq"), None),
        P("dp"),
        P("dp", None),
        P("dp", None),
        P("dp", None),
        P("dp", None),
        P("dp", None),
        P(("dp", "seq"), None),
        P("dp", None),
        P("dp"),
    )
    return jax.shard_map(
        body,
        mesh=mesh,
        in_specs=placed,
        out_specs=(
            P(("dp", "seq"), None),
            P(("dp", "seq"), None),
            P("dp"),
            P("dp", None),
            P("dp", None),
            P("dp", None),
            P("dp", None),
            P("dp", None),
        ),
        check_vma=False,
    )
```

```python
import functools
import math

import jax
import jax.numpy as jnp
from jax import lax
from jax.experimental import pallas as pl
from jax.experimental.pallas import tpu as pltpu
from jax.sharding import PartitionSpec as P

HEADS = 12
HEAD_DIM = 64

eps = 1e-05

MASKS = (0, 2, 1, 3)


def time_table(time_steps, model_width):
    half_dim = model_width // 2
    frequency = jnp.exp(-math.log(10000.0) * jnp.arange(half_dim, dtype=jnp.float32) / half_dim)
    angles = time_steps[:, None] * frequency[None, :]
    return jnp.concatenate([jnp.cos(angles), jnp.sin(angles)], axis=1)


def low(values_in):
    return values_in.astype(jnp.bfloat16)


def wide(values_in):
    return values_in.astype(jnp.float32)


HEAD_TILE = 128
COST = 1.0
VMEM_GRANT = 16 * 1024 * 1024
MASK_FILL = -1e30
GELU_IN = math.sqrt(2.0 / math.pi)
GELU_CUBE = 0.044715


def rope_tables(positions):
    half_dim = HEAD_DIM // 2
    column = jnp.arange(2 * HEAD_DIM, dtype=jnp.int32)
    frequency = jnp.exp(
        -math.log(10000.0) * 2.0 * (column % half_dim).astype(jnp.float32) / HEAD_DIM
    )
    angles = positions.astype(jnp.float32)[:, None] * frequency[None, :]
    sign = jnp.where(column % HEAD_DIM < half_dim, -1.0, 1.0)
    return (jnp.cos(angles), jnp.sin(angles) * sign[None, :])


def dot_nn(left, right):
    return lax.dot_general(
        left, right, (((1,), (0,)), ((), ())), preferred_element_type=jnp.float32
    )


def dot_nt(left, right):
    return lax.dot_general(
        left, right, (((1,), (1,)), ((), ())), preferred_element_type=jnp.float32
    )


def dot_tn(left, right):
    return lax.dot_general(
        left, right, (((0,), (0,)), ((), ())), preferred_element_type=jnp.float32
    )


def norm_rows(values_in):
    average = jnp.mean(values_in, axis=-1, keepdims=True)
    centred = values_in - average
    variance = jnp.mean(centred * centred, axis=-1, keepdims=True)
    scaling = lax.rsqrt(variance + eps)
    return (centred * scaling, scaling)


def swap_halves(values_in):
    column = lax.broadcasted_iota(jnp.int32, values_in.shape, 1)
    ahead = pltpu.roll(values_in, HEAD_TILE - HEAD_DIM // 2, 1)
    behind = pltpu.roll(values_in, HEAD_DIM // 2, 1)
    return jnp.where(column % HEAD_DIM < HEAD_DIM // 2, ahead, behind)


def whole(count):
    return [pl.BlockSpec(memory_space=pltpu.VMEM)] * count


def scalars():
    return [pl.BlockSpec(memory_space=pltpu.SMEM)]


def run(kernel, out_shapes, args, flops, scratch=(), name=None):
    nbytes = sum(a.size * a.dtype.itemsize for a in args)
    nbytes += sum(math.prod(o.shape) * o.dtype.itemsize for o in out_shapes)
    call = pl.pallas_call(
        kernel,
        out_shape=out_shapes,
        in_specs=scalars() + whole(len(args) - 1),
        out_specs=whole(len(out_shapes)),
        scratch_shapes=list(scratch),
        cost_estimate=pl.CostEstimate(flops=int(flops * COST), bytes_accessed=int(nbytes * COST), transcendentals=0),
        compiler_params=pltpu.CompilerParams(vmem_limit_bytes=VMEM_GRANT),
        name=name,
    )
    return call(*args)


def shaped(shape, kind=jnp.bfloat16):
    return jax.ShapeDtypeStruct(shape, kind)


FIRST, OWNER, PLACE = 2, 6, 10


def block_segment(info, block, rows, axis):
    shape = (rows, 1) if axis == 0 else (1, rows)
    position = info[FIRST + block] + lax.broadcasted_iota(jnp.int32, shape, axis)
    return (position >= info[0]).astype(jnp.int32) + (position >= info[1]).astype(jnp.int32)


def place_rows(info, chunks, first, rows, dest):
    for index, chunk in enumerate(chunks):
        at = pl.multiple_of(info[PLACE + index] * rows, rows)
        dest[pl.ds(at, rows), : chunk.shape[1]] = chunk[first : first + rows, :]


def store_blocks(info, sums_ref, outs):
    if len(outs) == 1:
        outs[0][...] = sums_ref[...]
    else:
        for index, dest in enumerate(outs):
            dest[...] = sums_ref[info[PLACE + index]]


def first_part_kernel(info, qkv_ref, out_ref, dest):
    span = dest.shape[1] // 4
    for part in range(4):

        @pl.when(info[0] == part)
        def _():
            for third in range(3):
                at = (third * 4 + part) * span
                dest[:, third * span : (third + 1) * span] = qkv_ref[:, at : at + span]
            dest[:, 3 * span :] = out_ref[:, part * span : (part + 1) * span]


def modulation_kernel(info, embed_ref, weight_ref, out_ref):
    width = out_ref.shape[2]
    for third in range(3):
        part = dot_nn(embed_ref[...], weight_ref[:, third * width : (third + 1) * width])
        for group in range(out_ref.shape[0]):
            out_ref[group, third : third + 1, :] = part[group : group + 1, :]


def second_part_kernel(count, info, up_ref, down_ref, dest):
    rows = up_ref.shape[0]
    piece = down_ref.shape[0] // 4
    for part in range(4):

        @pl.when(info[0] == part)
        def _():
            for index in range(count):
                at = (index * 4 + part) * piece
                dest[:rows, index * piece : (index + 1) * piece] = up_ref[:, at : at + piece]
            dest[rows:, :] = down_ref[part * piece : (part + 1) * piece, :]


def qkv_kernel(heads, count, info, *refs):
    gain, cos_ref, sin_ref = refs[:3]
    tok_refs = refs[3:7]
    chunks = refs[7 : 7 + count]
    hidden_ref, weight_ref, own_ref, q_ref, k_ref, v_ref, all_ref = refs[7 + count :]
    rows, width = tok_refs[0].shape
    lw = heads * HEAD_DIM
    place_rows(info, chunks, 0, width // count, weight_ref)
    own_ref[...] = weight_ref[:, 3 * lw : 4 * lw]
    gain_row = gain[...]
    for block in range(4):
        all_ref[block] = tok_refs[block][...]

    @pl.loop(0, 4)
    def _(block):
        normed, _ = norm_rows(wide(all_ref[block]))
        hidden = low(normed * gain_row)
        here = pl.ds(pl.multiple_of(block * rows, rows), rows)
        hidden_ref[here, :] = hidden
        both = dot_nn(hidden, weight_ref[:, : 2 * lw])
        last = dot_nn(hidden, weight_ref[:, 2 * lw : 2 * lw + 2 * HEAD_TILE])
        cos_part = cos_ref[here, :]
        sin_part = sin_ref[here, :]
        turned = []
        for tile in range(2 * lw // HEAD_TILE):
            piece = both[:, tile * HEAD_TILE : (tile + 1) * HEAD_TILE]
            turned.append(piece * cos_part + swap_halves(piece) * sin_part)
        column = lax.broadcasted_iota(jnp.int32, (rows, HEAD_TILE), 1)
        segment = block_segment(info, block, rows, 0)
        first_fill = jnp.where(segment == 1, 0.0, MASK_FILL)
        second_fill = jnp.where(segment == 2, 0.0, MASK_FILL)
        q_mark = jnp.where(
            column == HEAD_DIM, first_fill, jnp.where(column == HEAD_DIM + 1, second_fill, 0.0)
        )
        first_mark = jnp.where(segment == 1, 1.0, 0.0)
        second_mark = jnp.where(segment == 2, 1.0, 0.0)
        k_mark = jnp.where(
            column == HEAD_DIM,
            first_mark,
            jnp.where(
                column == HEAD_DIM + 1, second_mark, jnp.where(column < HEAD_DIM + 5, 1.0, 0.0)
            ),
        )
        v_mark = jnp.where(column < HEAD_DIM + 2, 1.0, 0.0)
        for head in range(heads):
            q_at, k_at = head, heads + head
            q_tile = turned[q_at // 2]
            k_tile = turned[k_at // 2]
            v_tile = last[:, HEAD_TILE * (head // 2) : HEAD_TILE * (head // 2 + 1)]
            if q_at % 2:
                q_tile = pltpu.roll(q_tile, HEAD_DIM, 1)
            if k_at % 2:
                k_tile = pltpu.roll(k_tile, HEAD_DIM, 1)
            if head % 2:
                v_tile = pltpu.roll(v_tile, HEAD_DIM, 1)
            there = slice(head * HEAD_TILE, (head + 1) * HEAD_TILE)
            q_ref[here, there] = low(jnp.where(column < HEAD_DIM, q_tile * 0.125, q_mark))
            k_ref[here, there] = low(jnp.where(column < HEAD_DIM, k_tile, k_mark))
            v_ref[here, there] = low(jnp.where(column < HEAD_DIM, v_tile, v_mark))


def attend_kernel(heads, rows, info, q_ref, k_ref, v_ref, *outs):
    att_refs = outs[:4]
    stat_ref, all_ref = outs[4:]
    column = lax.broadcasted_iota(jnp.int32, (rows, HEAD_TILE), 1)

    @pl.loop(0, 4)
    def _(block):
        here = pl.ds(pl.multiple_of(block * rows, rows), rows)
        results = []
        for head in range(heads):
            there = slice(head * HEAD_TILE, (head + 1) * HEAD_TILE)
            queries = q_ref[here, there]
            scores = dot_nt(queries, k_ref[:, there])
            row_max = jnp.max(scores, axis=-1, keepdims=True)
            weights = low(jnp.exp(scores - row_max))
            summed = dot_nn(weights, v_ref[:, there])
            row_sum = summed[:, HEAD_DIM : HEAD_DIM + 1]
            results.append(summed / row_sum)
            minus = -(row_max + jnp.log(row_sum))
            first = low(minus)
            second = low(minus - wide(first))
            third = low(minus - wide(first) - wide(second))
            stat_ref[here, there] = jnp.where(
                column == HEAD_DIM + 2,
                first,
                jnp.where(
                    column == HEAD_DIM + 3, second, jnp.where(column == HEAD_DIM + 4, third, queries)
                ),
            )
        for head in range(0, heads, 2):
            if head + 1 < heads:
                both = jnp.where(
                    column < HEAD_DIM, results[head], pltpu.roll(results[head + 1], HEAD_DIM, 1)
                )
                all_ref[here, head * HEAD_DIM : (head + 2) * HEAD_DIM] = low(both)
            else:
                all_ref[here, head * HEAD_DIM :] = low(results[head][:, :HEAD_DIM])

    for block in range(4):
        att_refs[block][...] = all_ref[block * rows : (block + 1) * rows, :]


def natural(info, blocks, dest):
    for block in range(4):
        dest[info[OWNER + block]] = blocks[block][...]


def middle_kernel(info, tok_ref, mod_ref, *refs):
    middle_ref, hidden_ref, att_ref, weight_ref = refs[8:]
    natural(info, refs[:4], weight_ref)
    natural(info, refs[4:8], att_ref)
    span = weight_ref.shape[2]
    for columns in range(4):
        there = slice(columns * span, (columns + 1) * span)
        total = wide(tok_ref[:, there])
        for part in range(4):
            total = total + dot_nn(
                att_ref[part], weight_ref[columns, part * span : (part + 1) * span, :]
            )
        middle_ref[:, there] = total
    normed, _ = norm_rows(middle_ref[...])
    hidden_ref[...] = low(normed * (1.0 + mod_ref[0:1, :]) + mod_ref[1:2, :])


def act_grad_kernel(count, skip, info, mod_ref, *refs):
    dy_refs = refs[:4]
    chunks = refs[4 : 4 + count]
    mlp_ref, act_ref, weight_ref = refs[4 + count :]
    rows = dy_refs[0].shape[0]
    place_rows(info, chunks, skip, weight_ref.shape[0] // count, weight_ref)
    gate = mod_ref[2:3, :]
    for block in range(4):
        here = slice(block * rows, (block + 1) * rows)
        mlp_ref[here, :] = low(gate * wide(dy_refs[block][...]))

    @pl.loop(0, 2)
    def _(turn):
        here = pl.ds(pl.multiple_of(turn * 2 * rows, 2 * rows), 2 * rows)
        act_ref[here, :] = low(dot_nt(mlp_ref[here, :], weight_ref[...]))


def forward_kernel(count, info, act_grad, *refs):
    hid_refs = refs[:4]
    chunks = refs[4 : 4 + count]
    act_ref, pre_ref, near_ref, far_ref, weight_ref, all_ref = refs[4 + count :]
    rows = hid_refs[0].shape[0]
    place_rows(info, chunks, 0, weight_ref.shape[0] // count, weight_ref)
    for block in range(4):
        all_ref[block] = hid_refs[block][...]

    @pl.loop(0, 2)
    def _(turn):
        there = pl.ds(pl.multiple_of(turn * rows, rows), rows)
        for half, dest in ((1, far_ref), (0, near_ref)):
            here = pl.ds(pl.multiple_of((2 * half + turn) * rows, rows), rows)
            pre = dot_nn(all_ref[2 * half + turn], weight_ref[...])
            square = pre * pre
            inner = jnp.tanh(GELU_IN * (pre + GELU_CUBE * (square * pre)))
            side = 0.5 * (1.0 + inner)
            act_ref[here, :] = low(pre * side)
            slope = side + 0.5 * pre * (1.0 - inner * inner) * (
                GELU_IN * (1.0 + 3.0 * GELU_CUBE * square)
            )
            grad_pre = low(wide(act_grad[here, :]) * slope)
            pre_ref[here, :] = grad_pre
            dest[there, :] = low(dot_nt(grad_pre, weight_ref[...]))


def weight_grad_kernel(count, info, act_ref, mlp_ref, pre_ref, *refs):
    hid_refs = refs[:4]
    outs, sums_ref = refs[4:-1], refs[-1]
    rows = hid_refs[0].shape[0]
    per = act_ref.shape[1] // count
    up = dot_tn(hid_refs[0][...], pre_ref[:rows, :])
    for block in range(1, 4):
        up = up + dot_tn(hid_refs[block][...], pre_ref[block * rows : (block + 1) * rows, :])
    for index in range(count):
        sums_ref[index, :per, :] = low(up[index * per : (index + 1) * per, :])
    down = dot_tn(act_ref[...], mlp_ref[...])
    for index in range(count):
        sums_ref[index, per:, :] = low(down[index * per : (index + 1) * per, :])
    store_blocks(info, sums_ref, outs)


def down_kernel(count, skip, info, act_ref, *refs):
    dy_refs = refs[:4]
    chunks = refs[4 : 4 + count]
    near_ref, far_ref, gate_ref, weight_ref = refs[4 + count :]
    rows = dy_refs[0].shape[0]
    place_rows(info, chunks, skip, weight_ref.shape[0] // count, weight_ref)
    total = jnp.zeros(gate_ref.shape, jnp.float32)
    for block in (2, 3, 1, 0):
        here = slice(block * rows, (block + 1) * rows)
        part = dot_nn(act_ref[here, :], weight_ref[...])
        total = total + jnp.sum(wide(dy_refs[block][...]) * part, axis=0, keepdims=True)
        dest = near_ref if block < 2 else far_ref
        dest[(block % 2) * rows : (block % 2 + 1) * rows, :] = low(part)
    gate_ref[...] = total


def branch_kernel(info, mod_ref, middle_ref, dy_ref, own_ref, core_ref, chip_ref, gate_ref, *refs):
    mid_ref, branch_ref, sums_ref = refs[4:7]
    att_refs = (refs[7], refs[8], None, refs[9])
    weight_ref, parts_ref = refs[10:]
    natural(info, refs[:4], weight_ref)
    rows, width = dy_ref.shape
    grad_hidden = wide(own_ref[:rows, :]) + wide(core_ref[:rows, :]) + wide(chip_ref[...])
    normed, scaling = norm_rows(middle_ref[...])
    sums_ref[0:1, :] = jnp.sum(grad_hidden * normed, axis=0, keepdims=True)
    sums_ref[1:2, :] = jnp.sum(grad_hidden, axis=0, keepdims=True)
    sums_ref[2:3, :] = gate_ref[...]
    grad_normed = grad_hidden * (1.0 + mod_ref[0:1, :])
    first_mean = jnp.mean(grad_normed, axis=-1, keepdims=True)
    second_mean = jnp.mean(grad_normed * normed, axis=-1, keepdims=True)
    mid_ref[...] = wide(dy_ref[...]) + scaling * (grad_normed - first_mean - normed * second_mean)
    span = weight_ref.shape[2]
    branch_ref[:, :width] = low(mid_ref[...])
    branch_ref[:, width + span :] = jnp.zeros(
        (rows, branch_ref.shape[1] - width - span), jnp.bfloat16
    )
    for columns in range(4):
        parts_ref[columns] = low(mid_ref[:, columns * span : (columns + 1) * span])
    for block, dest in enumerate(att_refs):
        at = pl.multiple_of(info[OWNER + block] * span, HEAD_DIM)
        total = dot_nt(parts_ref[0], weight_ref[0, pl.ds(at, span), :])
        for columns in range(1, 4):
            total = total + dot_nt(parts_ref[columns], weight_ref[columns, pl.ds(at, span), :])
        if dest is None:
            branch_ref[:, width : width + span] = low(total)
        else:
            dest[...] = low(total)


def out_grad_kernel(info, att_ref, core_att_ref, branch_ref, core_branch_ref, near_ref, parts_ref):
    span = att_ref.shape[2]
    for columns in range(4):
        here = slice(columns * span, (columns + 1) * span)
        parts_ref[columns] = branch_ref[:, here]
        parts_ref[4 + columns] = core_branch_ref[:, here]
    for block in range(2):
        owner = info[OWNER + block]
        branch, core_branch = parts_ref[owner], parts_ref[4 + owner]
        for part in range(4):
            near_ref[block, part * span : (part + 1) * span, :] = low(
                dot_tn(att_ref[part], branch) + dot_tn(core_att_ref[part], core_branch)
            )


def attend_back_kernel(heads, rows, info, cos_ref, sin_ref, q_ref, k_ref, v_ref, *refs):
    att = refs[:4]
    span = heads * HEAD_DIM
    width = 4 * span
    grads = ((refs[4], 0), (refs[5], 0), (refs[6], width), (refs[7], 0))
    out_ref, gx_ref, turn_ref, dq_ref, dk_ref, dv_ref = refs[8:]
    column = lax.broadcasted_iota(jnp.int32, (rows, HEAD_TILE), 1)

    def tile_of(ref, base, head):
        at = base + HEAD_TILE * (head // 2)
        if base or head % 2 or head + 1 < heads:
            tile = wide(ref[:, at : at + HEAD_TILE])
            return pltpu.roll(tile, HEAD_DIM, 1) if head % 2 else tile
        last = wide(ref[:, at:])
        return jnp.concatenate([last, jnp.zeros_like(last)], axis=1)

    for head in range(heads):
        there = slice(head * HEAD_TILE, (head + 1) * HEAD_TILE)
        for block in range(4):
            here = slice(block * rows, (block + 1) * rows)
            grad = jnp.where(column < HEAD_DIM, tile_of(*grads[block], head), 0.0)
            minus = -jnp.sum(grad * tile_of(att[block], 0, head), axis=-1, keepdims=True)
            first = wide(low(minus))
            gx_ref[here, :] = low(
                jnp.where(
                    column == HEAD_DIM,
                    first,
                    jnp.where(column == HEAD_DIM + 1, minus - first, grad),
                )
            )
        for block in range(4):
            here = slice(block * rows, (block + 1) * rows)
            keys = k_ref[here, there]
            probs = jnp.exp(dot_nt(keys, q_ref[:, there]))
            prob_grad = dot_nt(v_ref[here, there], gx_ref[...])
            score_grad = low(probs * prob_grad)
            dv_ref[here, there] = dot_nn(low(probs), gx_ref[...])
            dk_ref[here, there] = dot_nn(score_grad, q_ref[:, there])
            part = dot_tn(keys, score_grad)
            if block == 0:
                turn_ref[...] = part
            else:
                turn_ref[...] += part
        dq_ref[:, there] = jnp.transpose(turn_ref[...]) * 0.125

    for block in range(4):
        here = slice(block * rows, (block + 1) * rows)
        heads_of = [dq_ref[here, h * HEAD_TILE : (h + 1) * HEAD_TILE] for h in range(heads)]
        heads_of += [dk_ref[here, h * HEAD_TILE : (h + 1) * HEAD_TILE] for h in range(heads)]
        heads_of += [dv_ref[here, h * HEAD_TILE : (h + 1) * HEAD_TILE] for h in range(heads)]
        heads_of.append(jnp.zeros((rows, HEAD_TILE), jnp.float32))
        for tile in range((3 * heads + 1) // 2):
            both = jnp.where(
                column < HEAD_DIM,
                heads_of[2 * tile],
                pltpu.roll(heads_of[2 * tile + 1], HEAD_DIM, 1),
            )
            if tile < heads:
                both = both * cos_ref[here, :] - swap_halves(both) * sin_ref[here, :]
            out_ref[here, tile * HEAD_TILE : (tile + 1) * HEAD_TILE] = low(both)


def hidden_grad_kernel(rows, info, grad_ref, weight_ref, near_ref, far_ref):
    span = grad_ref.shape[1]

    @pl.loop(0, 2)
    def _(turn):
        there = pl.ds(pl.multiple_of(turn * rows, rows), rows)
        for half, dest in ((1, far_ref), (0, near_ref)):
            here = pl.ds(pl.multiple_of((2 * half + turn) * rows, rows), rows)
            dest[there, :] = low(dot_nt(grad_ref[here, :], weight_ref[:, :span]))


def qkv_grad_kernel(count, used, info, hidden_ref, grad_ref, near_ref, chip_ref, *refs):
    outs, sums_ref = refs[:-1], refs[-1]
    total = dot_tn(hidden_ref[...], grad_ref[...])
    out_total = wide(near_ref[0]) + wide(chip_ref[0])
    per = total.shape[0] // count
    for index in range(count):
        here = slice(index * per, (index + 1) * per)
        sums_ref[index, :, :used] = low(total[here, :used])
        sums_ref[index, :, used:] = low(out_total[here, :])
    store_blocks(info, sums_ref, outs)


def input_kernel(info, gain, tok_ref, mid_ref, own_ref, core_ref, chip_ref, out_ref):
    rows = tok_ref.shape[0]
    grad_hidden = wide(own_ref[:rows, :]) + wide(core_ref[:rows, :]) + wide(chip_ref[:rows, :])
    normed, scaling = norm_rows(wide(tok_ref[...]))
    grad_normed = grad_hidden * gain[...]
    first_mean = jnp.mean(grad_normed, axis=-1, keepdims=True)
    second_mean = jnp.mean(grad_normed * normed, axis=-1, keepdims=True)
    out_ref[...] = low(
        mid_ref[...] + scaling * (grad_normed - first_mean - normed * second_mean)
    )


def finish_mlp_kernel(count, info, *refs):
    blocks = refs[:4]
    up_ref, down_ref, all_ref = refs[4:]
    natural(info, blocks, all_ref)
    rows = up_ref.shape[0]
    piece = down_ref.shape[0] // 4
    for part in range(4):
        value = wide(all_ref[part])
        for index in range(count):
            at = (index * 4 + part) * piece
            up_ref[:, at : at + piece] = value[:rows, index * piece : (index + 1) * piece]
        down_ref[part * piece : (part + 1) * piece, :] = value[rows:, :]


def finish_qkv_kernel(info, *refs):
    blocks = refs[:4]
    weight_ref, gain_ref, out_ref, own_ref, sums_ref, all_ref = refs[4:]
    natural(info, blocks, all_ref)
    span = all_ref.shape[2] // 4
    total = jnp.zeros((out_ref.shape[0], 1), jnp.float32)
    for part in range(4):
        value = wide(all_ref[part])
        for third in range(3):
            at = (third * 4 + part) * span
            piece = value[:, third * span : (third + 1) * span]
            total = total + jnp.sum(
                wide(weight_ref[:, at : at + span]) * piece, axis=1, keepdims=True
            )
            out_ref[:, at : at + span] = piece
        own_ref[:, part * span : (part + 1) * span] = value[:, 3 * span :]
    turned = jnp.transpose(jnp.broadcast_to(total, (total.shape[0], HEAD_TILE)))
    sums_ref[...] = turned[0:1, :] / gain_ref[...]


def hop(values_in, mask):
    return lax.ppermute(values_in, "seq", [(i, i ^ mask) for i in range(lax.axis_size("seq"))])


def ring_of(count):
    return [0] + list(range(1, count, 2)) + [i for i in range(count - 1, 0, -1) if i % 2 == 0]


def ring_next(data_count):
    outer = data_count // 2
    ring = ring_of(outer)
    follow = {ring[i]: ring[(i + 1) % outer] for i in range(outer)}
    return [(z * 2 + y, follow[z] * 2 + y) for z in range(outer) for y in range(2)]


def pair(values_in):
    return lax.ppermute(values_in, "dp", [(i, i ^ 1) for i in range(lax.axis_size("dp"))])


def dp_sum_direct(blocks):
    data_count = lax.axis_size("dp")
    if data_count != 8:
        return wide(lax.psum_scatter(blocks, "dp", scatter_dimension=0, tiled=False))
    return jnp.sum(wide(lax.all_to_all(blocks, "dp", 0, 0, tiled=True)), axis=0)


def after(values_in, *earlier):
    return lax.optimization_barrier((values_in,) + earlier)[0]


def onward(values_in):
    return lax.ppermute(values_in, "dp", ring_next(lax.axis_size("dp")))


def kernel_info(layout, rank, index, tok_rows):
    data_count = lax.axis_size("dp")
    column = jnp.arange(PLACE + 8, dtype=jnp.int32)

    def owner(block):
        return rank ^ ((block & 1) * 2 + (block >> 1))

    values = jnp.where(column == 0, layout[0, 0], layout[0, 1])
    values = jnp.where(column >= FIRST, owner(column - FIRST) * tok_rows, values)
    values = jnp.where(column >= OWNER, owner(column - OWNER), values)
    if data_count == 8:
        step = column - PLACE
        at = index >> 1
        at = ((at ^ (at >> 1)) - (step >> 1)) & 3
        place = (at ^ (at >> 1)) * 2 + ((index + step) & 1)
    else:
        place = jnp.zeros_like(column)
    return jnp.where(column >= PLACE, place, values)


def gathered_whole(chunk, sizes):
    gathered = lax.all_gather(chunk, "dp", axis=0)
    parts = []
    at = 0
    for size in sizes:
        parts.append(gathered[:, at : at + size].reshape(-1, chunk.shape[1]))
        at += size
    return [jnp.concatenate(parts, axis=0)]


def four(values_in):
    chip = hop(values_in, 2)
    return [values_in, chip, hop(values_in, 1), hop(chip, 1)]


def beyond(values_in, mask):
    return lax.ppermute(values_in, "dp", [(i, i ^ mask) for i in range(lax.axis_size("dp"))])


def doubled(parts, other, bit):
    return jnp.where(
        bit, jnp.concatenate([other, parts], axis=0), jnp.concatenate([parts, other], axis=0)
    )


def body(tokens, ln1_gain, w_qkv, w_out, w_ada, w_up, w_down, out_grad, layout, timestep):
    seq_count = lax.axis_size("seq")
    data_count = lax.axis_size("dp")
    ringed = data_count == 8
    rank = lax.axis_index("seq")
    index = lax.axis_index("dp")
    high = [(index >> place) & 1 == 1 for place in range(data_count.bit_length() - 1)]
    tokens, rank, index, high = lax.optimization_barrier((tokens, rank, index, high))
    tok_rows, width = tokens.shape
    group_rows = tok_rows * seq_count
    heads_local = HEADS // seq_count
    local_width = heads_local * HEAD_DIM
    head_columns = heads_local * HEAD_TILE
    padded = (3 * heads_local + 1) // 2 * HEAD_TILE
    rows = w_qkv.shape[0]
    hidden = w_up.shape[1] // seq_count
    down_piece = w_down.shape[0] // seq_count
    rank_word = rank.reshape(1).astype(jnp.int32)

    tok_chip = hop(tokens, 2)
    first = run(
        first_part_kernel,
        [shaped((rows, 4 * local_width))],
        [rank_word, w_qkv, w_out],
        0,
        name="first_part",
    )[0]
    if ringed:
        held = [first, onward(first)]
        beside = [pair(first)]
        held[1], beside[0], tokens = lax.optimization_barrier((held[1], beside[0], tokens))
        held.append(onward(held[1]))
        beside.append(pair(held[1]))
        tok_core = hop(tokens, 1)
        held[2], beside[1], tok_chip, tok_core = lax.optimization_barrier(
            (held[2], beside[1], tok_chip, tok_core)
        )
        held.append(onward(held[2]))
        beside.append(pair(held[2]))
        tok_both = hop(tok_chip, 1)
    else:
        tok_core, tok_both = hop(tokens, 1), hop(tok_chip, 1)
    tok_blocks = [tokens, tok_chip, tok_core, tok_both]

    embed = low(time_table(wide(timestep), width))
    sent = jnp.stack(
        [embed.reshape(data_count, rows), jnp.broadcast_to(ln1_gain, (data_count, rows))], axis=1
    )
    taken = lax.all_to_all(sent, "dp", 0, 0, tiled=True)
    embeds = taken[:, 0]
    gain = wide(taken[:, 1].reshape(1, width))
    mod_parts = run(
        modulation_kernel,
        [shaped((data_count, 3, width), jnp.float32)],
        [rank_word, after(embeds, held[2]) if ringed else embeds, w_ada],
        2 * data_count * rows * w_ada.shape[1],
        name="modulation",
    )[0]

    def halves(parts, place):
        half = parts.shape[0] // 2
        kept = jnp.where(high[place], parts[half:], parts[:half])
        given = jnp.where(high[place], parts[:half], parts[half:])
        return kept, beyond(given, 1 << place)

    modulation = mod_parts
    for place in range(len(high) - 1, 2, -1):
        modulation = sum(halves(modulation, place))

    info = kernel_info(layout, rank, index, tok_rows)
    starts = info[FIRST:OWNER]

    second = run(
        functools.partial(second_part_kernel, data_count),
        [shaped((rows + down_piece, width))],
        [rank_word, w_up, w_down],
        0,
        name="second_part",
    )[0]
    if ringed:
        dy_core = hop(after(out_grad, held[2]), 1)
        held[3], beside[2], second, dy_core, *rest = lax.optimization_barrier(
            (
                held[3],
                beside[2],
                second,
                dy_core,
                gain,
                info,
                tok_blocks,
            )
        )
        gain, info, tok_blocks = rest
        modulation = after(modulation, held[3])
        beside.append(pair(held[3]))
        first_chunks = [part for both in zip(held, beside) for part in both]
        second = after(second, beside[3])
        held = [second, onward(second)]
        beside = [pair(second)]
        dy_chip = hop(after(out_grad, held[0]), 2)
    else:
        first_chunks = gathered_whole(first, [rows])
        second_chunks = gathered_whole(second, [rows, down_piece])
        dy_chip, dy_core = hop(out_grad, 2), hop(out_grad, 1)
    if ringed:
        starts = after(starts, first_chunks[6])
    positions = (starts[:, None] + jnp.arange(tok_rows, dtype=jnp.int32)[None, :]).reshape(-1)
    cos_table, sin_table = rope_tables(positions)
    kept, sums = halves(modulation, 2)
    if ringed:
        gain, sums = lax.optimization_barrier((gain, sums))
    kept, sums = halves(kept + sums, 1)
    count = len(first_chunks)
    up_rows = rows * (data_count // count)

    hidden_one, qkv_weight, own_out, queries, keys, values = run(
        functools.partial(qkv_kernel, heads_local, count),
        [
            shaped((group_rows, width)),
            shaped((width, 4 * local_width)),
            shaped((width, local_width)),
            shaped((group_rows, head_columns)),
            shaped((group_rows, head_columns)),
            shaped((group_rows, head_columns)),
        ],
        [info, gain, cos_table, sin_table] + tok_blocks + first_chunks,
        2 * group_rows * width * padded,
        scratch=[pltpu.VMEM((seq_count, tok_rows, width), jnp.bfloat16)],
        name="qkv",
    )
    if ringed:
        queries, own_out, held[1], beside[0], sums = lax.optimization_barrier(
            (queries, own_out, held[1], beside[0], sums)
        )
        beside.append(pair(held[1]))
        held.append(onward(held[1]))
    kept, sums = halves(kept + sums, 0)
    chip_out = hop(own_out, 2)
    core_out = hop(own_out, 1)
    *att_parts, marked = run(
        functools.partial(attend_kernel, heads_local, tok_rows),
        [shaped((tok_rows, local_width))] * 4 + [shaped((group_rows, head_columns))],
        [info, queries, keys, values],
        4 * group_rows * group_rows * head_columns,
        scratch=[pltpu.VMEM((group_rows, local_width), jnp.bfloat16)],
        name="attend",
    )
    if ringed:
        att_parts, held[2], beside[1], chip_out, core_out, dy_chip, sums = lax.optimization_barrier(
            (att_parts, held[2], beside[1], chip_out, core_out, dy_chip, sums)
        )
        beside.append(pair(held[2]))
        held.append(onward(held[2]))
    modulation = (kept + sums)[0]
    att_own = [att_parts[0]] + [hop(att_parts[j], MASKS[j]) for j in (1, 2, 3)]
    out_blocks = [own_out, chip_out, core_out, hop(after(chip_out, att_own[2]), 1)]
    if ringed:
        att_own, held[3], beside[2] = lax.optimization_barrier((att_own, held[3], beside[2]))
    middle, hidden_two, att_ordered = run(
        middle_kernel,
        [
            shaped((tok_rows, width), jnp.float32),
            shaped((tok_rows, width)),
            shaped((seq_count, tok_rows, local_width)),
        ],
        [info, tokens, modulation] + out_blocks + att_own,
        2 * tok_rows * width * width,
        scratch=[pltpu.VMEM((seq_count, width, local_width), jnp.bfloat16)],
        name="middle",
    )

    chip_hidden = hop(hidden_two, 2)
    if ringed:
        beside.append(pair(held[3]))
        second_chunks = [part for both in zip(held, beside) for part in both]
    dy_blocks = [out_grad, dy_chip, dy_core, hop(after(dy_chip, hidden_two), 1)]
    grad_mlp, grad_act = run(
        functools.partial(act_grad_kernel, count, up_rows),
        [shaped((group_rows, width)), shaped((group_rows, hidden))],
        [info, modulation] + dy_blocks + second_chunks,
        2 * group_rows * width * hidden,
        scratch=[pltpu.VMEM((hidden, width), jnp.bfloat16)],
        name="act_grad",
    )
    hid_blocks = [
        hidden_two,
        chip_hidden,
        hop(hidden_two, 1),
        hop(after(chip_hidden, grad_act), 1),
    ]
    half = shaped((group_rows // 2, width))
    activated, grad_pre, gh_near, gh_far = run(
        functools.partial(forward_kernel, count),
        [shaped((group_rows, hidden)), shaped((group_rows, hidden)), half, half],
        [info, grad_act] + hid_blocks + second_chunks,
        4 * group_rows * width * hidden,
        scratch=[
            pltpu.VMEM((width, hidden), jnp.bfloat16),
            pltpu.VMEM((seq_count, tok_rows, width), jnp.bfloat16),
        ],
        name="forward",
    )
    block_shape = (rows + down_piece, width)
    grad_weights = run(
        functools.partial(weight_grad_kernel, data_count),
        [shaped(block_shape)] * count if ringed else [shaped((data_count,) + block_shape)],
        [info, activated, grad_mlp, grad_pre] + hid_blocks,
        4 * group_rows * width * hidden,
        scratch=[pltpu.VMEM((data_count,) + block_shape, jnp.bfloat16)],
        name="weight_grad",
    )
    gh_core = hop(gh_far, 1)
    gh_core, grad_weights = lax.optimization_barrier((gh_core, grad_weights))
    gh_send = low(wide(gh_near[tok_rows:]) + wide(gh_core[tok_rows:]))
    gh_chip = hop(gh_send, 2)
    mlp_near, mlp_far, grad_gate = run(
        functools.partial(down_kernel, count, up_rows),
        [half, half, shaped((1, width), jnp.float32)],
        [info, after(activated, gh_send)] + dy_blocks + second_chunks,
        2 * group_rows * width * hidden,
        scratch=[pltpu.VMEM((hidden, width), jnp.bfloat16)],
        name="down",
    )
    if ringed:
        mlp_keep, mlp_give = list(grad_weights[0::2]), list(grad_weights[1::2])
        mlp_taken = pair(after(mlp_give[1], gh_send))
        gh_chip, mlp_far, mlp_taken = lax.optimization_barrier((gh_chip, mlp_far, mlp_taken))
        mlp_ring = low(wide(mlp_keep[1]) + wide(mlp_taken))
        gh_chip, mlp_ring = lax.optimization_barrier((gh_chip, mlp_ring))
        mlp_carried = onward(mlp_ring)
        mlp_taken = pair(after(mlp_give[2], mlp_ring))
    else:
        gh_chip, mlp_far = lax.optimization_barrier((gh_chip, mlp_far))
    mlp_core = hop(mlp_far, 1)
    core_attended = hop(after(att_ordered, gh_chip), 1)

    branch_columns = -(-(width + local_width) // HEAD_TILE) * HEAD_TILE
    grad_middle, branch, grad_mod, *grad_parts = run(
        branch_kernel,
        [
            shaped((tok_rows, width), jnp.float32),
            shaped((tok_rows, branch_columns)),
            shaped((3, width), jnp.float32),
        ]
        + [shaped((tok_rows, local_width))] * 3,
        [info, modulation, after(middle, mlp_near), out_grad, gh_near, gh_core, gh_chip]
        + [grad_gate]
        + out_blocks,
        2 * tok_rows * width * width,
        scratch=[
            pltpu.VMEM((seq_count, width, local_width), jnp.bfloat16),
            pltpu.VMEM((seq_count, tok_rows, local_width), jnp.bfloat16),
        ],
        name="branch",
    )
    grad_parts, mlp_core = lax.optimization_barrier((grad_parts, mlp_core))
    core_branch = hop(branch, 1)
    grad_att = [grad_parts[0], hop(grad_parts[1], 2), core_branch, hop(grad_parts[2], 3)]
    out_sums = run(
        out_grad_kernel,
        [shaped((2, width, local_width))],
        [info, att_ordered, core_attended, branch, core_branch],
        2 * tok_rows * width * width,
        scratch=[pltpu.VMEM((2 * seq_count, tok_rows, local_width), jnp.bfloat16)],
        name="out_grad",
    )[0]

    if ringed:
        del grad_att[2]
        grad_att, out_sums, mlp_taken, mlp_carried = lax.optimization_barrier(
            (grad_att, out_sums, mlp_taken, mlp_carried)
        )
        grad_att.insert(2, core_branch)
        mlp_ring = low(wide(mlp_keep[2]) + wide(mlp_taken) + wide(mlp_carried))
        mlp_carried = onward(mlp_ring)
        mlp_taken = pair(after(mlp_give[3], mlp_ring))
    out_chip = hop(out_sums[1:], 2)
    mod_core = hop(grad_mod, 1)
    grad_qkv = run(
        functools.partial(attend_back_kernel, heads_local, tok_rows),
        [shaped((group_rows, padded))],
        [info, cos_table, sin_table, marked, keys, values] + att_parts + grad_att,
        10 * group_rows * group_rows * head_columns,
        scratch=[
            pltpu.VMEM((group_rows, HEAD_TILE), jnp.bfloat16),
            pltpu.VMEM((HEAD_TILE, group_rows), jnp.float32),
            pltpu.VMEM((group_rows, head_columns), jnp.float32),
            pltpu.VMEM((group_rows, head_columns), jnp.float32),
            pltpu.VMEM((group_rows, head_columns), jnp.float32),
        ],
        name="attend_back",
    )[0]
    grad_qkv, out_chip, mod_core = lax.optimization_barrier((grad_qkv, out_chip, mod_core))
    grad_mod = grad_mod + mod_core
    mod_chip = hop(grad_mod, 2)
    mlp_send = low(wide(after(mlp_near[tok_rows:], grad_qkv)) + wide(mlp_core[tok_rows:]))
    mlp_chip = hop(mlp_send, 2)
    if ringed:
        grad_qkv, mlp_taken, mlp_carried = lax.optimization_barrier(
            (grad_qkv, mlp_taken, mlp_carried)
        )
    qkv_sums = run(
        functools.partial(qkv_grad_kernel, data_count, 3 * local_width),
        [shaped((rows, 4 * local_width))] * count
        if ringed
        else [shaped((data_count, rows, 4 * local_width))],
        [info, hidden_one, grad_qkv, out_sums, out_chip],
        2 * group_rows * width * padded,
        scratch=[pltpu.VMEM((data_count, rows, 4 * local_width), jnp.bfloat16)],
        name="qkv_grad",
    )
    gq_near, gq_far = run(
        functools.partial(hidden_grad_kernel, tok_rows),
        [half, half],
        [info, after(grad_qkv, qkv_sums[0]), qkv_weight],
        2 * group_rows * width * padded,
        name="hidden_grad",
    )
    if ringed:
        qkv_keep, qkv_give = list(qkv_sums[0::2]), list(qkv_sums[1::2])
        qkv_taken = pair(qkv_give[1])
        gq_far, qkv_taken, mod_chip = lax.optimization_barrier((gq_far, qkv_taken, mod_chip))
        qkv_ring = low(wide(qkv_keep[1]) + wide(qkv_taken))
        qkv_carried = onward(qkv_ring)
        qkv_taken = pair(after(qkv_give[2], qkv_ring))
    grad_mod = (grad_mod + mod_chip)[None]
    mod_other = beyond(grad_mod, 1)
    gq_core = hop(gq_far, 1)
    if ringed:
        mlp_ring = low(wide(after(mlp_keep[3], gq_core)) + wide(mlp_taken) + wide(mlp_carried))
        mlp_carried = onward(mlp_ring)
        mlp_taken = pair(after(mlp_give[0], mlp_ring))
    gq_send = low(wide(gq_near[tok_rows:]) + wide(gq_core[tok_rows:]))
    if ringed:
        qkv_carried, qkv_taken, gq_send = lax.optimization_barrier(
            (qkv_carried, qkv_taken, gq_send)
        )
        qkv_ring = low(wide(qkv_keep[2]) + wide(qkv_taken) + wide(qkv_carried))
        qkv_carried = onward(qkv_ring)
        qkv_taken = pair(after(qkv_give[3], qkv_ring))
    if ringed:
        qkv_carried, qkv_taken, mlp_chip, mod_other = lax.optimization_barrier(
            (qkv_carried, qkv_taken, mlp_chip, mod_other)
        )
        mlp_carried, mlp_taken, qkv_carried = lax.optimization_barrier(
            (mlp_carried, mlp_taken, qkv_carried)
        )
        sum_mlp = low(wide(mlp_keep[0]) + wide(mlp_taken) + wide(mlp_carried))
        qkv_ring = low(wide(qkv_keep[3]) + wide(qkv_taken) + wide(qkv_carried))
        qkv_carried = onward(qkv_ring)
        qkv_taken = pair(after(qkv_give[0], qkv_ring))
    else:
        sum_mlp = low(dp_sum_direct(grad_weights[0]))
    gq_chip = hop(gq_send, 2)
    grad_mod = doubled(grad_mod, mod_other, high[0])
    mlp_far = hop(sum_mlp, 2)
    grad_inputs = run(
        input_kernel,
        [shaped((tok_rows, width))],
        [info, gain, tokens, grad_middle, gq_near, gq_core, gq_chip],
        20 * tok_rows * width,
        name="input",
    )[0]
    for place in range(1, len(high)):
        grad_mod = doubled(grad_mod, beyond(grad_mod, 1 << place), high[place])
    grad_mods = grad_mod.reshape(data_count, 3 * width)
    if ringed:
        qkv_carried, qkv_taken, gq_chip = lax.optimization_barrier(
            (qkv_carried, qkv_taken, gq_chip)
        )
        sum_qkv = low(wide(qkv_keep[0]) + wide(qkv_taken) + wide(qkv_carried))
    else:
        sum_qkv = low(dp_sum_direct(qkv_sums[0]))
    mlp_out = wide(mlp_near[:tok_rows]) + wide(mlp_core[:tok_rows]) + wide(mlp_chip)
    result = low(middle + modulation[2:3] * mlp_out)
    final_ada = lax.dot_general(
        wide(embeds), grad_mods, (((0,), (0,)), ((), ())), precision=lax.Precision.HIGHEST
    )

    mlp_blocks = [sum_mlp, mlp_far, hop(sum_mlp, 1), hop(after(mlp_far, sum_qkv, grad_inputs), 1)]
    final_up, final_down = run(
        functools.partial(finish_mlp_kernel, data_count),
        [shaped(w_up.shape, jnp.float32), shaped(w_down.shape, jnp.float32)],
        [info] + mlp_blocks,
        0,
        scratch=[pltpu.VMEM((seq_count,) + block_shape, jnp.bfloat16)],
        name="finish_mlp",
    )
    qkv_far, final_up, grad_inputs = lax.optimization_barrier(
        (hop(sum_qkv, 2), final_up, grad_inputs)
    )
    qkv_blocks = [sum_qkv, qkv_far, hop(after(sum_qkv, qkv_far), 1), hop(qkv_far, 1)]
    final_qkv, final_out, final_gain = run(
        finish_qkv_kernel,
        [
            shaped(w_qkv.shape, jnp.float32),
            shaped(w_out.shape, jnp.float32),
            shaped((1, rows), jnp.float32),
        ],
        [info] + qkv_blocks + [w_qkv, wide(ln1_gain).reshape(1, rows)],
        0,
        scratch=[pltpu.VMEM((seq_count, rows, 4 * local_width), jnp.bfloat16)],
        name="finish_qkv",
    )
    return (
        result,
        grad_inputs,
        final_gain.reshape(-1),
        final_qkv,
        final_out,
        final_ada,
        final_up,
        final_down,
    )


def solution(mesh):
    placed = (
        P(("dp", "seq"), None),
        P("dp"),
        P("dp", None),
        P("dp", None),
        P("dp", None),
        P("dp", None),
        P("dp", None),
        P(("dp", "seq"), None),
        P("dp", None),
        P("dp"),
    )
    return jax.shard_map(
        body,
        mesh=mesh,
        in_specs=placed,
        out_specs=(
            P(("dp", "seq"), None),
            P(("dp", "seq"), None),
            P("dp"),
            P("dp", None),
            P("dp", None),
            P("dp", None),
            P("dp", None),
            P("dp", None),
        ),
        check_vma=False,
    )
```
